32 devices in a mesh: dp: 4 (over z), row: 4 (over y, x), col: 2 (over core).
Axes of the slice: x: 2, y: 2, z: 4, core: 2. Of those that a mesh axis runs over, the one named last changes fastest.
Arguments:
- tokens: bfloat16 [8, 1024, 2048], P(('dp', 'col'), 'row'), may hold values from -6 to 6
- prefix_len: int32 [8], P(('dp', 'col')), may hold values from 102 to 512, as said below
- norm1_gain: bfloat16 [2048], replicated, may hold values from 0.5 to 1.5
- norm1_bias: bfloat16 [2048], replicated, may hold values from -1.1953125 to 1.1953125
- query_key_value_weight: bfloat16 [2048, 3, 2048], P(('dp', 'col'), None, 'row'), may hold values from -0.125 to 0.125
- query_key_value_bias: bfloat16 [3, 2048], P(None, 'row'), may hold values from -2.5 to 2.5
- attention_output_weight: bfloat16 [2048, 2048], P(('dp', 'col'), 'row'), may hold values from -0.75 to 0.75
- norm2_gain: bfloat16 [2048], replicated, may hold values from 0.5 to 1.5
- norm2_bias: bfloat16 [2048], replicated, may hold values from -1.1953125 to 1.1953125
- gate_up_projection_weight: bfloat16 [2048, 2, 5632], P(('dp', 'row'), None, 'col'), may hold values from -0.125 to 0.125
- down_projection_weight: bfloat16 [2048, 5632], P(('dp', 'row'), 'col'), may hold values from -0.078125 to 0.078125
- grad_out: bfloat16 [8, 1024, 2048], P(('dp', 'col'), 'row'), may hold values from -30 to 30
Outputs:
- layer_out: bfloat16 [8, 1024, 2048], P(('dp', 'col'), 'row')
- input_token_gradient: float32 [8, 1024, 2048], P(('dp', 'col'), 'row')
- grad_norm1_gain: float32 [2048], replicated
- grad_norm1_bias: float32 [2048], replicated
- grad_qkv_weight: float32 [2048, 3, 2048], P(('dp', 'col'), None, 'row')
- grad_qkv_bias: float32 [3, 2048], P(None, 'row')
- grad_out_weight: float32 [2048, 2048], P(('dp', 'col'), 'row')
- grad_norm2_gain: float32 [2048], replicated
- grad_norm2_bias: float32 [2048], replicated
- grad_gate_up_weight: float32 [2048, 2, 5632], P(('dp', 'row'), None, 'col')
- grad_down_weight: float32 [2048, 5632], P(('dp', 'row'), 'col')
The draws below stay inside these ranges and needn't reach their ends.
Inputs may be any that keep to these rules, and one draw needn't show every extreme that they name: `prefix_len`: both ends of the range occur in every draw.
All inputs are finite; a program needn't handle non-finite values.
Results may differ from the reference program's by a relative error of at most 0.02.
Values may be sent and summed in bfloat16 or wider, within the bound.
No kernel may reach another device: no remote copies, remote signals or barrier semaphores. Data moves between devices by JAX's collectives and lax.ppermute only.
A program may use at most 192 MiB of HBM per device.

```python
import math
from functools import partial
import jax
import jax.numpy as jnp
from jax import lax

D = 2048
H = 32
HD = 64
ROT = 16
FF = 5632
LEN = 1024
SEQS = 8


def draw_prefix_len(key, part):
    key_values, key_order = jax.random.split(key)
    lengths = jax.random.randint(key_values, (SEQS,), LEN // 10, LEN // 2 + 1)
    order = jax.random.permutation(key_order, SEQS)
    lengths = jnp.where(order == 0, LEN // 2, lengths)
    lengths = jnp.where(order == 1, LEN // 10, lengths)
    return lengths.astype(jnp.int32)


def draw_grad_out(key, part):
    seq_frac = jnp.arange(SEQS, dtype=jnp.float32) / max(SEQS - 1, 1)
    tok_frac = jnp.arange(LEN, dtype=jnp.float32) / max(LEN - 1, 1)
    base_vals = jax.random.normal(key, (SEQS, LEN, D), jnp.float32)
    scaling = (1.0 + 2.0 * seq_frac[:, None, None]) * (1.0 + 2.0 * tok_frac[None, :, None]) / 3.0
    return jnp.clip(base_vals * scaling, -30.0, 30.0).astype(jnp.bfloat16)


def block_levels(stream_key, dims, shards, least, largest):
    def one(dim, parts):
        draws = jax.random.uniform(jax.random.fold_in(jax.random.fold_in(stream_key, 6), dim), (parts,), jnp.float32, least / len(shards), largest / len(shards))
        return jnp.repeat(jnp.exp(draws), dims[dim] // parts).reshape((-1,) + (1,) * (len(dims) - dim - 1))

    factor_of = one(*shards[0])
    for cut in shards[1:]:
        factor_of = factor_of * one(*cut)
    return factor_of


def normal_values(rng, extent, width, bound, pieces=(), kind=jnp.bfloat16):
    result = jax.random.normal(rng, extent, jnp.float32) * width
    if len(pieces) > 0:
        result = block_levels(rng, extent, pieces, -0.22, 0.18) * result
    return jnp.clip(result, min=-bound, max=bound).astype(kind)


def setup_inputs(seed: int = 0) -> dict:
    splits = jax.random.split(jax.random.key(seed), 13)
    return {
        "tokens": normal_values(splits[0], (SEQS, LEN, D), 1.0, 6.0, ((0, 8), (1, 4))),
        "prefix_len": draw_prefix_len(jax.random.fold_in(splits[12], 71), 0),
        "norm1_gain": jnp.clip(1.0 + 0.1 * jax.random.normal(splits[2], (D,), jnp.float32), 0.5, 1.5).astype(jnp.bfloat16),
        "norm1_bias": normal_values(splits[3], (D,), 0.3, 1.1953125),
        "query_key_value_weight": normal_values(splits[4], (D, 3, D), D ** -0.5, 0.125, ((0, 8), (2, 4))),
        "query_key_value_bias": normal_values(splits[5], (3, D), 0.5, 2.5, ((1, 4),)),
        "attention_output_weight": normal_values(splits[6], (D, D), (D // 32) ** -0.5, 0.75, ((0, 8), (1, 4))),
        "norm2_gain": jnp.clip(1.0 + 0.1 * jax.random.normal(splits[7], (D,), jnp.float32), 0.5, 1.5).astype(jnp.bfloat16),
        "norm2_bias": normal_values(splits[8], (D,), 0.3, 1.1953125),
        "gate_up_projection_weight": normal_values(splits[9], (D, 2, FF), D ** -0.5, 0.125, ((0, 16), (2, 2))),
        "down_projection_weight": normal_values(splits[10], (D, FF), FF ** -0.5, 0.078125, ((0, 16), (1, 2))),
        "grad_out": draw_grad_out(jax.random.fold_in(splits[12], 71), 0),
    }


@jax.custom_vjp
def low(v):
    return lax.optimization_barrier(v.astype(jnp.bfloat16)).astype(jnp.float32)

@jax.custom_vjp
def lowered_backward(v):
    return v

def low_keep(v):
    return (low(v), None)

def low_pass(kept, grad):
    return (grad,)

def back_keep(v):
    return (v, None)

def back_low(kept, grad):
    return (low(grad),)
low.defvjp(low_keep, low_pass)
lowered_backward.defvjp(back_keep, back_low)
norm_eps = 1e-05
rope_base = 10000.0
highest_precision = lax.Precision.HIGHEST

def layer_norm(values, norm_gain, norm_shift):
    centre = lax.optimization_barrier(jnp.mean(values, axis=-1, keepdims=True))
    centred = values - centre
    variance = lax.optimization_barrier(jnp.mean(centred * centred, axis=-1, keepdims=True))
    return centred * lax.rsqrt(variance + norm_eps) * norm_gain + norm_shift

def rotary_tables():
    half_rot = ROT // 2
    freqs = rope_base ** (-jnp.arange(half_rot, dtype=jnp.float32) * 2.0 / ROT)
    angles = jnp.arange(LEN, dtype=jnp.float32)[:, None] * freqs[None, :]
    return (jnp.cos(angles)[:, None, :], jnp.sin(angles)[:, None, :])

def rotate(heads, cosine, sines):
    half_rot = ROT // 2
    first = heads[..., :half_rot]
    second = heads[..., half_rot:ROT]
    return jnp.concatenate([first * cosine - second * sines, second * cosine + first * sines, heads[..., ROT:]], axis=-1)

def attend(seq_item):
    queries, keys_all, values, prefix = seq_item
    scores = jnp.einsum('qhd,khd->hqk', queries, keys_all, precision=highest_precision) * (1.0 / math.sqrt(HD))
    scores = lowered_backward(scores)
    key_place = jnp.arange(LEN)
    allowed = (key_place[None, :] <= key_place[:, None]) | (key_place[None, :] < prefix)
    scores = jnp.where(allowed[None, :, :], scores, -1e+30)
    attn_probs = low(jax.nn.softmax(scores, axis=-1))
    return jnp.einsum('hqk,khd->qhd', attn_probs, values, precision=highest_precision)

def block_forward(token_blk, prefix_blk, params):
    norm1_gain, norm1_bias, query_key_value_weight, query_key_value_bias, attention_output_weight, norm2_gain, norm2_bias, gate_up_projection_weight, down_projection_weight = params
    seq_count = token_blk.shape[0]
    cosine, sines = rotary_tables()
    first_norm_input = low(layer_norm(token_blk, norm1_gain, norm1_bias))
    projected_values = jnp.einsum('wbv,vtp->wbtp', first_norm_input, query_key_value_weight, precision=highest_precision) + query_key_value_bias
    projected_values = lowered_backward(projected_values)
    head_shape = (seq_count, LEN, H, HD)
    queries = low(rotate(projected_values[:, :, 0].reshape(head_shape), cosine, sines))
    keys_all = low(rotate(projected_values[:, :, 1].reshape(head_shape), cosine, sines))
    values = low(projected_values[:, :, 2].reshape(head_shape))
    attention_result = lax.map(jax.checkpoint(attend), (queries, keys_all, values, prefix_blk))
    attention_result = low(lowered_backward(attention_result.reshape(seq_count, LEN, D)))
    residual_branch = lowered_backward(jnp.einsum('woh,ch->woc', attention_result, attention_output_weight, precision=highest_precision))
    middle = token_blk + residual_branch
    second_norm_input = low(layer_norm(middle, norm2_gain, norm2_bias))
    gate_up_values = lowered_backward(jnp.einsum('ekx,xzi->ekzi', second_norm_input, gate_up_projection_weight, precision=highest_precision))
    hidden_state = low(jax.nn.silu(gate_up_values[:, :, 0]) * gate_up_values[:, :, 1])
    mixed_state = lowered_backward(jnp.einsum('zxq,iq->zxi', hidden_state, down_projection_weight, precision=highest_precision))
    return middle + mixed_state

def whole_layer(prefix_len, tokens, norm1_gain, norm1_bias, query_key_value_weight, query_key_value_bias, attention_output_weight, norm2_gain, norm2_bias, gate_up_projection_weight, down_projection_weight):
    params = (norm1_gain, norm1_bias, query_key_value_weight, query_key_value_bias, attention_output_weight, norm2_gain, norm2_bias, gate_up_projection_weight, down_projection_weight)
    group_size = math.gcd(SEQS, 4)
    group_count = SEQS // group_size
    token_blocks = tokens.reshape(group_count, group_size, LEN, D)
    prefix_blocks = prefix_len.reshape(group_count, group_size)

    def one_group(pair):
        return block_forward(pair[0], pair[1], params)
    outputs = lax.map(jax.checkpoint(one_group), (token_blocks, prefix_blocks))
    return outputs.reshape(SEQS, LEN, D)

def reference(tokens, prefix_len, norm1_gain, norm1_bias, query_key_value_weight, query_key_value_bias, attention_output_weight, norm2_gain, norm2_bias, gate_up_projection_weight, down_projection_weight, grad_out):
    floats = tuple((item.astype(jnp.float32) for item in (tokens, norm1_gain, norm1_bias, query_key_value_weight, query_key_value_bias, attention_output_weight, norm2_gain, norm2_bias, gate_up_projection_weight, down_projection_weight)))
    layer_out, pullback = jax.vjp(partial(whole_layer, prefix_len), *floats)
    grads = pullback(grad_out.astype(jnp.float32))
    return (layer_out.astype(jnp.bfloat16), grads[0], grads[1], grads[2], grads[3], grads[4], grads[5], grads[6], grads[7], grads[8], grads[9])
```

```python
import math

import jax
import jax.numpy as jnp
from jax import lax
from jax.sharding import PartitionSpec as P

HD = 64
ROT = 16

norm_eps = 1e-05
rope_base = 10000.0
masked_fill = -1e30

bf16 = jnp.bfloat16
f32 = jnp.float32


def layer_norm_forward(values, norm_gain, norm_shift):
    centre = jnp.mean(values, axis=-1, keepdims=True)
    centred = values - centre
    variance = jnp.mean(centred * centred, axis=-1, keepdims=True)
    inverse = lax.rsqrt(variance + norm_eps)
    normed = centred * inverse
    return (normed * norm_gain + norm_shift, normed, inverse)


def layer_norm_backward(incoming, normed, inverse, norm_gain):
    scaled = incoming * norm_gain
    inner = jnp.mean(scaled, axis=-1, keepdims=True)
    along = jnp.mean(scaled * normed, axis=-1, keepdims=True)
    return inverse * (scaled - inner - normed * along)


def rotary_tables(length):
    half_rot = ROT // 2
    freqs = rope_base ** (-jnp.arange(half_rot, dtype=f32) * 2.0 / ROT)
    angles = jnp.arange(length, dtype=f32)[:, None] * freqs[None, :]
    return (jnp.cos(angles)[:, None, :], jnp.sin(angles)[:, None, :])


def rotate(heads, cosine, sines):
    half_rot = ROT // 2
    first = heads[..., :half_rot]
    second = heads[..., half_rot:ROT]
    return jnp.concatenate(
        [first * cosine - second * sines, second * cosine + first * sines, heads[..., ROT:]],
        axis=-1,
    )


def dot(left, right, dims):
    return lax.dot_general(left, right, (dims, ((), ())), preferred_element_type=f32)


def nn(left, right):
    return dot(left, right, ((1,), (0,)))


def nt(left, right):
    return dot(left, right, ((1,), (1,)))


def tn(left, right):
    return dot(left, right, ((0,), (0,)))


def visible(length, prefix):
    place = jnp.arange(length)
    return (place[None, :] <= place[:, None]) | (place[None, :] < prefix)


def attend_forward(queries, keys_all, values, prefix):
    scale = 1.0 / math.sqrt(HD)
    scores = jnp.einsum("qhd,khd->hqk", queries, keys_all, preferred_element_type=f32) * scale
    scores = jnp.where(visible(queries.shape[0], prefix)[None], scores, masked_fill)
    row_top = jnp.max(scores, axis=-1, keepdims=True)
    exp_scores = jnp.exp(scores - row_top)
    row_total = jnp.sum(exp_scores, axis=-1, keepdims=True)
    attn_probs = (exp_scores / row_total).astype(bf16)
    result = jnp.einsum("hqk,khd->qhd", attn_probs, values, preferred_element_type=f32)
    return result.astype(bf16), (row_top + jnp.log(row_total))


def attend_backward(queries, keys_all, values, prefix, log_sums, grad_rows):
    scale = 1.0 / math.sqrt(HD)
    scores = jnp.einsum("qhd,khd->hqk", queries, keys_all, preferred_element_type=f32) * scale
    allowed = visible(queries.shape[0], prefix)[None]
    attn_probs = jnp.where(allowed, jnp.exp(scores - log_sums), 0.0)
    grad_probs = jnp.einsum("qhd,khd->hqk", grad_rows, values, preferred_element_type=f32)
    inner = jnp.sum(attn_probs * grad_probs, axis=-1, keepdims=True)
    grad_scores = (attn_probs * (grad_probs - inner)).astype(bf16)
    grad_q = jnp.einsum("hqk,khd->qhd", grad_scores, keys_all, preferred_element_type=f32) * scale
    grad_k = jnp.einsum("hqk,qhd->khd", grad_scores, queries, preferred_element_type=f32) * scale
    grad_v = jnp.einsum(
        "hqk,qhd->khd", attn_probs.astype(bf16), grad_rows, preferred_element_type=f32
    )
    return grad_q, grad_k, grad_v


def make_body(mesh):
    R = mesh.shape["row"]
    C = mesh.shape["col"]
    N = max(R, C)

    def row_permute(block, k):
        return lax.ppermute(block, "row", [(i, i ^ k) for i in range(R)])

    def gather_rel(block):
        if R != 4:
            return [block] + [row_permute(block, k) for k in range(1, R)]
        half = block.shape[0] // 2
        one = row_permute(block, 1)
        two = row_permute(block, 2)
        top = row_permute(one[:half], 2)
        low = row_permute(two[half:], 1)
        return [block, one, two, jnp.concatenate([top, low], axis=0)]

    def scatter_rel(blocks):
        if R != 4:
            total = blocks[0]
            for k in range(1, R):
                total = total + row_permute(blocks[k].astype(bf16), k).astype(f32)
            return total
        half = blocks[0].shape[0] // 2
        b = [(x[:half], x[half:]) for x in blocks]
        top0 = row_permute(b[1][0].astype(bf16), 1)
        top2 = row_permute(b[3][0].astype(bf16), 1)
        low0 = row_permute(b[2][1].astype(bf16), 2)
        low1 = row_permute(b[3][1].astype(bf16), 2)
        top2 = row_permute((b[2][0].astype(f32) + top2.astype(f32)).astype(bf16), 2)
        low1 = row_permute((b[1][1].astype(f32) + low1.astype(f32)).astype(bf16), 1)
        top = b[0][0].astype(f32) + top0.astype(f32) + top2.astype(f32)
        low = b[0][1].astype(f32) + low0.astype(f32) + low1.astype(f32)
        return jnp.concatenate([top, low], axis=0)

    def xor_blocks(array, r):
        size = array.shape[0] // R
        return jnp.concatenate(
            [lax.dynamic_slice_in_dim(array, (r ^ k) * size, size, 0) for k in range(R)], axis=0
        )

    def source_place(s, c):
        return (s % (R // C)) * C + c if C <= R else c

    def source_dest(s, c, k):
        slot = source_place(s, c) ^ k
        if C <= R:
            return slot, s // (R // C)
        q = C // R
        return slot // q, s * q + slot % q

    def exchange_pairs(k):
        pairs = []
        for s in range(R):
            for c in range(C):
                dr, dc = source_dest(s, c, k)
                pairs.append((s * C + c, dr * C + dc))
        return pairs

    def spread_weights(pieces, u, v):
        out = jnp.zeros(pieces.shape, pieces.dtype)
        for k in range(N):
            sent = lax.dynamic_index_in_dim(pieces, u ^ k, 0, keepdims=True)
            got = lax.ppermute(sent, ("row", "col"), exchange_pairs(k))
            out = lax.dynamic_update_slice_in_dim(out, got, v ^ k, 0)
        return out

    def return_weights(pieces, u, v):
        out = jnp.zeros(pieces.shape, pieces.dtype)
        for k in range(N):
            sent = lax.dynamic_index_in_dim(pieces, v ^ k, 0, keepdims=True)
            got = lax.ppermute(sent, ("row", "col"), [(b, a) for a, b in exchange_pairs(k)])
            out = lax.dynamic_update_slice_in_dim(out, got, u ^ k, 0)
        return out

    def sum_everywhere(array):
        for name in ("col", "row", "dp"):
            size = mesh.shape[name]
            step = 1
            while step < size:
                array = array + lax.ppermute(array, name, [(i, i ^ step) for i in range(size)])
                step *= 2
        return array

    def body(
        tokens,
        prefix_len,
        norm1_gain,
        norm1_bias,
        query_key_value_weight,
        query_key_value_bias,
        attention_output_weight,
        norm2_gain,
        norm2_bias,
        gate_up_projection_weight,
        down_projection_weight,
        grad_out,
    ):
        r = lax.axis_index("row")
        c = lax.axis_index("col")
        block = tokens.shape[1]
        length = block * R
        width = tokens.shape[2]
        head_cols = query_key_value_weight.shape[2]
        heads = head_cols // HD
        prefix = prefix_len[0]
        w_rows, _, ff_local = gate_up_projection_weight.shape
        ff_slice = ff_local // R
        ff = ff_slice * C
        q_rows = max(1, C // R)
        u = source_place(r, c)
        v = r if C <= R else r * q_rows + c % q_rows

        cosine, sines = rotary_tables(length)
        gain1 = norm1_gain.astype(f32)
        gain2 = norm2_gain.astype(f32)
        inputs = tokens[0].astype(f32)
        first, first_std, first_inv = layer_norm_forward(inputs, gain1, norm1_bias.astype(f32))
        seq_in = jnp.concatenate(gather_rel(first.astype(bf16)), axis=0)

        w_qkv = lax.all_gather(
            query_key_value_weight.reshape(-1, 3 * head_cols), ("dp", "col"), axis=0, tiled=True
        )
        w_out = lax.all_gather(attention_output_weight, ("dp", "col"), axis=0, tiled=True)

        packed = jnp.concatenate(
            [
                gate_up_projection_weight[:, 0].reshape(w_rows, R, ff_slice),
                gate_up_projection_weight[:, 1].reshape(w_rows, R, ff_slice),
                down_projection_weight.reshape(w_rows, R, ff_slice),
            ],
            axis=2,
        )
        packed = packed.transpose(1, 0, 2).reshape(R, q_rows, w_rows // q_rows, 3 * ff_slice)
        packed = packed.reshape(R * q_rows, w_rows // q_rows, 3 * ff_slice)
        arrived = spread_weights(packed, u, v)
        a_rows = N // C
        arrived = arrived.reshape(a_rows, C, w_rows // q_rows, 3, ff_slice)
        arrived = arrived.transpose(3, 0, 2, 1, 4).reshape(3, a_rows * w_rows // q_rows, ff)
        gu_shard = jnp.concatenate([arrived[0], arrived[1]], axis=1)
        w_gu = lax.all_gather(gu_shard, ("dp", "col"), axis=0, tiled=True)
        w_down = lax.all_gather(arrived[2], ("dp", "col"), axis=0, tiled=True)

        dy = grad_out[0]
        dy_rel = jnp.concatenate(gather_rel(dy), axis=0)

        projected = nn(seq_in, w_qkv) + query_key_value_bias.astype(f32).reshape(-1)
        projected = xor_blocks(projected, r).reshape(length, 3, heads, HD)
        queries = rotate(projected[:, 0], cosine, sines).astype(bf16)
        keys_all = rotate(projected[:, 1], cosine, sines).astype(bf16)
        values = projected[:, 2].astype(bf16)
        attended, log_sums = attend_forward(queries, keys_all, values, prefix)
        attended = xor_blocks(attended.reshape(length, head_cols), r)
        own = nt(attended[:block], w_out)
        others = nt(attended[block:], w_out).astype(bf16)
        residual = scatter_rel([own] + [others[k * block : (k + 1) * block] for k in range(R - 1)])
        middle = inputs + residual

        second, second_std, second_inv = layer_norm_forward(
            middle, gain2, norm2_bias.astype(f32)
        )
        second_in = jnp.concatenate(gather_rel(second.astype(bf16)), axis=0)
        gate_up = nn(second_in, w_gu)
        gate_vals = gate_up[:, :ff]
        up_vals = gate_up[:, ff:]
        sig = jax.nn.sigmoid(gate_vals)
        swish = gate_vals * sig
        hidden = (swish * up_vals).astype(bf16)
        grad_down = tn(dy_rel, hidden).astype(bf16)
        grad_down = lax.psum_scatter(grad_down, ("dp", "col"), scatter_dimension=0, tiled=True)
        grad_hidden = nn(dy_rel, w_down)
        grad_gate = grad_hidden * up_vals * sig * (1.0 + gate_vals * (1.0 - sig))
        grad_up = grad_hidden * swish
        grad_gu_vals = jnp.concatenate([grad_gate.astype(bf16), grad_up.astype(bf16)], axis=1)
        own = nt(grad_gu_vals[:block], w_gu)
        others = nt(grad_gu_vals[block:], w_gu).astype(bf16)
        grad_second = scatter_rel(
            [own] + [others[k * block : (k + 1) * block] for k in range(R - 1)]
        )
        grad_gu = tn(second_in, grad_gu_vals).astype(bf16)
        grad_gu = lax.psum_scatter(grad_gu, ("dp", "col"), scatter_dimension=0, tiled=True)
        own = nt(hidden[:block], w_down)
        others = nt(hidden[block:], w_down).astype(bf16)
        mixed = scatter_rel([own] + [others[k * block : (k + 1) * block] for k in range(R - 1)])
        layer_out = (middle + mixed).astype(bf16)

        grad_middle = dy.astype(f32) + layer_norm_backward(
            grad_second, second_std, second_inv, gain2
        )
        gain2_grad = jnp.sum(grad_second * second_std, axis=0)
        bias2_grad = jnp.sum(grad_second, axis=0)

        branch = jnp.concatenate(gather_rel(grad_middle.astype(bf16)), axis=0)
        grad_heads = nn(branch, w_out).astype(bf16)
        grad_wout = tn(branch, attended).astype(bf16)
        grad_wout = lax.psum_scatter(grad_wout, ("dp", "col"), scatter_dimension=0, tiled=True)
        grad_heads = xor_blocks(grad_heads, r).reshape(length, heads, HD)
        grad_q, grad_k, grad_v = attend_backward(
            queries, keys_all, values, prefix, log_sums, grad_heads
        )
        grad_proj = jnp.stack(
            [rotate(grad_q, cosine, -sines), rotate(grad_k, cosine, -sines), grad_v], axis=1
        )
        grad_proj = grad_proj.reshape(length, 3 * head_cols).astype(bf16)
        grad_proj = xor_blocks(grad_proj, r)
        bias_local = jnp.sum(grad_proj, axis=0, dtype=f32).reshape(3, head_cols)
        grad_wqkv = tn(seq_in, grad_proj).astype(bf16)
        grad_wqkv = lax.psum_scatter(grad_wqkv, ("dp", "col"), scatter_dimension=0, tiled=True)
        own = nt(grad_proj[:block], w_qkv)
        others = nt(grad_proj[block:], w_qkv).astype(bf16)
        grad_first = scatter_rel(
            [own] + [others[k * block : (k + 1) * block] for k in range(R - 1)]
        )
        input_grad = grad_middle + layer_norm_backward(grad_first, first_std, first_inv, gain1)
        gain1_grad = jnp.sum(grad_first * first_std, axis=0)
        bias1_grad = jnp.sum(grad_first, axis=0)

        col_offset = r * head_cols
        bias_full = lax.dynamic_update_slice(
            jnp.zeros((3, width), f32), bias_local, (jnp.int32(0), col_offset)
        )
        early = jnp.concatenate([gain2_grad[None], bias2_grad[None], bias_full], axis=0)
        early = sum_everywhere(early)
        late = sum_everywhere(jnp.stack([gain1_grad, bias1_grad]))
        grad_bias = lax.dynamic_slice_in_dim(early[2:], col_offset, head_cols, 1)

        a = a_rows * w_rows // q_rows
        back = jnp.stack([grad_gu[:, :ff], grad_gu[:, ff:], grad_down]).reshape(
            3, a_rows, w_rows // q_rows, C, ff_slice
        )
        back = back.transpose(1, 3, 2, 0, 4).reshape(N, w_rows // q_rows, 3 * ff_slice)
        home = return_weights(back, u, v).reshape(R, w_rows, 3, ff_slice)
        home = home.transpose(1, 2, 0, 3).reshape(w_rows, 3, ff_local).astype(f32)
        return (
            layer_out[None],
            input_grad[None],
            late[0],
            late[1],
            grad_wqkv.astype(f32).reshape(-1, 3, head_cols),
            grad_bias,
            grad_wout.astype(f32),
            early[0],
            early[1],
            home[:, :2],
            home[:, 2],
        )

    return body


def solution(mesh):
    in_specs = (
        P(("dp", "col"), "row", None),
        P(("dp", "col")),
        P(),
        P(),
        P(("dp", "col"), None, "row"),
        P(None, "row"),
        P(("dp", "col"), "row"),
        P(),
        P(),
        P(("dp", "row"), None, "col"),
        P(("dp", "row"), "col"),
        P(("dp", "col"), "row", None),
    )
    out_specs = (
        P(("dp", "col"), "row", None),
        P(("dp", "col"), "row", None),
        P(),
        P(),
        P(("dp", "col"), None, "row"),
        P(None, "row"),
        P(("dp", "col"), "row"),
        P(),
        P(),
        P(("dp", "row"), None, "col"),
        P(("dp", "row"), "col"),
    )
    return jax.shard_map(
        make_body(mesh), mesh=mesh, in_specs=in_specs, out_specs=out_specs, check_vma=False
    )
```

```python
import functools
import math

import jax
import jax.numpy as jnp
from jax import lax
from jax.experimental import pallas as pl
from jax.experimental.pallas import tpu as pltpu
from jax.sharding import PartitionSpec as P

HD = 64
ROT = 16

norm_eps = 1e-05
rope_base = 10000.0
masked_fill = -1e30

bf16 = jnp.bfloat16
f32 = jnp.float32


def layer_norm_forward(values, norm_gain, norm_shift):
    centre = jnp.mean(values, axis=-1, keepdims=True)
    centred = values - centre
    variance = jnp.mean(centred * centred, axis=-1, keepdims=True)
    inverse = lax.rsqrt(variance + norm_eps)
    normed = centred * inverse
    return (normed * norm_gain + norm_shift, normed, inverse)


def layer_norm_backward(incoming, normed, inverse, norm_gain):
    scaled = incoming * norm_gain
    inner = jnp.mean(scaled, axis=-1, keepdims=True)
    along = jnp.mean(scaled * normed, axis=-1, keepdims=True)
    return inverse * (scaled - inner - normed * along)


def rotary_tables(places):
    half_rot = ROT // 2
    column = jnp.arange(2 * HD) % HD
    freqs = rope_base ** (-(column % half_rot).astype(f32) * 2.0 / ROT)
    angles = places.astype(f32)[:, None] * freqs[None, :]
    sines = jnp.sin(angles)
    cosine = jnp.where(column < ROT, jnp.cos(angles), 1.0)
    left = jnp.where((column >= half_rot) & (column < ROT), sines, 0.0)
    right = jnp.where(column < half_rot, -sines, 0.0)
    return jnp.stack([cosine, left, right])


def dot(left, right, dims):
    return lax.dot_general(left, right, (dims, ((), ())), preferred_element_type=f32)


def nn(left, right):
    return dot(left, right, ((1,), (0,)))


def nt(left, right):
    return dot(left, right, ((1,), (1,)))


def tn(left, right):
    return dot(left, right, ((0,), (0,)))


def key_blocks(jq, blocks):
    return max(jq + 1, blocks // 2)


def block_mask(qpos, kpos, jq, jk, blocks, prefix):
    if jk < jq:
        return None
    causal = kpos <= qpos
    if jk >= blocks // 2:
        return causal
    early = kpos < prefix
    return (causal | early) if jk == jq else early


def head_lane(head):
    lane = lax.broadcasted_iota(jnp.int32, (1, 2 * HD), 1)
    return (lane < HD) if head == 0 else (lane >= HD)


def forward_kernel(blocks, size, info, proj, table, qkv, out, sums):
    w = 2 * HD
    scale = 1.0 / math.sqrt(HD)
    r, prefix = info[0], info[1]
    for j in range(blocks):
        rows = pl.ds(j * size, size)
        cosine, left, right = table[0, rows], table[1, rows], table[2, rows]
        for part in range(2):
            x = proj[rows, part * w : (part + 1) * w]
            x = x * cosine + pltpu.roll(x, 8, 1) * left + pltpu.roll(x, w - 8, 1) * right
            qkv[rows, part * w : (part + 1) * w] = x.astype(bf16)
        qkv[rows, 2 * w : 3 * w] = proj[rows, 2 * w : 3 * w].astype(bf16)
    places = [pl.ds(pl.multiple_of((j ^ r) * size, size), size) for j in range(blocks)]
    for jq in range(blocks):
        count = key_blocks(jq, blocks)
        q = qkv[places[jq], 0:w].astype(f32) * scale
        qpos = jq * size + lax.broadcasted_iota(jnp.int32, (size, size), 0)
        results = []
        tops = []
        for head in range(2):
            qh = jnp.where(head_lane(head), q, 0.0).astype(bf16)
            scores = []
            for jk in range(count):
                s = nt(qh, qkv[places[jk], w : 2 * w])
                kpos = jk * size + lax.broadcasted_iota(jnp.int32, (size, size), 1)
                mask = block_mask(qpos, kpos, jq, jk, blocks, prefix)
                scores.append(s if mask is None else jnp.where(mask, s, masked_fill))
            top = jnp.max(scores[0], axis=1, keepdims=True)
            for s in scores[1:]:
                top = jnp.maximum(top, jnp.max(s, axis=1, keepdims=True))
            total = 0.0
            result = 0.0
            for jk in range(count):
                e = jnp.exp(scores[jk] - top)
                total = total + jnp.sum(e, axis=1, keepdims=True)
                result = result + nn(e.astype(bf16), qkv[places[jk], 2 * w : 3 * w])
            results.append(result / total)
            tops.append(top + jnp.log(total))
        out[places[jq], :] = jnp.where(head_lane(0), results[0], results[1]).astype(bf16)
        both = jnp.where(head_lane(0), tops[0], tops[1])
        flipped = both.T
        sums[0, jq, 0:8, :] = flipped[0:8]
        sums[0, jq, 8:16, :] = flipped[HD : HD + 8]


def backward_kernel(blocks, size, info, qkv, table, sums, grads, out, bias, qm, km, gm, acc):
    w = 2 * HD
    scale = 1.0 / math.sqrt(HD)
    r, prefix = info[0], info[1]
    for head in range(2):
        lanes = head_lane(head)
        for j in range(blocks):
            rows = pl.ds(j * size, size)
            q = qkv[rows, 0:w].astype(f32) * scale
            k = qkv[rows, w : 2 * w].astype(f32) * scale
            qm[head, rows] = jnp.where(lanes, q, 0.0).astype(bf16)
            km[head, rows] = jnp.where(lanes, k, 0.0).astype(bf16)
            gm[head, rows] = jnp.where(lanes, grads[rows, :].astype(f32), 0.0).astype(bf16)
    acc[...] = jnp.zeros_like(acc)
    places = [pl.ds(pl.multiple_of((j ^ r) * size, size), size) for j in range(blocks)]
    for jq in range(blocks):
        count = key_blocks(jq, blocks)
        rq = places[jq]
        qpos = jq * size + lax.broadcasted_iota(jnp.int32, (size, size), 1)
        grad_q = 0.0
        for head in range(2):
            top = sums[0, jq, 8 * head : 8 * head + 1, :]
            probs = []
            products = []
            inner = 0.0
            for jk in range(count):
                s = nt(qkv[places[jk], w : 2 * w], qm[head, rq])
                p = jnp.exp(s - top)
                kpos = jk * size + lax.broadcasted_iota(jnp.int32, (size, size), 0)
                mask = block_mask(qpos, kpos, jq, jk, blocks, prefix)
                if mask is not None:
                    p = jnp.where(mask, p, 0.0)
                t = p * nt(qkv[places[jk], 2 * w : 3 * w], gm[head, rq])
                inner = inner + jnp.sum(t, axis=0, keepdims=True)
                probs.append(p)
                products.append(t)
            for jk in range(count):
                rk = places[jk]
                d = (products[jk] - probs[jk] * inner).astype(bf16)
                acc[1, rk] += nn(probs[jk].astype(bf16), gm[head, rq])
                acc[0, rk] += nn(d, qm[head, rq])
                grad_q = grad_q + tn(d, km[head, rk])
        cosine, left, right = table[0, rq], table[1, rq], table[2, rq]
        x = grad_q
        x = x * cosine - pltpu.roll(x, 8, 1) * left - pltpu.roll(x, w - 8, 1) * right
        out[rq, 0:w] = x.astype(bf16)
    bias_q = 0.0
    bias_k = 0.0
    bias_v = 0.0
    for j in range(blocks):
        rows = pl.ds(j * size, size)
        x = acc[0, rows]
        x = x * table[0, rows]
        x = x - pltpu.roll(acc[0, rows], 8, 1) * table[1, rows]
        x = x - pltpu.roll(acc[0, rows], w - 8, 1) * table[2, rows]
        x = x.astype(bf16)
        y = acc[1, rows].astype(bf16)
        out[rows, w : 2 * w] = x
        out[rows, 2 * w : 3 * w] = y
        bias_q = bias_q + jnp.sum(out[rows, 0:w].astype(f32), axis=0, keepdims=True)
        bias_k = bias_k + jnp.sum(x.astype(f32), axis=0, keepdims=True)
        bias_v = bias_v + jnp.sum(y.astype(f32), axis=0, keepdims=True)
    row = jnp.concatenate([bias_q, bias_k, bias_v], axis=1)
    bias[0] = jnp.broadcast_to(row, (8, 3 * w))


def attend_forward(info, projected, table, blocks):
    length = projected.shape[0]
    w = 2 * HD
    pairs = projected.shape[1] // (3 * w)
    size = length // blocks
    spec = pltpu.PrefetchScalarGridSpec(
        num_scalar_prefetch=1,
        grid=(pairs,),
        in_specs=[
            pl.BlockSpec((length, 3 * w), lambda p, i: (0, p)),
            pl.BlockSpec((3, length, w), lambda p, i: (0, 0, 0)),
        ],
        out_specs=[
            pl.BlockSpec((length, 3 * w), lambda p, i: (0, p)),
            pl.BlockSpec((length, w), lambda p, i: (0, p)),
            pl.BlockSpec((1, blocks, 16, size), lambda p, i: (p, 0, 0, 0)),
        ],
    )
    return pl.pallas_call(
        lambda *refs: forward_kernel(blocks, size, *refs),
        grid_spec=spec,
        out_shape=[
            jax.ShapeDtypeStruct((length, 3 * w * pairs), bf16),
            jax.ShapeDtypeStruct((length, w * pairs), bf16),
            jax.ShapeDtypeStruct((pairs, blocks, 16, size), f32),
        ],
        name="attend_forward",
        compiler_params=pltpu.CompilerParams(vmem_limit_bytes=48 << 20),
    )(info, projected, table)


def attend_backward(info, qkv, table, sums, grads, blocks):
    length = qkv.shape[0]
    w = 2 * HD
    pairs = qkv.shape[1] // (3 * w)
    size = length // blocks
    spec = pltpu.PrefetchScalarGridSpec(
        num_scalar_prefetch=1,
        grid=(pairs,),
        in_specs=[
            pl.BlockSpec((length, 3 * w), lambda p, i: (0, p)),
            pl.BlockSpec((3, length, w), lambda p, i: (0, 0, 0)),
            pl.BlockSpec((1, blocks, 16, size), lambda p, i: (p, 0, 0, 0)),
            pl.BlockSpec((length, w), lambda p, i: (0, p)),
        ],
        out_specs=[
            pl.BlockSpec((length, 3 * w), lambda p, i: (0, p)),
            pl.BlockSpec((1, 8, 3 * w), lambda p, i: (p, 0, 0)),
        ],
        scratch_shapes=[
            pltpu.VMEM((2, length, w), bf16),
            pltpu.VMEM((2, length, w), bf16),
            pltpu.VMEM((2, length, w), bf16),
            pltpu.VMEM((2, length, w), f32),
        ],
    )
    return pl.pallas_call(
        lambda *refs: backward_kernel(blocks, size, *refs),
        grid_spec=spec,
        out_shape=[
            jax.ShapeDtypeStruct((length, 3 * w * pairs), bf16),
            jax.ShapeDtypeStruct((pairs, 8, 3 * w), f32),
        ],
        name="attend_backward",
        compiler_params=pltpu.CompilerParams(vmem_limit_bytes=48 << 20),
    )(info, qkv, table, sums, grads)


def pack_kernel(R, q, info, gate_up, down, out):
    fs = down.shape[1] // R
    rows = down.shape[0] // q
    for slot in range(R * q):
        span = pl.ds((slot % q) * rows, rows)
        lo = (slot // q) * fs
        k = slot ^ info[2]
        out[k, :, 0:fs] = gate_up[0, span, lo : lo + fs]
        out[k, :, fs : 2 * fs] = gate_up[1, span, lo : lo + fs]
        out[k, :, 2 * fs : 3 * fs] = down[span, lo : lo + fs]


def unpack_kernel(C, info, *refs):
    pieces, (gate_up, down, held) = refs[:-3], refs[-3:]
    rows = held.shape[1]
    ff = down.shape[1]
    fs = ff // C
    for k, piece in enumerate(pieces):
        held[k ^ info[3]] = piece[...]
    for place in range(len(pieces)):
        span = pl.ds((place // C) * rows, rows)
        lo = (place % C) * fs
        gate_up[span, lo : lo + fs] = held[place, :, 0:fs]
        gate_up[span, ff + lo : ff + lo + fs] = held[place, :, fs : 2 * fs]
        down[span, lo : lo + fs] = held[place, :, 2 * fs : 3 * fs]


def pack_back_kernel(C, info, gate_up, down, out):
    rows = out.shape[1]
    ff = down.shape[1]
    fs = ff // C
    for place in range(out.shape[0]):
        span = pl.ds((place // C) * rows, rows)
        lo = (place % C) * fs
        k = place ^ info[3]
        out[k, :, 0:fs] = gate_up[span, lo : lo + fs]
        out[k, :, fs : 2 * fs] = gate_up[span, ff + lo : ff + lo + fs]
        out[k, :, 2 * fs : 3 * fs] = down[span, lo : lo + fs]


def unpack_back_kernel(R, q, info, *refs):
    pieces, (gate_up, down, held) = refs[:-3], refs[-3:]
    rows = held.shape[1]
    fs = down.shape[1] // R
    for k, piece in enumerate(pieces):
        held[k ^ info[2]] = piece[...]
    for slot in range(len(pieces)):
        span = pl.ds((slot % q) * rows, rows)
        lo = (slot // q) * fs
        gate_up[0, span, lo : lo + fs] = held[slot, :, 0:fs].astype(f32)
        gate_up[1, span, lo : lo + fs] = held[slot, :, fs : 2 * fs].astype(f32)
        down[span, lo : lo + fs] = held[slot, :, 2 * fs : 3 * fs].astype(f32)


def prepare_kernel(info, qkv, outer, out):
    w = 2 * HD
    cols = outer.shape[1]
    for pair in range(cols // w):
        for part in range(3):
            lo = (3 * pair + part) * w
            out[:, lo : lo + w] = qkv[part, :, pair * w : (pair + 1) * w]
    out[:, 3 * cols :] = outer[...]


def finish_kernel(info, grads, qkv, outer):
    w = 2 * HD
    cols = outer.shape[1]
    for pair in range(cols // w):
        for part in range(3):
            lo = (3 * pair + part) * w
            qkv[part, :, pair * w : (pair + 1) * w] = grads[:, lo : lo + w].astype(f32)
    outer[...] = grads[:, 3 * cols :].astype(f32)


def whole_call(kernel, info, arrays, shapes, scratch=()):
    def spec(shape):
        return pl.BlockSpec(shape, lambda i, s: (0,) * len(shape))

    return pl.pallas_call(
        kernel,
        grid_spec=pltpu.PrefetchScalarGridSpec(
            num_scalar_prefetch=1,
            grid=(1,),
            in_specs=[spec(a.shape) for a in arrays],
            out_specs=[spec(a.shape) for a in shapes],
            scratch_shapes=list(scratch),
        ),
        out_shape=shapes,
        compiler_params=pltpu.CompilerParams(vmem_limit_bytes=48 << 20),
    )(info, *arrays)


def make_body(mesh):
    R = mesh.shape["row"]
    C = mesh.shape["col"]
    N = max(R, C)

    def row_permute(block, k):
        return lax.ppermute(block, "row", [(i, i ^ k) for i in range(R)])

    def gather_rel(block, after=None):
        if R != 4:
            return [block] + [row_permute(block, k) for k in range(1, R)]
        half = block.shape[0] // 2
        if after is not None:
            block, _ = lax.optimization_barrier((block, after))
        one = row_permute(block, 1)
        two = row_permute(block, 2)
        top = row_permute(one[:half], 2)
        low = row_permute(two[half:], 1)
        return [block, one, two, jnp.concatenate([top, low], axis=0)]

    def scatter_rel(blocks):
        if R != 4:
            total = blocks[0]
            for k in range(1, R):
                total = total + row_permute(blocks[k].astype(bf16), k).astype(f32)
            return total
        half = blocks[0].shape[0] // 2
        b = [(x[:half], x[half:]) for x in blocks]
        top2 = row_permute(b[3][0].astype(bf16), 1)
        low1 = row_permute(b[3][1].astype(bf16), 2)
        top0 = row_permute(b[1][0].astype(bf16), 1)
        low0 = row_permute(b[2][1].astype(bf16), 2)
        top2 = row_permute((b[2][0].astype(f32) + top2.astype(f32)).astype(bf16), 2)
        low1 = row_permute((b[1][1].astype(f32) + low1.astype(f32)).astype(bf16), 1)
        top = b[0][0].astype(f32) + top0.astype(f32) + top2.astype(f32)
        low = b[0][1].astype(f32) + low0.astype(f32) + low1.astype(f32)
        return jnp.concatenate([top, low], axis=0)

    def source_place(s, c):
        return (s % (R // C)) * C + c if C <= R else c

    def source_dest(s, c, k):
        slot = source_place(s, c) ^ k
        if C <= R:
            return slot, s // (R // C)
        q = C // R
        return slot // q, s * q + slot % q

    def exchange_pairs(k):
        pairs = []
        for s in range(R):
            for c in range(C):
                dr, dc = source_dest(s, c, k)
                pairs.append((s * C + c, dr * C + dc))
        return pairs

    def spread(packed):
        return [lax.ppermute(packed[k], ("row", "col"), exchange_pairs(k)) for k in range(N)]

    def bring_back(packed):
        return [
            lax.ppermute(packed[k], ("row", "col"), [(b, a) for a, b in exchange_pairs(k)])
            for k in range(N)
        ]

    def sum_everywhere(array):
        for name in ("col", "row", "dp"):
            size = mesh.shape[name]
            step = 1
            while step < size:
                other = lax.ppermute(array, name, [(i, i ^ step) for i in range(size)])
                step *= 2
                array = array + other
        return array

    def body(
        tokens,
        prefix_len,
        norm1_gain,
        norm1_bias,
        query_key_value_weight,
        query_key_value_bias,
        attention_output_weight,
        norm2_gain,
        norm2_bias,
        gate_up_projection_weight,
        down_projection_weight,
        grad_out,
    ):
        r = lax.axis_index("row")
        c = lax.axis_index("col")
        block = tokens.shape[1]
        width = tokens.shape[2]
        head_cols = query_key_value_weight.shape[2]
        pairs = head_cols // (2 * HD)
        places = (jnp.arange(R)[:, None] ^ r) * block + jnp.arange(block)[None, :]
        table = rotary_tables(places.reshape(-1))
        w_rows, _, ff_local = gate_up_projection_weight.shape
        ff_slice = ff_local // R
        ff = ff_slice * C
        q_rows = max(1, C // R)
        u = source_place(r, c)
        v = r if C <= R else r * q_rows + c % q_rows
        info = jnp.stack([r, prefix_len[0], u, v]).astype(jnp.int32)
        rows = w_rows // q_rows
        a_rows = N // C * rows
        piece = (3 * ff_slice + 127) // 128 * 128

        gain1 = norm1_gain.astype(f32)
        gain2 = norm2_gain.astype(f32)
        inputs = tokens[0].astype(f32)
        first, first_std, first_inv = layer_norm_forward(inputs, gain1, norm1_bias.astype(f32))
        seq_in = jnp.concatenate(gather_rel(first.astype(bf16)), axis=0)

        (attn_shard,) = whole_call(
            prepare_kernel,
            info,
            [query_key_value_weight.transpose(1, 0, 2), attention_output_weight],
            [jax.ShapeDtypeStruct((attention_output_weight.shape[0], 4 * head_cols), bf16)],
        )
        w_attn = lax.all_gather(attn_shard, ("dp", "col"), axis=0, tiled=True)
        (packed,) = whole_call(
            functools.partial(pack_kernel, R, q_rows),
            info,
            [gate_up_projection_weight.transpose(1, 0, 2), down_projection_weight],
            [jax.ShapeDtypeStruct((N, rows, piece), bf16)],
        )
        packed, seq_in = lax.optimization_barrier((packed, seq_in))
        held = pltpu.VMEM((N, rows, piece), bf16)
        gu_shard, down_shard = whole_call(
            functools.partial(unpack_kernel, C),
            info,
            spread(packed),
            [
                jax.ShapeDtypeStruct((a_rows, 2 * ff), bf16),
                jax.ShapeDtypeStruct((a_rows, ff), bf16),
            ],
            [held],
        )
        w_gu = lax.all_gather(gu_shard, ("dp", "col"), axis=0, tiled=True)
        w_down = lax.all_gather(down_shard, ("dp", "col"), axis=0, tiled=True)

        w_attn, _ = lax.optimization_barrier((w_attn, gu_shard))
        w_qkv = w_attn[:, : 3 * head_cols]
        w_out = w_attn[:, 3 * head_cols :]
        dy_rel = jnp.concatenate(gather_rel(grad_out[0], gu_shard), axis=0)
        dy = grad_out[0]
        bias = query_key_value_bias.astype(f32).reshape(3, pairs, 2 * HD).transpose(1, 0, 2)
        projected = nn(seq_in, w_qkv) + bias.reshape(-1)

        qkv, attended, log_sums = attend_forward(info, projected, table, R)
        own = nt(attended[:block], w_out)
        others = nt(attended[block:], w_out).astype(bf16)
        residual = scatter_rel([own] + [others[k * block : (k + 1) * block] for k in range(R - 1)])
        middle = inputs + residual

        second, second_std, second_inv = layer_norm_forward(
            middle, gain2, norm2_bias.astype(f32)
        )
        second_in = jnp.concatenate(gather_rel(second.astype(bf16)), axis=0)
        gate_up = nn(second_in, w_gu)
        gate_vals = gate_up[:, :ff]
        up_vals = gate_up[:, ff:]
        sig = jax.nn.sigmoid(gate_vals)
        swish = gate_vals * sig
        hidden = (swish * up_vals).astype(bf16)
        grad_down = tn(dy_rel, hidden).astype(bf16)
        _, w_down = lax.optimization_barrier((grad_down, w_down))
        grad_down = lax.psum_scatter(grad_down, ("dp", "col"), scatter_dimension=0, tiled=True)
        grad_hidden = nn(dy_rel, w_down)
        grad_gate = grad_hidden * up_vals * sig * (1.0 + gate_vals * (1.0 - sig))
        grad_up = grad_hidden * swish
        grad_gu_vals = jnp.concatenate([grad_gate.astype(bf16), grad_up.astype(bf16)], axis=1)
        own = nt(grad_gu_vals[:block], w_gu)
        others = nt(grad_gu_vals[block:], w_gu).astype(bf16)
        others, second_in = lax.optimization_barrier((others, second_in))
        grad_second = scatter_rel(
            [own] + [others[k * block : (k + 1) * block] for k in range(R - 1)]
        )
        grad_gu = tn(second_in, grad_gu_vals).astype(bf16)
        grad_gu = lax.psum_scatter(grad_gu, ("dp", "col"), scatter_dimension=0, tiled=True)

        grad_middle = dy.astype(f32) + layer_norm_backward(
            grad_second, second_std, second_inv, gain2
        )
        gain2_grad = jnp.sum(grad_second * second_std, axis=0)
        bias2_grad = jnp.sum(grad_second, axis=0)

        branch = jnp.concatenate(gather_rel(grad_middle.astype(bf16)), axis=0)
        branch, hidden = lax.optimization_barrier((branch, hidden))
        own = nt(hidden[:block], w_down)
        others = nt(hidden[block:], w_down).astype(bf16)
        mixed = scatter_rel([own] + [others[k * block : (k + 1) * block] for k in range(R - 1)])
        layer_out = (middle + mixed).astype(bf16)
        grad_heads = nn(branch, w_out).astype(bf16)
        grad_proj, bias_local = attend_backward(info, qkv, table, log_sums, grad_heads, R)
        bias_local = bias_local[:, 0].reshape(pairs, 3, 2 * HD)
        bias_local = bias_local.transpose(1, 0, 2).reshape(3, head_cols)
        grad_attn = jnp.concatenate(
            [tn(seq_in, grad_proj).astype(bf16), tn(branch, attended).astype(bf16)], axis=1
        )
        grad_attn = lax.psum_scatter(grad_attn, ("dp", "col"), scatter_dimension=0, tiled=True)
        own = nt(grad_proj[:block], w_qkv)
        others = nt(grad_proj[block:], w_qkv).astype(bf16)
        others, grad_gu = lax.optimization_barrier((others, grad_gu))
        grad_first = scatter_rel(
            [own] + [others[k * block : (k + 1) * block] for k in range(R - 1)]
        )
        input_grad = grad_middle + layer_norm_backward(grad_first, first_std, first_inv, gain1)
        gain1_grad = jnp.sum(grad_first * first_std, axis=0)
        bias1_grad = jnp.sum(grad_first, axis=0)

        col_offset = r * head_cols
        bias_full = lax.dynamic_update_slice(
            jnp.zeros((3, width), f32), bias_local, (jnp.int32(0), col_offset)
        )
        sums = jnp.stack([gain1_grad, bias1_grad, gain2_grad, bias2_grad])
        sums = sum_everywhere(jnp.concatenate([sums, bias_full], axis=0))
        grad_bias = lax.dynamic_slice_in_dim(sums[4:], col_offset, head_cols, 1)

        (packed,) = whole_call(
            functools.partial(pack_back_kernel, C),
            info,
            [grad_gu, grad_down],
            [jax.ShapeDtypeStruct((N, rows, piece), bf16)],
        )
        home_gu, home_down = whole_call(
            functools.partial(unpack_back_kernel, R, q_rows),
            info,
            bring_back(packed),
            [
                jax.ShapeDtypeStruct((2, w_rows, ff_local), f32),
                jax.ShapeDtypeStruct((w_rows, ff_local), f32),
            ],
            [held],
        )
        home_qkv, home_out = whole_call(
            finish_kernel,
            info,
            [grad_attn],
            [
                jax.ShapeDtypeStruct((3, grad_attn.shape[0], head_cols), f32),
                jax.ShapeDtypeStruct((grad_attn.shape[0], head_cols), f32),
            ],
        )
        return (
            layer_out[None],
            input_grad[None],
            sums[0],
            sums[1],
            home_qkv.transpose(1, 0, 2),
            grad_bias,
            home_out,
            sums[2],
            sums[3],
            home_gu.transpose(1, 0, 2),
            home_down,
        )

    return body


def solution(mesh):
    in_specs = (
        P(("dp", "col"), "row", None),
        P(("dp", "col")),
        P(),
        P(),
        P(("dp", "col"), None, "row"),
        P(None, "row"),
        P(("dp", "col"), "row"),
        P(),
        P(),
        P(("dp", "row"), None, "col"),
        P(("dp", "row"), "col"),
        P(("dp", "col"), "row", None),
    )
    out_specs = (
        P(("dp", "col"), "row", None),
        P(("dp", "col"), "row", None),
        P(),
        P(),
        P(("dp", "col"), None, "row"),
        P(None, "row"),
        P(("dp", "col"), "row"),
        P(),
        P(),
        P(("dp", "row"), None, "col"),
        P(("dp", "row"), "col"),
    )
    body = make_body(mesh)

    return jax.shard_map(body, mesh=mesh, in_specs=in_specs, out_specs=out_specs, check_vma=False)
```

```python
import functools
import math

import jax
import jax.numpy as jnp
from jax import lax
from jax.experimental import pallas as pl
from jax.experimental.pallas import tpu as pltpu
from jax.sharding import PartitionSpec as P

HD = 64
ROT = 16

norm_eps = 1e-05
rope_base = 10000.0
masked_fill = -1e30

bf16 = jnp.bfloat16
f32 = jnp.float32


def layer_norm_forward(values, norm_gain, norm_shift):
    centre = jnp.mean(values, axis=-1, keepdims=True)
    centred = values - centre
    variance = jnp.mean(centred * centred, axis=-1, keepdims=True)
    inverse = lax.rsqrt(variance + norm_eps)
    normed = centred * inverse
    return (normed * norm_gain + norm_shift, normed, inverse)


def layer_norm_backward(incoming, normed, inverse, norm_gain):
    scaled = incoming * norm_gain
    inner = jnp.mean(scaled, axis=-1, keepdims=True)
    along = jnp.mean(scaled * normed, axis=-1, keepdims=True)
    return inverse * (scaled - inner - normed * along)


def rotary_tables(places):
    half_rot = ROT // 2
    column = jnp.arange(2 * HD) % HD
    freqs = rope_base ** (-(column % half_rot).astype(f32) * 2.0 / ROT)
    angles = places.astype(f32)[:, None] * freqs[None, :]
    sines = jnp.sin(angles)
    cosine = jnp.where(column < ROT, jnp.cos(angles), 1.0)
    left = jnp.where((column >= half_rot) & (column < ROT), sines, 0.0)
    right = jnp.where(column < half_rot, -sines, 0.0)
    return jnp.stack([cosine, left, right])


def dot(left, right, dims):
    return lax.dot_general(left, right, (dims, ((), ())), preferred_element_type=f32)


def nn(left, right):
    return dot(left, right, ((1,), (0,)))


def nt(left, right):
    return dot(left, right, ((1,), (1,)))


def tn(left, right):
    return dot(left, right, ((0,), (0,)))


def key_blocks(jq, blocks):
    return max(jq + 1, blocks // 2)


def block_mask(qpos, kpos, jq, jk, blocks, prefix):
    if jk < jq:
        return None
    causal = kpos <= qpos
    if jk >= blocks // 2:
        return causal
    early = kpos < prefix
    return (causal | early) if jk == jq else early


def head_lane(head):
    lane = lax.broadcasted_iota(jnp.int32, (1, 2 * HD), 1)
    return (lane < HD) if head == 0 else (lane >= HD)


def forward_kernel(blocks, size, info, proj, table, qkv, out, sums):
    w = 2 * HD
    scale = 1.0 / math.sqrt(HD)
    r, prefix = info[0], info[1]
    for j in range(blocks):
        rows = pl.ds(j * size, size)
        cosine, left, right = table[0, rows], table[1, rows], table[2, rows]
        for part in range(2):
            x = proj[rows, part * w : (part + 1) * w]
            x = x * cosine + pltpu.roll(x, 8, 1) * left + pltpu.roll(x, w - 8, 1) * right
            qkv[rows, part * w : (part + 1) * w] = x.astype(bf16)
        qkv[rows, 2 * w : 3 * w] = proj[rows, 2 * w : 3 * w].astype(bf16)
    places = [pl.ds(pl.multiple_of((j ^ r) * size, size), size) for j in range(blocks)]
    for jq in range(blocks):
        count = key_blocks(jq, blocks)
        q = qkv[places[jq], 0:w].astype(f32) * scale
        qpos = jq * size + lax.broadcasted_iota(jnp.int32, (size, size), 0)
        results = []
        tops = []
        for head in range(2):
            qh = jnp.where(head_lane(head), q, 0.0).astype(bf16)
            scores = []
            for jk in range(count):
                s = nt(qh, qkv[places[jk], w : 2 * w])
                kpos = jk * size + lax.broadcasted_iota(jnp.int32, (size, size), 1)
                mask = block_mask(qpos, kpos, jq, jk, blocks, prefix)
                scores.append(s if mask is None else jnp.where(mask, s, masked_fill))
            top = jnp.max(scores[0], axis=1, keepdims=True)
            for s in scores[1:]:
                top = jnp.maximum(top, jnp.max(s, axis=1, keepdims=True))
            total = 0.0
            result = 0.0
            for jk in range(count):
                e = jnp.exp(scores[jk] - top)
                total = total + jnp.sum(e, axis=1, keepdims=True)
                result = result + nn(e.astype(bf16), qkv[places[jk], 2 * w : 3 * w])
            results.append(result / total)
            tops.append(top + jnp.log(total))
        out[places[jq], :] = jnp.where(head_lane(0), results[0], results[1]).astype(bf16)
        both = jnp.where(head_lane(0), tops[0], tops[1])
        flipped = both.T
        sums[0, jq, 0:8, :] = flipped[0:8]
        sums[0, jq, 8:16, :] = flipped[HD : HD + 8]


def backward_kernel(blocks, size, info, qkv, table, sums, grads, out, bias, qm, km, gm, acc):
    w = 2 * HD
    scale = 1.0 / math.sqrt(HD)
    r, prefix = info[0], info[1]
    for head in range(2):
        lanes = head_lane(head)
        for j in range(blocks):
            rows = pl.ds(j * size, size)
            q = qkv[rows, 0:w].astype(f32) * scale
            k = qkv[rows, w : 2 * w].astype(f32) * scale
            qm[head, rows] = jnp.where(lanes, q, 0.0).astype(bf16)
            km[head, rows] = jnp.where(lanes, k, 0.0).astype(bf16)
            gm[head, rows] = jnp.where(lanes, grads[rows, :].astype(f32), 0.0).astype(bf16)
    acc[...] = jnp.zeros_like(acc)
    places = [pl.ds(pl.multiple_of((j ^ r) * size, size), size) for j in range(blocks)]
    for jq in range(blocks):
        count = key_blocks(jq, blocks)
        rq = places[jq]
        qpos = jq * size + lax.broadcasted_iota(jnp.int32, (size, size), 1)
        grad_q = 0.0
        for head in range(2):
            top = sums[0, jq, 8 * head : 8 * head + 1, :]
            probs = []
            products = []
            inner = 0.0
            for jk in range(count):
                s = nt(qkv[places[jk], w : 2 * w], qm[head, rq])
                p = jnp.exp(s - top)
                kpos = jk * size + lax.broadcasted_iota(jnp.int32, (size, size), 0)
                mask = block_mask(qpos, kpos, jq, jk, blocks, prefix)
                if mask is not None:
                    p = jnp.where(mask, p, 0.0)
                t = p * nt(qkv[places[jk], 2 * w : 3 * w], gm[head, rq])
                inner = inner + jnp.sum(t, axis=0, keepdims=True)
                probs.append(p)
                products.append(t)
            for jk in range(count):
                rk = places[jk]
                d = (products[jk] - probs[jk] * inner).astype(bf16)
                acc[1, rk] += nn(probs[jk].astype(bf16), gm[head, rq])
                acc[0, rk] += nn(d, qm[head, rq])
                grad_q = grad_q + tn(d, km[head, rk])
        cosine, left, right = table[0, rq], table[1, rq], table[2, rq]
        x = grad_q
        x = x * cosine - pltpu.roll(x, 8, 1) * left - pltpu.roll(x, w - 8, 1) * right
        out[rq, 0:w] = x.astype(bf16)
    bias_q = 0.0
    bias_k = 0.0
    bias_v = 0.0
    for j in range(blocks):
        rows = pl.ds(j * size, size)
        x = acc[0, rows]
        x = x * table[0, rows]
        x = x - pltpu.roll(acc[0, rows], 8, 1) * table[1, rows]
        x = x - pltpu.roll(acc[0, rows], w - 8, 1) * table[2, rows]
        x = x.astype(bf16)
        y = acc[1, rows].astype(bf16)
        out[rows, w : 2 * w] = x
        out[rows, 2 * w : 3 * w] = y
        bias_q = bias_q + jnp.sum(out[rows, 0:w].astype(f32), axis=0, keepdims=True)
        bias_k = bias_k + jnp.sum(x.astype(f32), axis=0, keepdims=True)
        bias_v = bias_v + jnp.sum(y.astype(f32), axis=0, keepdims=True)
    row = jnp.concatenate([bias_q, bias_k, bias_v], axis=1)
    bias[0] = jnp.broadcast_to(row, (8, 3 * w))


def attend_forward(info, projected, table, blocks):
    length = projected.shape[0]
    w = 2 * HD
    pairs = projected.shape[1] // (3 * w)
    size = length // blocks
    spec = pltpu.PrefetchScalarGridSpec(
        num_scalar_prefetch=1,
        grid=(pairs,),
        in_specs=[
            pl.BlockSpec((length, 3 * w), lambda p, i: (0, p)),
            pl.BlockSpec((3, length, w), lambda p, i: (0, 0, 0)),
        ],
        out_specs=[
            pl.BlockSpec((length, 3 * w), lambda p, i: (0, p)),
            pl.BlockSpec((length, w), lambda p, i: (0, p)),
            pl.BlockSpec((1, blocks, 16, size), lambda p, i: (p, 0, 0, 0)),
        ],
    )
    return pl.pallas_call(
        lambda *refs: forward_kernel(blocks, size, *refs),
        grid_spec=spec,
        out_shape=[
            jax.ShapeDtypeStruct((length, 3 * w * pairs), bf16),
            jax.ShapeDtypeStruct((length, w * pairs), bf16),
            jax.ShapeDtypeStruct((pairs, blocks, 16, size), f32),
        ],
        name="attend_forward",
        compiler_params=pltpu.CompilerParams(vmem_limit_bytes=48 << 20),
    )(info, projected, table)


def attend_backward(info, qkv, table, sums, grads, blocks):
    length = qkv.shape[0]
    w = 2 * HD
    pairs = qkv.shape[1] // (3 * w)
    size = length // blocks
    spec = pltpu.PrefetchScalarGridSpec(
        num_scalar_prefetch=1,
        grid=(pairs,),
        in_specs=[
            pl.BlockSpec((length, 3 * w), lambda p, i: (0, p)),
            pl.BlockSpec((3, length, w), lambda p, i: (0, 0, 0)),
            pl.BlockSpec((1, blocks, 16, size), lambda p, i: (p, 0, 0, 0)),
            pl.BlockSpec((length, w), lambda p, i: (0, p)),
        ],
        out_specs=[
            pl.BlockSpec((length, 3 * w), lambda p, i: (0, p)),
            pl.BlockSpec((1, 8, 3 * w), lambda p, i: (p, 0, 0)),
        ],
        scratch_shapes=[
            pltpu.VMEM((2, length, w), bf16),
            pltpu.VMEM((2, length, w), bf16),
            pltpu.VMEM((2, length, w), bf16),
            pltpu.VMEM((2, length, w), f32),
        ],
    )
    return pl.pallas_call(
        lambda *refs: backward_kernel(blocks, size, *refs),
        grid_spec=spec,
        out_shape=[
            jax.ShapeDtypeStruct((length, 3 * w * pairs), bf16),
            jax.ShapeDtypeStruct((pairs, 8, 3 * w), f32),
        ],
        name="attend_backward",
        compiler_params=pltpu.CompilerParams(vmem_limit_bytes=48 << 20),
    )(info, qkv, table, sums, grads)


def pack_kernel(R, q, info, gate_up, down, out):
    fs = down.shape[1] // R
    rows = down.shape[0] // q
    for slot in range(R * q):
        span = pl.ds((slot % q) * rows, rows)
        lo = (slot // q) * fs
        k = slot ^ info[2]
        out[k, :, 0:fs] = gate_up[0, span, lo : lo + fs]
        out[k, :, fs : 2 * fs] = gate_up[1, span, lo : lo + fs]
        out[k, :, 2 * fs : 3 * fs] = down[span, lo : lo + fs]


def unpack_kernel(C, info, *refs):
    pieces, (gate_up, down, held) = refs[:-3], refs[-3:]
    rows = held.shape[1]
    ff = down.shape[1]
    fs = ff // C
    for k, piece in enumerate(pieces):
        held[k ^ info[3]] = piece[...]
    for place in range(len(pieces)):
        span = pl.ds((place // C) * rows, rows)
        lo = (place % C) * fs
        gate_up[span, lo : lo + fs] = held[place, :, 0:fs]
        gate_up[span, ff + lo : ff + lo + fs] = held[place, :, fs : 2 * fs]
        down[span, lo : lo + fs] = held[place, :, 2 * fs : 3 * fs]


def pack_back_kernel(C, info, gate_up, down, out):
    rows = out.shape[1]
    ff = down.shape[1]
    fs = ff // C
    for place in range(out.shape[0]):
        span = pl.ds((place // C) * rows, rows)
        lo = (place % C) * fs
        k = place ^ info[3]
        out[k, :, 0:fs] = gate_up[span, lo : lo + fs]
        out[k, :, fs : 2 * fs] = gate_up[span, ff + lo : ff + lo + fs]
        out[k, :, 2 * fs : 3 * fs] = down[span, lo : lo + fs]


def unpack_back_kernel(R, q, info, *refs):
    pieces, (gate_up, down, held) = refs[:-3], refs[-3:]
    rows = held.shape[1]
    fs = down.shape[1] // R
    for k, piece in enumerate(pieces):
        held[k ^ info[2]] = piece[...]
    for slot in range(len(pieces)):
        span = pl.ds((slot % q) * rows, rows)
        lo = (slot // q) * fs
        gate_up[0, span, lo : lo + fs] = held[slot, :, 0:fs].astype(f32)
        gate_up[1, span, lo : lo + fs] = held[slot, :, fs : 2 * fs].astype(f32)
        down[span, lo : lo + fs] = held[slot, :, 2 * fs : 3 * fs].astype(f32)


def prepare_kernel(info, qkv, outer, out):
    w = 2 * HD
    cols = outer.shape[1]
    for pair in range(cols // w):
        for part in range(3):
            lo = (3 * pair + part) * w
            out[:, lo : lo + w] = qkv[part, :, pair * w : (pair + 1) * w]
    out[:, 3 * cols :] = outer[...]


def finish_kernel(info, grads, qkv, outer):
    w = 2 * HD
    cols = outer.shape[1]
    for pair in range(cols // w):
        for part in range(3):
            lo = (3 * pair + part) * w
            qkv[part, :, pair * w : (pair + 1) * w] = grads[:, lo : lo + w].astype(f32)
    outer[...] = grads[:, 3 * cols :].astype(f32)


def whole_call(kernel, info, arrays, shapes, scratch=()):
    def spec(shape):
        return pl.BlockSpec(shape, lambda i, s: (0,) * len(shape))

    return pl.pallas_call(
        kernel,
        grid_spec=pltpu.PrefetchScalarGridSpec(
            num_scalar_prefetch=1,
            grid=(1,),
            in_specs=[spec(a.shape) for a in arrays],
            out_specs=[spec(a.shape) for a in shapes],
            scratch_shapes=list(scratch),
        ),
        out_shape=shapes,
        compiler_params=pltpu.CompilerParams(vmem_limit_bytes=48 << 20),
    )(info, *arrays)


def make_body(mesh):
    R = mesh.shape["row"]
    C = mesh.shape["col"]
    N = max(R, C)

    def row_permute(block, k):
        return lax.ppermute(block, "row", [(i, i ^ k) for i in range(R)])

    def gather_rel(block, after=None):
        if R != 4:
            return [block] + [row_permute(block, k) for k in range(1, R)]
        half = block.shape[0] // 2
        if after is not None:
            block, _ = lax.optimization_barrier((block, after))
        one = row_permute(block, 1)
        two = row_permute(block, 2)
        top = row_permute(one[:half], 2)
        low = row_permute(two[half:], 1)
        return [block, one, two, jnp.concatenate([top, low], axis=0)]

    def scatter_rel(blocks):
        if R != 4:
            total = blocks[0]
            for k in range(1, R):
                total = total + row_permute(blocks[k].astype(bf16), k).astype(f32)
            return total
        half = blocks[0].shape[0] // 2
        b = [(x[:half], x[half:]) for x in blocks]
        top2 = row_permute(b[3][0].astype(bf16), 1)
        low1 = row_permute(b[3][1].astype(bf16), 2)
        top0 = row_permute(b[1][0].astype(bf16), 1)
        low0 = row_permute(b[2][1].astype(bf16), 2)
        top2 = row_permute((b[2][0].astype(f32) + top2.astype(f32)).astype(bf16), 2)
        low1 = row_permute((b[1][1].astype(f32) + low1.astype(f32)).astype(bf16), 1)
        top = b[0][0].astype(f32) + top0.astype(f32) + top2.astype(f32)
        low = b[0][1].astype(f32) + low0.astype(f32) + low1.astype(f32)
        return jnp.concatenate([top, low], axis=0)

    def source_place(s, c):
        return (s % (R // C)) * C + c if C <= R else c

    def source_dest(s, c, k):
        slot = source_place(s, c) ^ k
        if C <= R:
            return slot, s // (R // C)
        q = C // R
        return slot // q, s * q + slot % q

    def exchange_pairs(k):
        pairs = []
        for s in range(R):
            for c in range(C):
                dr, dc = source_dest(s, c, k)
                pairs.append((s * C + c, dr * C + dc))
        return pairs

    def spread(packed):
        return [lax.ppermute(packed[k], ("row", "col"), exchange_pairs(k)) for k in range(N)]

    def bring_back(packed):
        return [
            lax.ppermute(packed[k], ("row", "col"), [(b, a) for a, b in exchange_pairs(k)])
            for k in range(N)
        ]

    def sum_everywhere(array):
        for name in ("col", "row", "dp"):
            size = mesh.shape[name]
            step = 1
            while step < size:
                other = lax.ppermute(array, name, [(i, i ^ step) for i in range(size)])
                step *= 2
                array = array + other
        return array

    def body(
        tokens,
        prefix_len,
        norm1_gain,
        norm1_bias,
        query_key_value_weight,
        query_key_value_bias,
        attention_output_weight,
        norm2_gain,
        norm2_bias,
        gate_up_projection_weight,
        down_projection_weight,
        grad_out,
    ):
        r = lax.axis_index("row")
        c = lax.axis_index("col")
        block = tokens.shape[1]
        length = block * R
        width = tokens.shape[2]
        head_cols = query_key_value_weight.shape[2]
        pairs = head_cols // (2 * HD)
        places = (jnp.arange(R)[:, None] ^ r) * block + jnp.arange(block)[None, :]
        table = rotary_tables(places.reshape(-1))
        w_rows, _, ff_local = gate_up_projection_weight.shape
        ff_slice = ff_local // R
        ff = ff_slice * C
        q_rows = max(1, C // R)
        u = source_place(r, c)
        v = r if C <= R else r * q_rows + c % q_rows
        info = jnp.stack([r, prefix_len[0], u, v]).astype(jnp.int32)
        rows = w_rows // q_rows
        a_rows = N // C * rows
        piece = (3 * ff_slice + 127) // 128 * 128

        gain1 = norm1_gain.astype(f32)
        gain2 = norm2_gain.astype(f32)
        inputs = tokens[0].astype(f32)
        first, first_std, first_inv = layer_norm_forward(inputs, gain1, norm1_bias.astype(f32))
        seq_in = jnp.concatenate(gather_rel(first.astype(bf16)), axis=0)

        (attn_shard,) = whole_call(
            prepare_kernel,
            info,
            [query_key_value_weight.transpose(1, 0, 2), attention_output_weight],
            [jax.ShapeDtypeStruct((attention_output_weight.shape[0], 4 * head_cols), bf16)],
        )
        w_attn = lax.all_gather(attn_shard, ("dp", "col"), axis=0, tiled=True)
        (packed,) = whole_call(
            functools.partial(pack_kernel, R, q_rows),
            info,
            [gate_up_projection_weight.transpose(1, 0, 2), down_projection_weight],
            [jax.ShapeDtypeStruct((N, rows, piece), bf16)],
        )
        packed, seq_in = lax.optimization_barrier((packed, seq_in))
        held = pltpu.VMEM((N, rows, piece), bf16)
        gu_shard, down_shard = whole_call(
            functools.partial(unpack_kernel, C),
            info,
            spread(packed),
            [
                jax.ShapeDtypeStruct((a_rows, 2 * ff), bf16),
                jax.ShapeDtypeStruct((a_rows, ff), bf16),
            ],
            [held],
        )
        w_gu = lax.all_gather(gu_shard, ("dp", "col"), axis=0, tiled=True)
        w_down = lax.all_gather(down_shard, ("dp", "col"), axis=0, tiled=True)

        w_attn, _ = lax.optimization_barrier((w_attn, gu_shard))
        w_qkv = w_attn[:, : 3 * head_cols]
        w_out = w_attn[:, 3 * head_cols :]
        dy_rel = jnp.concatenate(gather_rel(grad_out[0], gu_shard), axis=0)
        dy = grad_out[0]
        bias = query_key_value_bias.astype(f32).reshape(3, pairs, 2 * HD).transpose(1, 0, 2)
        projected = nn(seq_in, w_qkv)
        projected = projected + bias.reshape(-1)

        qkv, attended, log_sums = attend_forward(info, projected, table, R)
        own = nt(attended[:block], w_out)
        others = nt(attended[block:], w_out).astype(bf16)
        residual = scatter_rel([own] + [others[k * block : (k + 1) * block] for k in range(R - 1)])
        middle = inputs + residual

        second, second_std, second_inv = layer_norm_forward(
            middle, gain2, norm2_bias.astype(f32)
        )
        second_in = jnp.concatenate(gather_rel(second.astype(bf16)), axis=0)
        gate_up = nn(second_in, w_gu)
        gate_vals = gate_up[:, :ff]
        up_vals = gate_up[:, ff:]
        sig = jax.nn.sigmoid(gate_vals)
        swish = gate_vals * sig
        hidden = (swish * up_vals).astype(bf16)
        grad_down = tn(dy_rel, hidden).astype(bf16)
        _, w_down = lax.optimization_barrier((grad_down, w_down))
        grad_down = lax.psum_scatter(grad_down, ("dp", "col"), scatter_dimension=0, tiled=True)
        grad_hidden = nn(dy_rel, w_down)
        grad_gate = grad_hidden * up_vals * sig * (1.0 + gate_vals * (1.0 - sig))
        grad_up = grad_hidden * swish
        grad_gu_vals = jnp.concatenate([grad_gate.astype(bf16), grad_up.astype(bf16)], axis=1)
        own = nt(grad_gu_vals[:block], w_gu)
        others = nt(grad_gu_vals[block:], w_gu).astype(bf16)
        others, second_in = lax.optimization_barrier((others, second_in))
        grad_second = scatter_rel(
            [own] + [others[k * block : (k + 1) * block] for k in range(R - 1)]
        )
        grad_gu = tn(second_in, grad_gu_vals).astype(bf16)
        grad_gu = lax.psum_scatter(grad_gu, ("dp", "col"), scatter_dimension=0, tiled=True)

        grad_middle = dy.astype(f32) + layer_norm_backward(
            grad_second, second_std, second_inv, gain2
        )
        gain2_grad = jnp.sum(grad_second * second_std, axis=0)
        bias2_grad = jnp.sum(grad_second, axis=0)

        branch = jnp.concatenate(gather_rel(grad_middle.astype(bf16)), axis=0)
        own = nt(hidden[:block], w_down)
        others = nt(hidden[block:], w_down).astype(bf16)
        others, _ = lax.optimization_barrier((others, branch))
        mixed = scatter_rel(
            [own] + [others[k * block : (k + 1) * block] for k in range(R - 1)]
        )
        layer_out = (middle + mixed).astype(bf16)
        grad_heads = nn(branch, w_out).astype(bf16)
        grad_proj, bias_local = attend_backward(info, qkv, table, log_sums, grad_heads, R)
        bias_local = bias_local[:, 0].reshape(pairs, 3, 2 * HD)
        bias_local = bias_local.transpose(1, 0, 2).reshape(3, head_cols)
        if C == 2:
            def columns(array, which):
                parts = array.reshape(length, -1, C, w_attn.shape[0] // (C * mesh.shape["dp"]))
                return lax.dynamic_index_in_dim(parts, which, 2, keepdims=False).reshape(length, -1)

            def pair_sum(left, right):
                away = tn(columns(left, 1 - c), right).astype(bf16)
                got = lax.ppermute(away, "col", [(0, 1), (1, 0)])
                return (tn(columns(left, c), right) + got.astype(f32)).astype(bf16)

            grad_attn = jnp.concatenate(
                [pair_sum(seq_in, grad_proj), pair_sum(branch, attended)], axis=1
            )
            grad_attn = lax.psum_scatter(grad_attn, "dp", scatter_dimension=0, tiled=True)
        else:
            grad_attn = jnp.concatenate(
                [tn(seq_in, grad_proj).astype(bf16), tn(branch, attended).astype(bf16)], axis=1
            )
            grad_attn = lax.psum_scatter(grad_attn, ("dp", "col"), scatter_dimension=0, tiled=True)
        own = nt(grad_proj[:block], w_qkv)
        others = nt(grad_proj[block:], w_qkv).astype(bf16)
        others, grad_gu = lax.optimization_barrier((others, grad_gu))
        grad_first = scatter_rel(
            [own] + [others[k * block : (k + 1) * block] for k in range(R - 1)]
        )
        input_grad = grad_middle + layer_norm_backward(grad_first, first_std, first_inv, gain1)
        gain1_grad = jnp.sum(grad_first * first_std, axis=0)
        bias1_grad = jnp.sum(grad_first, axis=0)

        col_offset = r * head_cols
        bias_full = lax.dynamic_update_slice(
            jnp.zeros((3, width), f32), bias_local, (jnp.int32(0), col_offset)
        )
        sums = jnp.stack([gain1_grad, bias1_grad, gain2_grad, bias2_grad])
        sums = sum_everywhere(jnp.concatenate([sums, bias_full], axis=0))
        grad_bias = lax.dynamic_slice_in_dim(sums[4:], col_offset, head_cols, 1)

        (packed,) = whole_call(
            functools.partial(pack_back_kernel, C),
            info,
            [grad_gu, grad_down],
            [jax.ShapeDtypeStruct((N, rows, piece), bf16)],
        )
        home_gu, home_down = whole_call(
            functools.partial(unpack_back_kernel, R, q_rows),
            info,
            bring_back(packed),
            [
                jax.ShapeDtypeStruct((2, w_rows, ff_local), f32),
                jax.ShapeDtypeStruct((w_rows, ff_local), f32),
            ],
            [held],
        )
        home_qkv, home_out = whole_call(
            finish_kernel,
            info,
            [grad_attn],
            [
                jax.ShapeDtypeStruct((3, grad_attn.shape[0], head_cols), f32),
                jax.ShapeDtypeStruct((grad_attn.shape[0], head_cols), f32),
            ],
        )
        return (
            layer_out[None],
            input_grad[None],
            sums[0],
            sums[1],
            home_qkv.transpose(1, 0, 2),
            grad_bias,
            home_out,
            sums[2],
            sums[3],
            home_gu.transpose(1, 0, 2),
            home_down,
        )

    return body


def solution(mesh):
    in_specs = (
        P(("dp", "col"), "row", None),
        P(("dp", "col")),
        P(),
        P(),
        P(("dp", "col"), None, "row"),
        P(None, "row"),
        P(("dp", "col"), "row"),
        P(),
        P(),
        P(("dp", "row"), None, "col"),
        P(("dp", "row"), "col"),
        P(("dp", "col"), "row", None),
    )
    out_specs = (
        P(("dp", "col"), "row", None),
        P(("dp", "col"), "row", None),
        P(),
        P(),
        P(("dp", "col"), None, "row"),
        P(None, "row"),
        P(("dp", "col"), "row"),
        P(),
        P(),
        P(("dp", "row"), None, "col"),
        P(("dp", "row"), "col"),
    )
    body = make_body(mesh)

    return jax.shard_map(body, mesh=mesh, in_specs=in_specs, out_specs=out_specs, check_vma=False)
```

```python
import functools
import math

import jax
import jax.numpy as jnp
from jax import lax
from jax.experimental import pallas as pl
from jax.experimental.pallas import tpu as pltpu
from jax.sharding import PartitionSpec as P


HD = 64
ROT = 16

norm_eps = 1e-05
rope_base = 10000.0
masked_fill = -1e30

bf16 = jnp.bfloat16
f32 = jnp.float32


def layer_norm_forward(values, norm_gain, norm_shift):
    centre = jnp.mean(values, axis=-1, keepdims=True)
    centred = values - centre
    variance = jnp.mean(centred * centred, axis=-1, keepdims=True)
    inverse = lax.rsqrt(variance + norm_eps)
    normed = centred * inverse
    return (normed * norm_gain + norm_shift, normed, inverse)


def layer_norm_backward(incoming, normed, inverse, norm_gain):
    scaled = incoming * norm_gain
    inner = jnp.mean(scaled, axis=-1, keepdims=True)
    along = jnp.mean(scaled * normed, axis=-1, keepdims=True)
    return inverse * (scaled - inner - normed * along)


def rotary_tables(places):
    half_rot = ROT // 2
    column = jnp.arange(2 * HD) % HD
    freqs = rope_base ** (-(column % half_rot).astype(f32) * 2.0 / ROT)
    angles = places.astype(f32)[:, None] * freqs[None, :]
    sines = jnp.sin(angles)
    cosine = jnp.where(column < ROT, jnp.cos(angles), 1.0)
    left = jnp.where((column >= half_rot) & (column < ROT), sines, 0.0)
    right = jnp.where(column < half_rot, -sines, 0.0)
    return jnp.stack([cosine, left, right])


def dot(left, right, dims):
    return lax.dot_general(left, right, (dims, ((), ())), preferred_element_type=f32)


def nn(left, right):
    return dot(left, right, ((1,), (0,)))


def nt(left, right):
    return dot(left, right, ((1,), (1,)))


def tn(left, right):
    return dot(left, right, ((0,), (0,)))


def key_blocks(jq, blocks):
    return max(jq + 1, blocks // 2)


def block_mask(qpos, kpos, jq, jk, blocks, prefix):
    if jk < jq:
        return None
    causal = kpos <= qpos
    if jk >= blocks // 2:
        return causal
    early = kpos < prefix
    return (causal | early) if jk == jq else early


def head_lane(head):
    lane = lax.broadcasted_iota(jnp.int32, (1, 2 * HD), 1)
    return (lane < HD) if head == 0 else (lane >= HD)


def forward_kernel(blocks, size, info, proj, table, qkv, out, sums):
    w = 2 * HD
    scale = 1.0 / math.sqrt(HD)
    r, prefix = info[0], info[1]
    for j in range(blocks):
        rows = pl.ds(j * size, size)
        cosine, left, right = table[0, rows], table[1, rows], table[2, rows]
        for part in range(2):
            x = proj[rows, part * w : (part + 1) * w]
            x = x * cosine + pltpu.roll(x, 8, 1) * left + pltpu.roll(x, w - 8, 1) * right
            qkv[rows, part * w : (part + 1) * w] = x.astype(bf16)
        qkv[rows, 2 * w : 3 * w] = proj[rows, 2 * w : 3 * w].astype(bf16)
    places = [pl.ds(pl.multiple_of((j ^ r) * size, size), size) for j in range(blocks)]
    for jq in range(blocks):
        count = key_blocks(jq, blocks)
        q = qkv[places[jq], 0:w].astype(f32) * scale
        qpos = jq * size + lax.broadcasted_iota(jnp.int32, (size, size), 0)
        results = []
        tops = []
        for head in range(2):
            qh = jnp.where(head_lane(head), q, 0.0).astype(bf16)
            scores = []
            for jk in range(count):
                s = nt(qh, qkv[places[jk], w : 2 * w])
                kpos = jk * size + lax.broadcasted_iota(jnp.int32, (size, size), 1)
                mask = block_mask(qpos, kpos, jq, jk, blocks, prefix)
                scores.append(s if mask is None else jnp.where(mask, s, masked_fill))
            top = jnp.max(scores[0], axis=1, keepdims=True)
            for s in scores[1:]:
                top = jnp.maximum(top, jnp.max(s, axis=1, keepdims=True))
            total = 0.0
            result = 0.0
            for jk in range(count):
                e = jnp.exp(scores[jk] - top)
                total = total + jnp.sum(e, axis=1, keepdims=True)
                result = result + nn(e.astype(bf16), qkv[places[jk], 2 * w : 3 * w])
            results.append(result / total)
            tops.append(top + jnp.log(total))
        out[places[jq], :] = jnp.where(head_lane(0), results[0], results[1]).astype(bf16)
        both = jnp.where(head_lane(0), tops[0], tops[1])
        flipped = both.T
        sums[0, jq, 0:8, :] = flipped[0:8]
        sums[0, jq, 8:16, :] = flipped[HD : HD + 8]


def backward_kernel(blocks, size, info, qkv, table, sums, grads, out, bias, qm, km, gm, acc):
    w = 2 * HD
    scale = 1.0 / math.sqrt(HD)
    r, prefix = info[0], info[1]
    for head in range(2):
        lanes = head_lane(head)
        for j in range(blocks):
            rows = pl.ds(j * size, size)
            q = qkv[rows, 0:w].astype(f32) * scale
            k = qkv[rows, w : 2 * w].astype(f32) * scale
            qm[head, rows] = jnp.where(lanes, q, 0.0).astype(bf16)
            km[head, rows] = jnp.where(lanes, k, 0.0).astype(bf16)
            gm[head, rows] = jnp.where(lanes, grads[rows, :].astype(f32), 0.0).astype(bf16)
    acc[...] = jnp.zeros_like(acc)
    places = [pl.ds(pl.multiple_of((j ^ r) * size, size), size) for j in range(blocks)]
    for jq in range(blocks):
        count = key_blocks(jq, blocks)
        rq = places[jq]
        qpos = jq * size + lax.broadcasted_iota(jnp.int32, (size, size), 1)
        grad_q = 0.0
        for head in range(2):
            top = sums[0, jq, 8 * head : 8 * head + 1, :]
            probs = []
            products = []
            inner = 0.0
            for jk in range(count):
                s = nt(qkv[places[jk], w : 2 * w], qm[head, rq])
                p = jnp.exp(s - top)
                kpos = jk * size + lax.broadcasted_iota(jnp.int32, (size, size), 0)
                mask = block_mask(qpos, kpos, jq, jk, blocks, prefix)
                if mask is not None:
                    p = jnp.where(mask, p, 0.0)
                t = p * nt(qkv[places[jk], 2 * w : 3 * w], gm[head, rq])
                inner = inner + jnp.sum(t, axis=0, keepdims=True)
                probs.append(p)
                products.append(t)
            for jk in range(count):
                rk = places[jk]
                d = (products[jk] - probs[jk] * inner).astype(bf16)
                acc[1, rk] += nn(probs[jk].astype(bf16), gm[head, rq])
                acc[0, rk] += nn(d, qm[head, rq])
                grad_q = grad_q + tn(d, km[head, rk])
        cosine, left, right = table[0, rq], table[1, rq], table[2, rq]
        x = grad_q
        x = x * cosine - pltpu.roll(x, 8, 1) * left - pltpu.roll(x, w - 8, 1) * right
        out[rq, 0:w] = x.astype(bf16)
    bias_q = 0.0
    bias_k = 0.0
    bias_v = 0.0
    for j in range(blocks):
        rows = pl.ds(j * size, size)
        x = acc[0, rows]
        x = x * table[0, rows]
        x = x - pltpu.roll(acc[0, rows], 8, 1) * table[1, rows]
        x = x - pltpu.roll(acc[0, rows], w - 8, 1) * table[2, rows]
        x = x.astype(bf16)
        y = acc[1, rows].astype(bf16)
        out[rows, w : 2 * w] = x
        out[rows, 2 * w : 3 * w] = y
        bias_q = bias_q + jnp.sum(out[rows, 0:w].astype(f32), axis=0, keepdims=True)
        bias_k = bias_k + jnp.sum(x.astype(f32), axis=0, keepdims=True)
        bias_v = bias_v + jnp.sum(y.astype(f32), axis=0, keepdims=True)
    row = jnp.concatenate([bias_q, bias_k, bias_v], axis=1)
    bias[0] = jnp.broadcast_to(row, (8, 3 * w))


def attend_forward(info, projected, table, blocks):
    length = projected.shape[0]
    w = 2 * HD
    pairs = projected.shape[1] // (3 * w)
    size = length // blocks
    spec = pltpu.PrefetchScalarGridSpec(
        num_scalar_prefetch=1,
        grid=(pairs,),
        in_specs=[
            pl.BlockSpec((length, 3 * w), lambda p, i: (0, p)),
            pl.BlockSpec((3, length, w), lambda p, i: (0, 0, 0)),
        ],
        out_specs=[
            pl.BlockSpec((length, 3 * w), lambda p, i: (0, p)),
            pl.BlockSpec((length, w), lambda p, i: (0, p)),
            pl.BlockSpec((1, blocks, 16, size), lambda p, i: (p, 0, 0, 0)),
        ],
    )
    return pl.pallas_call(
        lambda *refs: forward_kernel(blocks, size, *refs),
        grid_spec=spec,
        out_shape=[
            jax.ShapeDtypeStruct((length, 3 * w * pairs), bf16),
            jax.ShapeDtypeStruct((length, w * pairs), bf16),
            jax.ShapeDtypeStruct((pairs, blocks, 16, size), f32),
        ],
        name="attend_forward",
        compiler_params=pltpu.CompilerParams(vmem_limit_bytes=48 << 20),
    )(info, projected, table)


def attend_backward(info, qkv, table, sums, grads, blocks):
    length = qkv.shape[0]
    w = 2 * HD
    pairs = qkv.shape[1] // (3 * w)
    size = length // blocks
    spec = pltpu.PrefetchScalarGridSpec(
        num_scalar_prefetch=1,
        grid=(pairs,),
        in_specs=[
            pl.BlockSpec((length, 3 * w), lambda p, i: (0, p)),
            pl.BlockSpec((3, length, w), lambda p, i: (0, 0, 0)),
            pl.BlockSpec((1, blocks, 16, size), lambda p, i: (p, 0, 0, 0)),
            pl.BlockSpec((length, w), lambda p, i: (0, p)),
        ],
        out_specs=[
            pl.BlockSpec((length, 3 * w), lambda p, i: (0, p)),
            pl.BlockSpec((1, 8, 3 * w), lambda p, i: (p, 0, 0)),
        ],
        scratch_shapes=[
            pltpu.VMEM((2, length, w), bf16),
            pltpu.VMEM((2, length, w), bf16),
            pltpu.VMEM((2, length, w), bf16),
            pltpu.VMEM((2, length, w), f32),
        ],
    )
    return pl.pallas_call(
        lambda *refs: backward_kernel(blocks, size, *refs),
        grid_spec=spec,
        out_shape=[
            jax.ShapeDtypeStruct((length, 3 * w * pairs), bf16),
            jax.ShapeDtypeStruct((pairs, 8, 3 * w), f32),
        ],
        name="attend_backward",
        compiler_params=pltpu.CompilerParams(vmem_limit_bytes=48 << 20),
    )(info, qkv, table, sums, grads)


def pack_kernel(R, q, info, gate_up, down, out):
    fs = down.shape[1] // R
    rows = down.shape[0] // q
    for slot in range(R * q):
        span = pl.ds((slot % q) * rows, rows)
        lo = (slot // q) * fs
        k = slot ^ info[2]
        out[k, :, 0:fs] = gate_up[0, span, lo : lo + fs]
        out[k, :, fs : 2 * fs] = gate_up[1, span, lo : lo + fs]
        out[k, :, 2 * fs : 3 * fs] = down[span, lo : lo + fs]


def unpack_kernel(C, info, *refs):
    pieces, (gate_up, down, held) = refs[:-3], refs[-3:]
    rows = held.shape[1]
    ff = down.shape[1]
    fs = ff // C
    for k, piece in enumerate(pieces):
        held[k ^ info[3]] = piece[...]
    for place in range(len(pieces)):
        span = pl.ds((place // C) * rows, rows)
        lo = (place % C) * fs
        gate_up[span, lo : lo + fs] = held[place, :, 0:fs]
        gate_up[span, ff + lo : ff + lo + fs] = held[place, :, fs : 2 * fs]
        down[span, lo : lo + fs] = held[place, :, 2 * fs : 3 * fs]


def pack_back_kernel(C, info, gate_up, down, out):
    rows = out.shape[1]
    ff = down.shape[1]
    fs = ff // C
    for place in range(out.shape[0]):
        span = pl.ds((place // C) * rows, rows)
        lo = (place % C) * fs
        k = place ^ info[3]
        out[k, :, 0:fs] = gate_up[span, lo : lo + fs]
        out[k, :, fs : 2 * fs] = gate_up[span, ff + lo : ff + lo + fs]
        out[k, :, 2 * fs : 3 * fs] = down[span, lo : lo + fs]


def unpack_back_kernel(R, q, info, *refs):
    pieces, (gate_up, down, held) = refs[:-3], refs[-3:]
    rows = held.shape[1]
    fs = down.shape[1] // R
    for k, piece in enumerate(pieces):
        held[k ^ info[2]] = piece[...]
    for slot in range(len(pieces)):
        span = pl.ds((slot % q) * rows, rows)
        lo = (slot // q) * fs
        gate_up[0, span, lo : lo + fs] = held[slot, :, 0:fs].astype(f32)
        gate_up[1, span, lo : lo + fs] = held[slot, :, fs : 2 * fs].astype(f32)
        down[span, lo : lo + fs] = held[slot, :, 2 * fs : 3 * fs].astype(f32)


def prepare_kernel(info, qkv, outer, out):
    w = 2 * HD
    cols = outer.shape[1]
    for pair in range(cols // w):
        for part in range(3):
            lo = (3 * pair + part) * w
            out[:, lo : lo + w] = qkv[part, :, pair * w : (pair + 1) * w]
    out[:, 3 * cols :] = outer[...]


def finish_kernel(info, grads, qkv, outer):
    w = 2 * HD
    cols = outer.shape[1]
    for pair in range(cols // w):
        for part in range(3):
            lo = (3 * pair + part) * w
            qkv[part, :, pair * w : (pair + 1) * w] = grads[:, lo : lo + w].astype(f32)
    outer[...] = grads[:, 3 * cols :].astype(f32)


def whole_call(kernel, info, arrays, shapes, scratch=()):
    def spec(shape):
        return pl.BlockSpec(shape, lambda i, s: (0,) * len(shape))

    return pl.pallas_call(
        kernel,
        grid_spec=pltpu.PrefetchScalarGridSpec(
            num_scalar_prefetch=1,
            grid=(1,),
            in_specs=[spec(a.shape) for a in arrays],
            out_specs=[spec(a.shape) for a in shapes],
            scratch_shapes=list(scratch),
        ),
        out_shape=shapes,
        compiler_params=pltpu.CompilerParams(vmem_limit_bytes=48 << 20),
    )(info, *arrays)


def split_kernel(info, mine, other, mine_out, other_out):
    mine_out[...] = mine[...]
    other_out[...] = other[...]


def split_columns(info, array, parts):
    length, width = array.shape
    block = width // (2 * parts)
    shape = jax.ShapeDtypeStruct((length, width // 2), array.dtype)
    return pl.pallas_call(
        split_kernel,
        grid_spec=pltpu.PrefetchScalarGridSpec(
            num_scalar_prefetch=1,
            grid=(parts,),
            in_specs=[
                pl.BlockSpec((length, block), lambda j, s: (0, 2 * j + s[4])),
                pl.BlockSpec((length, block), lambda j, s: (0, 2 * j + 1 - s[4])),
            ],
            out_specs=[pl.BlockSpec((length, block), lambda j, s: (0, j))] * 2,
        ),
        out_shape=[shape, shape],
    )(info, array, array)


def make_body(mesh):
    R = mesh.shape["row"]
    C = mesh.shape["col"]
    N = max(R, C)

    def row_permute(block, k):
        return lax.ppermute(block, "row", [(i, i ^ k) for i in range(R)])

    def gather_rel(block, after=None):
        if R != 4:
            return [block] + [row_permute(block, k) for k in range(1, R)]
        half = block.shape[0] // 2
        if after is not None:
            block, _ = lax.optimization_barrier((block, after))
        one = row_permute(block, 1)
        two = row_permute(block, 2)
        top = row_permute(one[:half], 2)
        low = row_permute(two[half:], 1)
        return [block, one, two, jnp.concatenate([top, low], axis=0)]

    def scatter_rel(blocks):
        if R != 4:
            total = blocks[0]
            for k in range(1, R):
                total = total + row_permute(blocks[k].astype(bf16), k).astype(f32)
            return total
        half = blocks[0].shape[0] // 2
        b = [(x[:half], x[half:]) for x in blocks]
        top2 = row_permute(b[3][0].astype(bf16), 1)
        low1 = row_permute(b[3][1].astype(bf16), 2)
        top0 = row_permute(b[1][0].astype(bf16), 1)
        low0 = row_permute(b[2][1].astype(bf16), 2)
        top2 = row_permute((b[2][0].astype(f32) + top2.astype(f32)).astype(bf16), 2)
        low1 = row_permute((b[1][1].astype(f32) + low1.astype(f32)).astype(bf16), 1)
        top = b[0][0].astype(f32) + top0.astype(f32) + top2.astype(f32)
        low = b[0][1].astype(f32) + low0.astype(f32) + low1.astype(f32)
        return jnp.concatenate([top, low], axis=0)

    def source_place(s, c):
        return (s % (R // C)) * C + c if C <= R else c

    def source_dest(s, c, k):
        slot = source_place(s, c) ^ k
        if C <= R:
            return slot, s // (R // C)
        q = C // R
        return slot // q, s * q + slot % q

    def exchange_pairs(k):
        pairs = []
        for s in range(R):
            for c in range(C):
                dr, dc = source_dest(s, c, k)
                pairs.append((s * C + c, dr * C + dc))
        return pairs

    def spread(packed):
        return [lax.ppermute(packed[k], ("row", "col"), exchange_pairs(k)) for k in range(N)]

    def bring_back(packed):
        return [
            lax.ppermute(packed[k], ("row", "col"), [(b, a) for a, b in exchange_pairs(k)])
            for k in range(N)
        ]

    def sum_everywhere(array):
        for name in ("col", "row", "dp"):
            size = mesh.shape[name]
            step = 1
            while step < size:
                other = lax.ppermute(array, name, [(i, i ^ step) for i in range(size)])
                step *= 2
                array = array + other
        return array

    def body(
        tokens,
        prefix_len,
        norm1_gain,
        norm1_bias,
        query_key_value_weight,
        query_key_value_bias,
        attention_output_weight,
        norm2_gain,
        norm2_bias,
        gate_up_projection_weight,
        down_projection_weight,
        grad_out,
    ):
        r = lax.axis_index("row")
        c = lax.axis_index("col")
        block = tokens.shape[1]
        width = tokens.shape[2]
        head_cols = query_key_value_weight.shape[2]
        pairs = head_cols // (2 * HD)
        places = (jnp.arange(R)[:, None] ^ r) * block + jnp.arange(block)[None, :]
        table = rotary_tables(places.reshape(-1))
        w_rows, _, ff_local = gate_up_projection_weight.shape
        ff_slice = ff_local // R
        ff = ff_slice * C
        q_rows = max(1, C // R)
        u = source_place(r, c)
        v = r if C <= R else r * q_rows + c % q_rows
        info = jnp.stack([r, prefix_len[0], u, v, c]).astype(jnp.int32)
        rows = w_rows // q_rows
        a_rows = N // C * rows
        piece = (3 * ff_slice + 127) // 128 * 128

        gain1 = norm1_gain.astype(f32)
        gain2 = norm2_gain.astype(f32)
        inputs = tokens[0].astype(f32)
        first, first_std, first_inv = layer_norm_forward(inputs, gain1, norm1_bias.astype(f32))
        seq_in = jnp.concatenate(gather_rel(first.astype(bf16)), axis=0)

        (attn_shard,) = whole_call(
            prepare_kernel,
            info,
            [query_key_value_weight.transpose(1, 0, 2), attention_output_weight],
            [jax.ShapeDtypeStruct((attention_output_weight.shape[0], 4 * head_cols), bf16)],
        )
        w_attn = lax.all_gather(attn_shard, ("dp", "col"), axis=0, tiled=True)
        (packed,) = whole_call(
            functools.partial(pack_kernel, R, q_rows),
            info,
            [gate_up_projection_weight.transpose(1, 0, 2), down_projection_weight],
            [jax.ShapeDtypeStruct((N, rows, piece), bf16)],
        )
        packed, seq_in = lax.optimization_barrier((packed, seq_in))
        held = pltpu.VMEM((N, rows, piece), bf16)
        gu_shard, down_shard = whole_call(
            functools.partial(unpack_kernel, C),
            info,
            spread(packed),
            [
                jax.ShapeDtypeStruct((a_rows, 2 * ff), bf16),
                jax.ShapeDtypeStruct((a_rows, ff), bf16),
            ],
            [held],
        )
        w_gu = lax.all_gather(gu_shard, ("dp", "col"), axis=0, tiled=True)
        w_down = lax.all_gather(down_shard, ("dp", "col"), axis=0, tiled=True)

        w_attn, _ = lax.optimization_barrier((w_attn, gu_shard))
        w_qkv = w_attn[:, : 3 * head_cols]
        w_out = w_attn[:, 3 * head_cols :]
        dy_rel = jnp.concatenate(gather_rel(grad_out[0], gu_shard), axis=0)
        dy = grad_out[0]
        bias = query_key_value_bias.astype(f32).reshape(3, pairs, 2 * HD).transpose(1, 0, 2)
        projected = nn(seq_in, w_qkv)
        projected = projected + bias.reshape(-1)

        qkv, attended, log_sums = attend_forward(info, projected, table, R)
        own = nt(attended[:block], w_out)
        others = nt(attended[block:], w_out).astype(bf16)
        residual = scatter_rel([own] + [others[k * block : (k + 1) * block] for k in range(R - 1)])
        middle = inputs + residual

        second, second_std, second_inv = layer_norm_forward(
            middle, gain2, norm2_bias.astype(f32)
        )
        second_in = jnp.concatenate(gather_rel(second.astype(bf16)), axis=0)
        gate_up = nn(second_in, w_gu)
        gate_vals = gate_up[:, :ff]
        up_vals = gate_up[:, ff:]
        sig = jax.nn.sigmoid(gate_vals)
        swish = gate_vals * sig
        hidden = (swish * up_vals).astype(bf16)
        grad_down = tn(dy_rel, hidden).astype(bf16)
        _, w_down = lax.optimization_barrier((grad_down, w_down))
        grad_down = lax.psum_scatter(grad_down, ("dp", "col"), scatter_dimension=0, tiled=True)
        grad_hidden = nn(dy_rel, w_down)
        grad_gate = grad_hidden * up_vals * sig * (1.0 + gate_vals * (1.0 - sig))
        grad_up = grad_hidden * swish
        grad_gu_vals = jnp.concatenate([grad_gate.astype(bf16), grad_up.astype(bf16)], axis=1)
        own = nt(grad_gu_vals[:block], w_gu)
        others = nt(grad_gu_vals[block:], w_gu).astype(bf16)
        others, second_in = lax.optimization_barrier((others, second_in))
        grad_second = scatter_rel(
            [own] + [others[k * block : (k + 1) * block] for k in range(R - 1)]
        )
        grad_gu = tn(second_in, grad_gu_vals).astype(bf16)
        grad_gu = lax.psum_scatter(grad_gu, ("dp", "col"), scatter_dimension=0, tiled=True)

        grad_middle = dy.astype(f32) + layer_norm_backward(
            grad_second, second_std, second_inv, gain2
        )
        gain2_grad = jnp.sum(grad_second * second_std, axis=0)
        bias2_grad = jnp.sum(grad_second, axis=0)

        branch = jnp.concatenate(gather_rel(grad_middle.astype(bf16)), axis=0)
        own = nt(hidden[:block], w_down)
        others = nt(hidden[block:], w_down).astype(bf16)
        others, _ = lax.optimization_barrier((others, branch))
        mixed = scatter_rel(
            [own] + [others[k * block : (k + 1) * block] for k in range(R - 1)]
        )
        layer_out = (middle + mixed).astype(bf16)
        grad_heads = nn(branch, w_out).astype(bf16)
        grad_proj, bias_local = attend_backward(info, qkv, table, log_sums, grad_heads, R)
        bias_local = bias_local[:, 0].reshape(pairs, 3, 2 * HD)
        bias_local = bias_local.transpose(1, 0, 2).reshape(3, head_cols)
        if C == 2:
            def pair_sum(left, right):
                mine, other = split_columns(info, left, mesh.shape["dp"])
                got = lax.ppermute(tn(other, right).astype(bf16), "col", [(0, 1), (1, 0)])
                return (tn(mine, right) + got.astype(f32)).astype(bf16)

            grad_attn = jnp.concatenate(
                [pair_sum(seq_in, grad_proj), pair_sum(branch, attended)],
                axis=1,
            )
            grad_attn = lax.psum_scatter(grad_attn, "dp", scatter_dimension=0, tiled=True)
        else:
            grad_attn = jnp.concatenate(
                [tn(seq_in, grad_proj).astype(bf16), tn(branch, attended).astype(bf16)], axis=1
            )
            grad_attn = lax.psum_scatter(grad_attn, ("dp", "col"), scatter_dimension=0, tiled=True)
        own = nt(grad_proj[:block], w_qkv)
        others = nt(grad_proj[block:], w_qkv).astype(bf16)
        grad_first = scatter_rel(
            [own] + [others[k * block : (k + 1) * block] for k in range(R - 1)]
        )
        input_grad = grad_middle + layer_norm_backward(grad_first, first_std, first_inv, gain1)
        gain1_grad = jnp.sum(grad_first * first_std, axis=0)
        bias1_grad = jnp.sum(grad_first, axis=0)

        col_offset = r * head_cols
        bias_full = lax.dynamic_update_slice(
            jnp.zeros((3, width), f32), bias_local, (jnp.int32(0), col_offset)
        )
        sums = jnp.stack([gain1_grad, bias1_grad, gain2_grad, bias2_grad])
        sums = sum_everywhere(jnp.concatenate([sums, bias_full], axis=0))
        grad_bias = lax.dynamic_slice_in_dim(sums[4:], col_offset, head_cols, 1)

        (packed,) = whole_call(
            functools.partial(pack_back_kernel, C),
            info,
            [grad_gu, grad_down],
            [jax.ShapeDtypeStruct((N, rows, piece), bf16)],
        )
        home_gu, home_down = whole_call(
            functools.partial(unpack_back_kernel, R, q_rows),
            info,
            bring_back(packed),
            [
                jax.ShapeDtypeStruct((2, w_rows, ff_local), f32),
                jax.ShapeDtypeStruct((w_rows, ff_local), f32),
            ],
            [held],
        )
        home_qkv, home_out = whole_call(
            finish_kernel,
            info,
            [grad_attn],
            [
                jax.ShapeDtypeStruct((3, grad_attn.shape[0], head_cols), f32),
                jax.ShapeDtypeStruct((grad_attn.shape[0], head_cols), f32),
            ],
        )
        return (
            layer_out[None],
            input_grad[None],
            sums[0],
            sums[1],
            home_qkv.transpose(1, 0, 2),
            grad_bias,
            home_out,
            sums[2],
            sums[3],
            home_gu.transpose(1, 0, 2),
            home_down,
        )

    return body


def solution(mesh):
    in_specs = (
        P(("dp", "col"), "row", None),
        P(("dp", "col")),
        P(),
        P(),
        P(("dp", "col"), None, "row"),
        P(None, "row"),
        P(("dp", "col"), "row"),
        P(),
        P(),
        P(("dp", "row"), None, "col"),
        P(("dp", "row"), "col"),
        P(("dp", "col"), "row", None),
    )
    out_specs = (
        P(("dp", "col"), "row", None),
        P(("dp", "col"), "row", None),
        P(),
        P(),
        P(("dp", "col"), None, "row"),
        P(None, "row"),
        P(("dp", "col"), "row"),
        P(),
        P(),
        P(("dp", "row"), None, "col"),
        P(("dp", "row"), "col"),
    )
    body = make_body(mesh)

    return jax.shard_map(body, mesh=mesh, in_specs=in_specs, out_specs=out_specs, check_vma=False)
```

```python
import functools
import math

import jax
import jax.numpy as jnp
from jax import lax
from jax.experimental import pallas as pl
from jax.experimental.pallas import tpu as pltpu
from jax.sharding import PartitionSpec as P


HD = 64
ROT = 16

norm_eps = 1e-05
rope_base = 10000.0
masked_fill = -1e30

bf16 = jnp.bfloat16
f32 = jnp.float32


def layer_norm_forward(values, norm_gain, norm_shift):
    centre = jnp.mean(values, axis=-1, keepdims=True)
    centred = values - centre
    variance = jnp.mean(centred * centred, axis=-1, keepdims=True)
    inverse = lax.rsqrt(variance + norm_eps)
    normed = centred * inverse
    return (normed * norm_gain + norm_shift, normed, inverse)


def layer_norm_backward(incoming, normed, inverse, norm_gain):
    scaled = incoming * norm_gain
    inner = jnp.mean(scaled, axis=-1, keepdims=True)
    along = jnp.mean(scaled * normed, axis=-1, keepdims=True)
    return inverse * (scaled - inner - normed * along)


def rotary_tables(places):
    half_rot = ROT // 2
    column = jnp.arange(2 * HD) % HD
    freqs = rope_base ** (-(column % half_rot).astype(f32) * 2.0 / ROT)
    angles = places.astype(f32)[:, None] * freqs[None, :]
    sines = jnp.sin(angles)
    cosine = jnp.where(column < ROT, jnp.cos(angles), 1.0)
    left = jnp.where((column >= half_rot) & (column < ROT), sines, 0.0)
    right = jnp.where(column < half_rot, -sines, 0.0)
    return jnp.stack([cosine, left, right])


def dot(left, right, dims):
    return lax.dot_general(left, right, (dims, ((), ())), preferred_element_type=f32)


def nn(left, right):
    return dot(left, right, ((1,), (0,)))


def nt(left, right):
    return dot(left, right, ((1,), (1,)))


def tn(left, right):
    return dot(left, right, ((0,), (0,)))


def key_blocks(jq, blocks):
    return max(jq + 1, blocks // 2)


def block_mask(qpos, kpos, jq, jk, blocks, prefix):
    if jk < jq:
        return None
    causal = kpos <= qpos
    if jk >= blocks // 2:
        return causal
    early = kpos < prefix
    return (causal | early) if jk == jq else early


def head_lane(head):
    lane = lax.broadcasted_iota(jnp.int32, (1, 2 * HD), 1)
    return (lane < HD) if head == 0 else (lane >= HD)


def forward_kernel(blocks, size, info, proj, table, qkv, out, sums):
    w = 2 * HD
    scale = 1.0 / math.sqrt(HD)
    r, prefix = info[0], info[1]
    for j in range(blocks):
        rows = pl.ds(j * size, size)
        cosine, left, right = table[0, rows], table[1, rows], table[2, rows]
        for part in range(2):
            x = proj[rows, part * w : (part + 1) * w]
            x = x * cosine + pltpu.roll(x, 8, 1) * left + pltpu.roll(x, w - 8, 1) * right
            qkv[rows, part * w : (part + 1) * w] = x.astype(bf16)
        qkv[rows, 2 * w : 3 * w] = proj[rows, 2 * w : 3 * w].astype(bf16)
    places = [pl.ds(pl.multiple_of((j ^ r) * size, size), size) for j in range(blocks)]
    for jq in range(blocks):
        count = key_blocks(jq, blocks)
        q = qkv[places[jq], 0:w].astype(f32) * scale
        qpos = jq * size + lax.broadcasted_iota(jnp.int32, (size, size), 0)
        results = []
        tops = []
        for head in range(2):
            qh = jnp.where(head_lane(head), q, 0.0).astype(bf16)
            scores = []
            for jk in range(count):
                s = nt(qh, qkv[places[jk], w : 2 * w])
                kpos = jk * size + lax.broadcasted_iota(jnp.int32, (size, size), 1)
                mask = block_mask(qpos, kpos, jq, jk, blocks, prefix)
                scores.append(s if mask is None else jnp.where(mask, s, masked_fill))
            top = jnp.max(scores[0], axis=1, keepdims=True)
            for s in scores[1:]:
                top = jnp.maximum(top, jnp.max(s, axis=1, keepdims=True))
            total = 0.0
            result = 0.0
            for jk in range(count):
                e = jnp.exp(scores[jk] - top)
                total = total + jnp.sum(e, axis=1, keepdims=True)
                result = result + nn(e.astype(bf16), qkv[places[jk], 2 * w : 3 * w])
            results.append(result / total)
            tops.append(top + jnp.log(total))
        out[places[jq], :] = jnp.where(head_lane(0), results[0], results[1]).astype(bf16)
        both = jnp.where(head_lane(0), tops[0], tops[1])
        flipped = both.T
        sums[0, jq, 0:8, :] = flipped[0:8]
        sums[0, jq, 8:16, :] = flipped[HD : HD + 8]


def backward_kernel(blocks, size, info, qkv, table, sums, grads, out, bias, qm, km, gm, acc):
    w = 2 * HD
    scale = 1.0 / math.sqrt(HD)
    r, prefix = info[0], info[1]
    for head in range(2):
        lanes = head_lane(head)
        for j in range(blocks):
            rows = pl.ds(j * size, size)
            q = qkv[rows, 0:w].astype(f32) * scale
            k = qkv[rows, w : 2 * w].astype(f32) * scale
            qm[head, rows] = jnp.where(lanes, q, 0.0).astype(bf16)
            km[head, rows] = jnp.where(lanes, k, 0.0).astype(bf16)
            gm[head, rows] = jnp.where(lanes, grads[rows, :].astype(f32), 0.0).astype(bf16)
    acc[...] = jnp.zeros_like(acc)
    places = [pl.ds(pl.multiple_of((j ^ r) * size, size), size) for j in range(blocks)]
    for jq in range(blocks):
        count = key_blocks(jq, blocks)
        rq = places[jq]
        qpos = jq * size + lax.broadcasted_iota(jnp.int32, (size, size), 1)
        grad_q = 0.0
        for head in range(2):
            top = sums[0, jq, 8 * head : 8 * head + 1, :]
            probs = []
            products = []
            inner = 0.0
            for jk in range(count):
                s = nt(qkv[places[jk], w : 2 * w], qm[head, rq])
                p = jnp.exp(s - top)
                kpos = jk * size + lax.broadcasted_iota(jnp.int32, (size, size), 0)
                mask = block_mask(qpos, kpos, jq, jk, blocks, prefix)
                if mask is not None:
                    p = jnp.where(mask, p, 0.0)
                t = p * nt(qkv[places[jk], 2 * w : 3 * w], gm[head, rq])
                inner = inner + jnp.sum(t, axis=0, keepdims=True)
                probs.append(p)
                products.append(t)
            for jk in range(count):
                rk = places[jk]
                d = (products[jk] - probs[jk] * inner).astype(bf16)
                acc[1, rk] += nn(probs[jk].astype(bf16), gm[head, rq])
                acc[0, rk] += nn(d, qm[head, rq])
                grad_q = grad_q + tn(d, km[head, rk])
        cosine, left, right = table[0, rq], table[1, rq], table[2, rq]
        x = grad_q
        x = x * cosine - pltpu.roll(x, 8, 1) * left - pltpu.roll(x, w - 8, 1) * right
        out[rq, 0:w] = x.astype(bf16)
    bias_q = 0.0
    bias_k = 0.0
    bias_v = 0.0
    for j in range(blocks):
        rows = pl.ds(j * size, size)
        x = acc[0, rows]
        x = x * table[0, rows]
        x = x - pltpu.roll(acc[0, rows], 8, 1) * table[1, rows]
        x = x - pltpu.roll(acc[0, rows], w - 8, 1) * table[2, rows]
        x = x.astype(bf16)
        y = acc[1, rows].astype(bf16)
        out[rows, w : 2 * w] = x
        out[rows, 2 * w : 3 * w] = y
        bias_q = bias_q + jnp.sum(out[rows, 0:w].astype(f32), axis=0, keepdims=True)
        bias_k = bias_k + jnp.sum(x.astype(f32), axis=0, keepdims=True)
        bias_v = bias_v + jnp.sum(y.astype(f32), axis=0, keepdims=True)
    row = jnp.concatenate([bias_q, bias_k, bias_v], axis=1)
    bias[0] = jnp.broadcast_to(row, (8, 3 * w))


def attend_forward(info, projected, table, blocks):
    length = projected.shape[0]
    w = 2 * HD
    pairs = projected.shape[1] // (3 * w)
    size = length // blocks
    spec = pltpu.PrefetchScalarGridSpec(
        num_scalar_prefetch=1,
        grid=(pairs,),
        in_specs=[
            pl.BlockSpec((length, 3 * w), lambda p, i: (0, p)),
            pl.BlockSpec((3, length, w), lambda p, i: (0, 0, 0)),
        ],
        out_specs=[
            pl.BlockSpec((length, 3 * w), lambda p, i: (0, p)),
            pl.BlockSpec((length, w), lambda p, i: (0, p)),
            pl.BlockSpec((1, blocks, 16, size), lambda p, i: (p, 0, 0, 0)),
        ],
    )
    return pl.pallas_call(
        lambda *refs: forward_kernel(blocks, size, *refs),
        grid_spec=spec,
        out_shape=[
            jax.ShapeDtypeStruct((length, 3 * w * pairs), bf16),
            jax.ShapeDtypeStruct((length, w * pairs), bf16),
            jax.ShapeDtypeStruct((pairs, blocks, 16, size), f32),
        ],
        name="attend_forward",
        compiler_params=pltpu.CompilerParams(vmem_limit_bytes=48 << 20),
    )(info, projected, table)


def attend_backward(info, qkv, table, sums, grads, blocks):
    length = qkv.shape[0]
    w = 2 * HD
    pairs = qkv.shape[1] // (3 * w)
    size = length // blocks
    spec = pltpu.PrefetchScalarGridSpec(
        num_scalar_prefetch=1,
        grid=(pairs,),
        in_specs=[
            pl.BlockSpec((length, 3 * w), lambda p, i: (0, p)),
            pl.BlockSpec((3, length, w), lambda p, i: (0, 0, 0)),
            pl.BlockSpec((1, blocks, 16, size), lambda p, i: (p, 0, 0, 0)),
            pl.BlockSpec((length, w), lambda p, i: (0, p)),
        ],
        out_specs=[
            pl.BlockSpec((length, 3 * w), lambda p, i: (0, p)),
            pl.BlockSpec((1, 8, 3 * w), lambda p, i: (p, 0, 0)),
        ],
        scratch_shapes=[
            pltpu.VMEM((2, length, w), bf16),
            pltpu.VMEM((2, length, w), bf16),
            pltpu.VMEM((2, length, w), bf16),
            pltpu.VMEM((2, length, w), f32),
        ],
    )
    return pl.pallas_call(
        lambda *refs: backward_kernel(blocks, size, *refs),
        grid_spec=spec,
        out_shape=[
            jax.ShapeDtypeStruct((length, 3 * w * pairs), bf16),
            jax.ShapeDtypeStruct((pairs, 8, 3 * w), f32),
        ],
        name="attend_backward",
        compiler_params=pltpu.CompilerParams(vmem_limit_bytes=48 << 20),
    )(info, qkv, table, sums, grads)


def pack_kernel(R, q, info, gate_up, down, out):
    fs = down.shape[1] // R
    rows = down.shape[0] // q
    for slot in range(R * q):
        span = pl.ds((slot % q) * rows, rows)
        lo = (slot // q) * fs
        k = slot ^ info[2]
        out[k, :, 0:fs] = gate_up[0, span, lo : lo + fs]
        out[k, :, fs : 2 * fs] = gate_up[1, span, lo : lo + fs]
        out[k, :, 2 * fs : 3 * fs] = down[span, lo : lo + fs]


def unpack_kernel(C, info, *refs):
    pieces, (gate_up, down, held) = refs[:-3], refs[-3:]
    rows = held.shape[1]
    ff = down.shape[1]
    fs = ff // C
    for k, piece in enumerate(pieces):
        held[k ^ info[3]] = piece[...]
    for place in range(len(pieces)):
        span = pl.ds((place // C) * rows, rows)
        lo = (place % C) * fs
        gate_up[span, lo : lo + fs] = held[place, :, 0:fs]
        gate_up[span, ff + lo : ff + lo + fs] = held[place, :, fs : 2 * fs]
        down[span, lo : lo + fs] = held[place, :, 2 * fs : 3 * fs]


def pack_back_kernel(C, info, gate_up, down, out):
    rows = out.shape[1]
    ff = down.shape[1]
    fs = ff // C
    for place in range(out.shape[0]):
        span = pl.ds((place // C) * rows, rows)
        lo = (place % C) * fs
        k = place ^ info[3]
        out[k, :, 0:fs] = gate_up[span, lo : lo + fs]
        out[k, :, fs : 2 * fs] = gate_up[span, ff + lo : ff + lo + fs]
        out[k, :, 2 * fs : 3 * fs] = down[span, lo : lo + fs]


def unpack_back_kernel(R, q, info, *refs):
    pieces, (gate_up, down, held) = refs[:-3], refs[-3:]
    rows = held.shape[1]
    fs = down.shape[1] // R
    for k, piece in enumerate(pieces):
        held[k ^ info[2]] = piece[...]
    for slot in range(len(pieces)):
        span = pl.ds((slot % q) * rows, rows)
        lo = (slot // q) * fs
        gate_up[0, span, lo : lo + fs] = held[slot, :, 0:fs].astype(f32)
        gate_up[1, span, lo : lo + fs] = held[slot, :, fs : 2 * fs].astype(f32)
        down[span, lo : lo + fs] = held[slot, :, 2 * fs : 3 * fs].astype(f32)


def prepare_kernel(info, qkv, outer, out):
    w = 2 * HD
    cols = outer.shape[1]
    for pair in range(cols // w):
        for part in range(3):
            lo = (3 * pair + part) * w
            out[:, lo : lo + w] = qkv[part, :, pair * w : (pair + 1) * w]
    out[:, 3 * cols :] = outer[...]


def finish_kernel(info, grads, qkv, outer):
    w = 2 * HD
    cols = outer.shape[1]
    for pair in range(cols // w):
        for part in range(3):
            lo = (3 * pair + part) * w
            qkv[part, :, pair * w : (pair + 1) * w] = grads[:, lo : lo + w].astype(f32)
    outer[...] = grads[:, 3 * cols :].astype(f32)


def whole_call(kernel, info, arrays, shapes, scratch=()):
    def spec(shape):
        return pl.BlockSpec(shape, lambda i, s: (0,) * len(shape))

    return pl.pallas_call(
        kernel,
        grid_spec=pltpu.PrefetchScalarGridSpec(
            num_scalar_prefetch=1,
            grid=(1,),
            in_specs=[spec(a.shape) for a in arrays],
            out_specs=[spec(a.shape) for a in shapes],
            scratch_shapes=list(scratch),
        ),
        out_shape=shapes,
        compiler_params=pltpu.CompilerParams(vmem_limit_bytes=48 << 20),
    )(info, *arrays)


def split_kernel(info, mine, other, mine_out, other_out):
    mine_out[...] = mine[...]
    other_out[...] = other[...]


def split_columns(info, array, parts):
    length, width = array.shape
    block = width // (2 * parts)
    shape = jax.ShapeDtypeStruct((length, width // 2), array.dtype)
    return pl.pallas_call(
        split_kernel,
        grid_spec=pltpu.PrefetchScalarGridSpec(
            num_scalar_prefetch=1,
            grid=(parts,),
            in_specs=[
                pl.BlockSpec((length, block), lambda j, s: (0, 2 * j + s[4])),
                pl.BlockSpec((length, block), lambda j, s: (0, 2 * j + 1 - s[4])),
            ],
            out_specs=[pl.BlockSpec((length, block), lambda j, s: (0, j))] * 2,
        ),
        out_shape=[shape, shape],
    )(info, array, array)


def make_body(mesh):
    R = mesh.shape["row"]
    C = mesh.shape["col"]
    N = max(R, C)

    def row_permute(block, k):
        return lax.ppermute(block, "row", [(i, i ^ k) for i in range(R)])

    def gather_rel(block, after=None):
        if R != 4:
            return [block] + [row_permute(block, k) for k in range(1, R)]
        half = block.shape[0] // 2
        if after is not None:
            block, _ = lax.optimization_barrier((block, after))
        one = row_permute(block, 1)
        two = row_permute(block, 2)
        top = row_permute(one[:half], 2)
        low = row_permute(two[half:], 1)
        return [block, one, two, jnp.concatenate([top, low], axis=0)]

    def scatter_rel(blocks):
        if R != 4:
            total = blocks[0]
            for k in range(1, R):
                total = total + row_permute(blocks[k].astype(bf16), k).astype(f32)
            return total
        half = blocks[0].shape[0] // 2
        b = [(x[:half], x[half:]) for x in blocks]
        top2 = row_permute(b[3][0].astype(bf16), 1)
        low1 = row_permute(b[3][1].astype(bf16), 2)
        top0 = row_permute(b[1][0].astype(bf16), 1)
        low0 = row_permute(b[2][1].astype(bf16), 2)
        top2 = row_permute((b[2][0].astype(f32) + top2.astype(f32)).astype(bf16), 2)
        low1 = row_permute((b[1][1].astype(f32) + low1.astype(f32)).astype(bf16), 1)
        top = b[0][0].astype(f32) + top0.astype(f32) + top2.astype(f32)
        low = b[0][1].astype(f32) + low0.astype(f32) + low1.astype(f32)
        return jnp.concatenate([top, low], axis=0)

    def source_place(s, c):
        return (s % (R // C)) * C + c if C <= R else c

    def source_dest(s, c, k):
        slot = source_place(s, c) ^ k
        if C <= R:
            return slot, s // (R // C)
        q = C // R
        return slot // q, s * q + slot % q

    def exchange_pairs(k):
        pairs = []
        for s in range(R):
            for c in range(C):
                dr, dc = source_dest(s, c, k)
                pairs.append((s * C + c, dr * C + dc))
        return pairs

    def spread(packed):
        return [lax.ppermute(packed[k], ("row", "col"), exchange_pairs(k)) for k in range(N)]

    def bring_back(packed):
        return [
            lax.ppermute(packed[k], ("row", "col"), [(b, a) for a, b in exchange_pairs(k)])
            for k in range(N)
        ]

    def sum_everywhere(array):
        for name in ("col", "row", "dp"):
            size = mesh.shape[name]
            step = 1
            while step < size:
                other = lax.ppermute(array, name, [(i, i ^ step) for i in range(size)])
                step *= 2
                array = array + other
        return array

    def pair_sum(mine, other, right):
        away = tn(other, right).astype(bf16)
        got = lax.ppermute(away, "col", [(0, 1), (1, 0)])
        return (tn(mine, right) + got.astype(f32)).astype(bf16)

    def body(
        tokens,
        prefix_len,
        norm1_gain,
        norm1_bias,
        query_key_value_weight,
        query_key_value_bias,
        attention_output_weight,
        norm2_gain,
        norm2_bias,
        gate_up_projection_weight,
        down_projection_weight,
        grad_out,
    ):
        r = lax.axis_index("row")
        c = lax.axis_index("col")
        block = tokens.shape[1]
        width = tokens.shape[2]
        head_cols = query_key_value_weight.shape[2]
        pairs = head_cols // (2 * HD)
        places = (jnp.arange(R)[:, None] ^ r) * block + jnp.arange(block)[None, :]
        table = rotary_tables(places.reshape(-1))
        w_rows, _, ff_local = gate_up_projection_weight.shape
        ff_slice = ff_local // R
        ff = ff_slice * C
        q_rows = max(1, C // R)
        u = source_place(r, c)
        v = r if C <= R else r * q_rows + c % q_rows
        info = jnp.stack([r, prefix_len[0], u, v, c]).astype(jnp.int32)
        rows = w_rows // q_rows
        a_rows = N // C * rows
        piece = (3 * ff_slice + 127) // 128 * 128

        gain1 = norm1_gain.astype(f32)
        gain2 = norm2_gain.astype(f32)
        inputs = tokens[0].astype(f32)
        first, first_std, first_inv = layer_norm_forward(inputs, gain1, norm1_bias.astype(f32))
        seq_in = jnp.concatenate(gather_rel(first.astype(bf16)), axis=0)

        (attn_shard,) = whole_call(
            prepare_kernel,
            info,
            [query_key_value_weight.transpose(1, 0, 2), attention_output_weight],
            [jax.ShapeDtypeStruct((attention_output_weight.shape[0], 4 * head_cols), bf16)],
        )
        w_attn = lax.all_gather(attn_shard, ("dp", "col"), axis=0, tiled=True)
        (packed,) = whole_call(
            functools.partial(pack_kernel, R, q_rows),
            info,
            [gate_up_projection_weight.transpose(1, 0, 2), down_projection_weight],
            [jax.ShapeDtypeStruct((N, rows, piece), bf16)],
        )
        packed, seq_in = lax.optimization_barrier((packed, seq_in))
        held = pltpu.VMEM((N, rows, piece), bf16)
        gu_shard, down_shard = whole_call(
            functools.partial(unpack_kernel, C),
            info,
            spread(packed),
            [
                jax.ShapeDtypeStruct((a_rows, 2 * ff), bf16),
                jax.ShapeDtypeStruct((a_rows, ff), bf16),
            ],
            [held],
        )
        w_gu = lax.all_gather(gu_shard, ("dp", "col"), axis=0, tiled=True)
        w_down = lax.all_gather(down_shard, ("dp", "col"), axis=0, tiled=True)

        w_attn, _ = lax.optimization_barrier((w_attn, gu_shard))
        w_qkv = w_attn[:, : 3 * head_cols]
        w_out = w_attn[:, 3 * head_cols :]
        dy_rel = jnp.concatenate(gather_rel(grad_out[0], gu_shard), axis=0)
        dy = grad_out[0]
        bias = query_key_value_bias.astype(f32).reshape(3, pairs, 2 * HD).transpose(1, 0, 2)
        projected = nn(seq_in, w_qkv)
        projected = projected + bias.reshape(-1)

        qkv, attended, log_sums = attend_forward(info, projected, table, R)
        own = nt(attended[:block], w_out)
        others = nt(attended[block:], w_out).astype(bf16)
        residual = scatter_rel([own] + [others[k * block : (k + 1) * block] for k in range(R - 1)])
        middle = inputs + residual

        second, second_std, second_inv = layer_norm_forward(
            middle, gain2, norm2_bias.astype(f32)
        )
        second_in = jnp.concatenate(gather_rel(second.astype(bf16)), axis=0)
        gate_up = nn(second_in, w_gu)
        gate_vals = gate_up[:, :ff]
        up_vals = gate_up[:, ff:]
        sig = jax.nn.sigmoid(gate_vals)
        swish = gate_vals * sig
        hidden = (swish * up_vals).astype(bf16)
        if C == 2:
            seq_halves = split_columns(info, seq_in, mesh.shape["dp"])
            halves = split_columns(info, dy_rel, mesh.shape["dp"])
            grad_down = pair_sum(*halves, hidden)
            _, w_down = lax.optimization_barrier((grad_down, w_down))
            grad_down = lax.psum_scatter(grad_down, "dp", scatter_dimension=0, tiled=True)
        else:
            grad_down = tn(dy_rel, hidden).astype(bf16)
            _, w_down = lax.optimization_barrier((grad_down, w_down))
            grad_down = lax.psum_scatter(grad_down, ("dp", "col"), scatter_dimension=0, tiled=True)
        grad_hidden = nn(dy_rel, w_down)
        grad_gate = grad_hidden * up_vals * sig * (1.0 + gate_vals * (1.0 - sig))
        grad_up = grad_hidden * swish
        grad_gu_vals = jnp.concatenate([grad_gate.astype(bf16), grad_up.astype(bf16)], axis=1)
        own = nt(grad_gu_vals[:block], w_gu)
        others = nt(grad_gu_vals[block:], w_gu).astype(bf16)
        others, second_in = lax.optimization_barrier((others, second_in))
        grad_second = scatter_rel(
            [own] + [others[k * block : (k + 1) * block] for k in range(R - 1)]
        )
        grad_gu = tn(second_in, grad_gu_vals).astype(bf16)
        grad_gu = lax.psum_scatter(grad_gu, ("dp", "col"), scatter_dimension=0, tiled=True)

        grad_middle = dy.astype(f32) + layer_norm_backward(
            grad_second, second_std, second_inv, gain2
        )
        gain2_grad = jnp.sum(grad_second * second_std, axis=0)
        bias2_grad = jnp.sum(grad_second, axis=0)

        branch = jnp.concatenate(gather_rel(grad_middle.astype(bf16)), axis=0)
        own = nt(hidden[:block], w_down)
        others = nt(hidden[block:], w_down).astype(bf16)
        others, _ = lax.optimization_barrier((others, branch))
        mixed = scatter_rel(
            [own] + [others[k * block : (k + 1) * block] for k in range(R - 1)]
        )
        layer_out = (middle + mixed).astype(bf16)
        grad_heads = nn(branch, w_out).astype(bf16)
        grad_proj, bias_local = attend_backward(info, qkv, table, log_sums, grad_heads, R)
        bias_local = bias_local[:, 0].reshape(pairs, 3, 2 * HD)
        bias_local = bias_local.transpose(1, 0, 2).reshape(3, head_cols)
        if C == 2:
            halves = split_columns(info, branch, mesh.shape["dp"])
            grad_attn = jnp.concatenate(
                [pair_sum(*seq_halves, grad_proj), pair_sum(*halves, attended)],
                axis=1,
            )
            grad_attn = lax.psum_scatter(grad_attn, "dp", scatter_dimension=0, tiled=True)
        else:
            grad_attn = jnp.concatenate(
                [tn(seq_in, grad_proj).astype(bf16), tn(branch, attended).astype(bf16)], axis=1
            )
            grad_attn = lax.psum_scatter(grad_attn, ("dp", "col"), scatter_dimension=0, tiled=True)
        own = nt(grad_proj[:block], w_qkv)
        others = nt(grad_proj[block:], w_qkv).astype(bf16)
        grad_first = scatter_rel(
            [own] + [others[k * block : (k + 1) * block] for k in range(R - 1)]
        )
        input_grad = grad_middle + layer_norm_backward(grad_first, first_std, first_inv, gain1)
        gain1_grad = jnp.sum(grad_first * first_std, axis=0)
        bias1_grad = jnp.sum(grad_first, axis=0)

        col_offset = r * head_cols
        bias_full = lax.dynamic_update_slice(
            jnp.zeros((3, width), f32), bias_local, (jnp.int32(0), col_offset)
        )
        sums = jnp.stack([gain1_grad, bias1_grad, gain2_grad, bias2_grad])
        sums = sum_everywhere(jnp.concatenate([sums, bias_full], axis=0))
        grad_bias = lax.dynamic_slice_in_dim(sums[4:], col_offset, head_cols, 1)

        (packed,) = whole_call(
            functools.partial(pack_back_kernel, C),
            info,
            [grad_gu, grad_down],
            [jax.ShapeDtypeStruct((N, rows, piece), bf16)],
        )
        home_gu, home_down = whole_call(
            functools.partial(unpack_back_kernel, R, q_rows),
            info,
            bring_back(packed),
            [
                jax.ShapeDtypeStruct((2, w_rows, ff_local), f32),
                jax.ShapeDtypeStruct((w_rows, ff_local), f32),
            ],
            [held],
        )
        home_qkv, home_out = whole_call(
            finish_kernel,
            info,
            [grad_attn],
            [
                jax.ShapeDtypeStruct((3, grad_attn.shape[0], head_cols), f32),
                jax.ShapeDtypeStruct((grad_attn.shape[0], head_cols), f32),
            ],
        )
        return (
            layer_out[None],
            input_grad[None],
            sums[0],
            sums[1],
            home_qkv.transpose(1, 0, 2),
            grad_bias,
            home_out,
            sums[2],
            sums[3],
            home_gu.transpose(1, 0, 2),
            home_down,
        )

    return body


def solution(mesh):
    in_specs = (
        P(("dp", "col"), "row", None),
        P(("dp", "col")),
        P(),
        P(),
        P(("dp", "col"), None, "row"),
        P(None, "row"),
        P(("dp", "col"), "row"),
        P(),
        P(),
        P(("dp", "row"), None, "col"),
        P(("dp", "row"), "col"),
        P(("dp", "col"), "row", None),
    )
    out_specs = (
        P(("dp", "col"), "row", None),
        P(("dp", "col"), "row", None),
        P(),
        P(),
        P(("dp", "col"), None, "row"),
        P(None, "row"),
        P(("dp", "col"), "row"),
        P(),
        P(),
        P(("dp", "row"), None, "col"),
        P(("dp", "row"), "col"),
    )
    body = make_body(mesh)

    return jax.shard_map(body, mesh=mesh, in_specs=in_specs, out_specs=out_specs, check_vma=False)
```

```python
import functools
import math

import jax
import jax.numpy as jnp
from jax import lax
from jax.experimental import pallas as pl
from jax.experimental.pallas import tpu as pltpu
from jax.sharding import PartitionSpec as P


HD = 64
ROT = 16

norm_eps = 1e-05
rope_base = 10000.0
masked_fill = -1e30

DP, ROW, COL = "dp", "row", "col"

bf16 = jnp.bfloat16
f32 = jnp.float32


def layer_norm_forward(values, norm_gain, norm_shift):
    centre = jnp.mean(values, axis=-1, keepdims=True)
    centred = values - centre
    variance = jnp.mean(centred * centred, axis=-1, keepdims=True)
    inverse = lax.rsqrt(variance + norm_eps)
    normed = centred * inverse
    return (normed * norm_gain + norm_shift, normed, inverse)


def layer_norm_backward(incoming, normed, inverse, norm_gain):
    scaled = incoming * norm_gain
    inner = jnp.mean(scaled, axis=-1, keepdims=True)
    along = jnp.mean(scaled * normed, axis=-1, keepdims=True)
    return inverse * (scaled - inner - normed * along)


def rotary_tables(places):
    half_rot = ROT // 2
    column = jnp.arange(2 * HD) % HD
    freqs = rope_base ** (-(column % half_rot).astype(f32) * 2.0 / ROT)
    angles = places.astype(f32)[:, None] * freqs[None, :]
    sines = jnp.sin(angles)
    cosine = jnp.where(column < ROT, jnp.cos(angles), 1.0)
    left = jnp.where((column >= half_rot) & (column < ROT), sines, 0.0)
    right = jnp.where(column < half_rot, -sines, 0.0)
    return jnp.stack([cosine, left, right])


def dot(left, right, dims):
    return lax.dot_general(left, right, (dims, ((), ())), preferred_element_type=f32)


def nn(left, right):
    return dot(left, right, ((1,), (0,)))


def nt(left, right):
    return dot(left, right, ((1,), (1,)))


def tn(left, right):
    return dot(left, right, ((0,), (0,)))


def key_blocks(jq, blocks):
    return max(jq + 1, blocks // 2)


def block_mask(qpos, kpos, jq, jk, blocks, prefix):
    if jk < jq:
        return None
    causal = kpos <= qpos
    if jk >= blocks // 2:
        return causal
    early = kpos < prefix
    return (causal | early) if jk == jq else early


def head_lane(head):
    lane = lax.broadcasted_iota(jnp.int32, (1, 2 * HD), 1)
    return (lane < HD) if head == 0 else (lane >= HD)


def forward_kernel(blocks, size, info, proj, table, qkv, out, sums):
    w = 2 * HD
    scale = 1.0 / math.sqrt(HD)
    r, prefix = info[0], info[1]
    for j in range(blocks):
        rows = pl.ds(j * size, size)
        cosine, left, right = table[0, rows], table[1, rows], table[2, rows]
        for part in range(2):
            x = proj[rows, part * w : (part + 1) * w]
            x = x * cosine + pltpu.roll(x, 8, 1) * left + pltpu.roll(x, w - 8, 1) * right
            qkv[rows, part * w : (part + 1) * w] = x.astype(bf16)
        qkv[rows, 2 * w : 3 * w] = proj[rows, 2 * w : 3 * w].astype(bf16)
    places = [pl.ds(pl.multiple_of((j ^ r) * size, size), size) for j in range(blocks)]
    for jq in range(blocks):
        count = key_blocks(jq, blocks)
        q = qkv[places[jq], 0:w].astype(f32) * scale
        qpos = jq * size + lax.broadcasted_iota(jnp.int32, (size, size), 0)
        results = []
        tops = []
        for head in range(2):
            qh = jnp.where(head_lane(head), q, 0.0).astype(bf16)
            scores = []
            for jk in range(count):
                s = nt(qh, qkv[places[jk], w : 2 * w])
                kpos = jk * size + lax.broadcasted_iota(jnp.int32, (size, size), 1)
                mask = block_mask(qpos, kpos, jq, jk, blocks, prefix)
                scores.append(s if mask is None else jnp.where(mask, s, masked_fill))
            top = jnp.max(scores[0], axis=1, keepdims=True)
            for s in scores[1:]:
                top = jnp.maximum(top, jnp.max(s, axis=1, keepdims=True))
            total = 0.0
            result = 0.0
            for jk in range(count):
                e = jnp.exp(scores[jk] - top)
                total = total + jnp.sum(e, axis=1, keepdims=True)
                result = result + nn(e.astype(bf16), qkv[places[jk], 2 * w : 3 * w])
            results.append(result / total)
            tops.append(top + jnp.log(total))
        out[places[jq], :] = jnp.where(head_lane(0), results[0], results[1]).astype(bf16)
        both = jnp.where(head_lane(0), tops[0], tops[1])
        flipped = both.T
        sums[0, jq, 0:8, :] = flipped[0:8]
        sums[0, jq, 8:16, :] = flipped[HD : HD + 8]


def backward_kernel(blocks, size, info, qkv, table, sums, grads, out, bias, qm, km, gm, acc):
    w = 2 * HD
    scale = 1.0 / math.sqrt(HD)
    r, prefix = info[0], info[1]
    for head in range(2):
        lanes = head_lane(head)
        for j in range(blocks):
            rows = pl.ds(j * size, size)
            q = qkv[rows, 0:w].astype(f32) * scale
            k = qkv[rows, w : 2 * w].astype(f32) * scale
            qm[head, rows] = jnp.where(lanes, q, 0.0).astype(bf16)
            km[head, rows] = jnp.where(lanes, k, 0.0).astype(bf16)
            gm[head, rows] = jnp.where(lanes, grads[rows, :].astype(f32), 0.0).astype(bf16)
    acc[...] = jnp.zeros_like(acc)
    places = [pl.ds(pl.multiple_of((j ^ r) * size, size), size) for j in range(blocks)]
    for jq in range(blocks):
        count = key_blocks(jq, blocks)
        rq = places[jq]
        qpos = jq * size + lax.broadcasted_iota(jnp.int32, (size, size), 1)
        grad_q = 0.0
        for head in range(2):
            top = sums[0, jq, 8 * head : 8 * head + 1, :]
            probs = []
            products = []
            inner = 0.0
            for jk in range(count):
                s = nt(qkv[places[jk], w : 2 * w], qm[head, rq])
                p = jnp.exp(s - top)
                kpos = jk * size + lax.broadcasted_iota(jnp.int32, (size, size), 0)
                mask = block_mask(qpos, kpos, jq, jk, blocks, prefix)
                if mask is not None:
                    p = jnp.where(mask, p, 0.0)
                t = p * nt(qkv[places[jk], 2 * w : 3 * w], gm[head, rq])
                inner = inner + jnp.sum(t, axis=0, keepdims=True)
                probs.append(p)
                products.append(t)
            for jk in range(count):
                rk = places[jk]
                d = (products[jk] - probs[jk] * inner).astype(bf16)
                acc[1, rk] += nn(probs[jk].astype(bf16), gm[head, rq])
                acc[0, rk] += nn(d, qm[head, rq])
                grad_q = grad_q + tn(d, km[head, rk])
        cosine, left, right = table[0, rq], table[1, rq], table[2, rq]
        x = grad_q
        x = x * cosine - pltpu.roll(x, 8, 1) * left - pltpu.roll(x, w - 8, 1) * right
        out[rq, 0:w] = x.astype(bf16)
    bias_q = 0.0
    bias_k = 0.0
    bias_v = 0.0
    for j in range(blocks):
        rows = pl.ds(j * size, size)
        x = acc[0, rows]
        x = x * table[0, rows]
        x = x - pltpu.roll(acc[0, rows], 8, 1) * table[1, rows]
        x = x - pltpu.roll(acc[0, rows], w - 8, 1) * table[2, rows]
        x = x.astype(bf16)
        y = acc[1, rows].astype(bf16)
        out[rows, w : 2 * w] = x
        out[rows, 2 * w : 3 * w] = y
        bias_q = bias_q + jnp.sum(out[rows, 0:w].astype(f32), axis=0, keepdims=True)
        bias_k = bias_k + jnp.sum(x.astype(f32), axis=0, keepdims=True)
        bias_v = bias_v + jnp.sum(y.astype(f32), axis=0, keepdims=True)
    row = jnp.concatenate([bias_q, bias_k, bias_v], axis=1)
    bias[0] = jnp.broadcast_to(row, (8, 3 * w))


def attend_forward(info, projected, table, blocks):
    length = projected.shape[0]
    w = 2 * HD
    pairs = projected.shape[1] // (3 * w)
    size = length // blocks
    spec = pltpu.PrefetchScalarGridSpec(
        num_scalar_prefetch=1,
        grid=(pairs,),
        in_specs=[
            pl.BlockSpec((length, 3 * w), lambda p, i: (0, p)),
            pl.BlockSpec((3, length, w), lambda p, i: (0, 0, 0)),
        ],
        out_specs=[
            pl.BlockSpec((length, 3 * w), lambda p, i: (0, p)),
            pl.BlockSpec((length, w), lambda p, i: (0, p)),
            pl.BlockSpec((1, blocks, 16, size), lambda p, i: (p, 0, 0, 0)),
        ],
    )
    return pl.pallas_call(
        lambda *refs: forward_kernel(blocks, size, *refs),
        grid_spec=spec,
        out_shape=[
            jax.ShapeDtypeStruct((length, 3 * w * pairs), bf16),
            jax.ShapeDtypeStruct((length, w * pairs), bf16),
            jax.ShapeDtypeStruct((pairs, blocks, 16, size), f32),
        ],
        name="attn_f",
        compiler_params=pltpu.CompilerParams(vmem_limit_bytes=48 << 20),
    )(info, projected, table)


def attend_backward(info, qkv, table, sums, grads, blocks):
    length = qkv.shape[0]
    w = 2 * HD
    pairs = qkv.shape[1] // (3 * w)
    size = length // blocks
    spec = pltpu.PrefetchScalarGridSpec(
        num_scalar_prefetch=1,
        grid=(pairs,),
        in_specs=[
            pl.BlockSpec((length, 3 * w), lambda p, i: (0, p)),
            pl.BlockSpec((3, length, w), lambda p, i: (0, 0, 0)),
            pl.BlockSpec((1, blocks, 16, size), lambda p, i: (p, 0, 0, 0)),
            pl.BlockSpec((length, w), lambda p, i: (0, p)),
        ],
        out_specs=[
            pl.BlockSpec((length, 3 * w), lambda p, i: (0, p)),
            pl.BlockSpec((1, 8, 3 * w), lambda p, i: (p, 0, 0)),
        ],
        scratch_shapes=[
            pltpu.VMEM((2, length, w), bf16),
            pltpu.VMEM((2, length, w), bf16),
            pltpu.VMEM((2, length, w), bf16),
            pltpu.VMEM((2, length, w), f32),
        ],
    )
    return pl.pallas_call(
        lambda *refs: backward_kernel(blocks, size, *refs),
        grid_spec=spec,
        out_shape=[
            jax.ShapeDtypeStruct((length, 3 * w * pairs), bf16),
            jax.ShapeDtypeStruct((pairs, 8, 3 * w), f32),
        ],
        name="attn_b",
        compiler_params=pltpu.CompilerParams(vmem_limit_bytes=48 << 20),
    )(info, qkv, table, sums, grads)


def pack_kernel(R, q, info, gate_up, down, out):
    fs = down.shape[1] // R
    rows = down.shape[0] // q
    for slot in range(R * q):
        span = pl.ds((slot % q) * rows, rows)
        lo = (slot // q) * fs
        k = slot ^ info[2]
        out[k, :, 0:fs] = gate_up[0, span, lo : lo + fs]
        out[k, :, fs : 2 * fs] = gate_up[1, span, lo : lo + fs]
        out[k, :, 2 * fs : 3 * fs] = down[span, lo : lo + fs]


def unpack_kernel(C, info, *refs):
    pieces, (gate_up, down, held) = refs[:-3], refs[-3:]
    rows = held.shape[1]
    ff = down.shape[1]
    fs = ff // C
    for k, piece in enumerate(pieces):
        held[k ^ info[3]] = piece[...]
    for place in range(len(pieces)):
        span = pl.ds((place // C) * rows, rows)
        lo = (place % C) * fs
        gate_up[span, lo : lo + fs] = held[place, :, 0:fs]
        gate_up[span, ff + lo : ff + lo + fs] = held[place, :, fs : 2 * fs]
        down[span, lo : lo + fs] = held[place, :, 2 * fs : 3 * fs]


def pack_back_kernel(C, info, gate_up, down, out):
    rows = out.shape[1]
    ff = down.shape[1]
    fs = ff // C
    for place in range(out.shape[0]):
        span = pl.ds((place // C) * rows, rows)
        lo = (place % C) * fs
        k = place ^ info[3]
        out[k, :, 0:fs] = gate_up[span, lo : lo + fs]
        out[k, :, fs : 2 * fs] = gate_up[span, ff + lo : ff + lo + fs]
        out[k, :, 2 * fs : 3 * fs] = down[span, lo : lo + fs]


def unpack_back_kernel(R, q, info, *refs):
    pieces, (gate_up, down, held) = refs[:-3], refs[-3:]
    rows = held.shape[1]
    fs = down.shape[1] // R
    for k, piece in enumerate(pieces):
        held[k ^ info[2]] = piece[...]
    for slot in range(len(pieces)):
        span = pl.ds((slot % q) * rows, rows)
        lo = (slot // q) * fs
        gate_up[0, span, lo : lo + fs] = held[slot, :, 0:fs].astype(f32)
        gate_up[1, span, lo : lo + fs] = held[slot, :, fs : 2 * fs].astype(f32)
        down[span, lo : lo + fs] = held[slot, :, 2 * fs : 3 * fs].astype(f32)


def prepare_kernel(info, qkv, outer, out):
    w = 2 * HD
    cols = outer.shape[1]
    for pair in range(cols // w):
        for part in range(3):
            lo = (3 * pair + part) * w
            out[:, lo : lo + w] = qkv[part, :, pair * w : (pair + 1) * w]
    out[:, 3 * cols :] = outer[...]


def finish_kernel(info, grads, qkv, outer):
    w = 2 * HD
    cols = outer.shape[1]
    for pair in range(cols // w):
        for part in range(3):
            lo = (3 * pair + part) * w
            qkv[part, :, pair * w : (pair + 1) * w] = grads[:, lo : lo + w].astype(f32)
    outer[...] = grads[:, 3 * cols :].astype(f32)


def whole_call(kernel, info, arrays, shapes, scratch=()):
    def spec(shape):
        return pl.BlockSpec(shape, lambda i, s: (0,) * len(shape))

    return pl.pallas_call(
        kernel,
        grid_spec=pltpu.PrefetchScalarGridSpec(
            num_scalar_prefetch=1,
            grid=(1,),
            in_specs=[spec(a.shape) for a in arrays],
            out_specs=[spec(a.shape) for a in shapes],
            scratch_shapes=list(scratch),
        ),
        out_shape=shapes,
        compiler_params=pltpu.CompilerParams(vmem_limit_bytes=48 << 20),
    )(info, *arrays)


def split_kernel(info, mine, other, mine_out, other_out):
    mine_out[...] = mine[...]
    other_out[...] = other[...]


def split_columns(info, array, parts):
    length, width = array.shape
    block = width // (2 * parts)
    shape = jax.ShapeDtypeStruct((length, width // 2), array.dtype)
    return pl.pallas_call(
        split_kernel,
        grid_spec=pltpu.PrefetchScalarGridSpec(
            num_scalar_prefetch=1,
            grid=(parts,),
            in_specs=[
                pl.BlockSpec((length, block), lambda j, s: (0, 2 * j + s[4])),
                pl.BlockSpec((length, block), lambda j, s: (0, 2 * j + 1 - s[4])),
            ],
            out_specs=[pl.BlockSpec((length, block), lambda j, s: (0, j))] * 2,
        ),
        out_shape=[shape, shape],
    )(info, array, array)


def make_body(mesh):
    R = mesh.shape[ROW]
    C = mesh.shape[COL]
    N = max(R, C)

    def row_permute(block, k):
        return lax.ppermute(block, ROW, [(i, i ^ k) for i in range(R)])

    def gather_rel(block, after=None):
        if R != 4:
            return [block] + [row_permute(block, k) for k in range(1, R)]
        half = block.shape[0] // 2
        if after is not None:
            block, _ = lax.optimization_barrier((block, after))
        one = row_permute(block, 1)
        two = row_permute(block, 2)
        top = row_permute(one[:half], 2)
        low = row_permute(two[half:], 1)
        return [block, one, two, jnp.concatenate([top, low], axis=0)]

    def scatter_rel(blocks):
        if R != 4:
            total = blocks[0]
            for k in range(1, R):
                total = total + row_permute(blocks[k].astype(bf16), k).astype(f32)
            return total
        half = blocks[0].shape[0] // 2
        b = [(x[:half], x[half:]) for x in blocks]
        top2 = row_permute(b[3][0].astype(bf16), 1)
        low1 = row_permute(b[3][1].astype(bf16), 2)
        top0 = row_permute(b[1][0].astype(bf16), 1)
        low0 = row_permute(b[2][1].astype(bf16), 2)
        top2 = row_permute((b[2][0].astype(f32) + top2.astype(f32)).astype(bf16), 2)
        low1 = row_permute((b[1][1].astype(f32) + low1.astype(f32)).astype(bf16), 1)
        top = b[0][0].astype(f32) + top0.astype(f32) + top2.astype(f32)
        low = b[0][1].astype(f32) + low0.astype(f32) + low1.astype(f32)
        return jnp.concatenate([top, low], axis=0)

    def source_place(s, c):
        return (s % (R // C)) * C + c if C <= R else c

    def source_dest(s, c, k):
        slot = source_place(s, c) ^ k
        if C <= R:
            return slot, s // (R // C)
        q = C // R
        return slot // q, s * q + slot % q

    def exchange_pairs(k):
        pairs = []
        for s in range(R):
            for c in range(C):
                dr, dc = source_dest(s, c, k)
                pairs.append((s * C + c, dr * C + dc))
        return pairs

    def spread(packed):
        return [lax.ppermute(packed[k], (ROW, COL), exchange_pairs(k)) for k in range(N)]

    def bring_back(packed):
        return [
            lax.ppermute(packed[k], (ROW, COL), [(b, a) for a, b in exchange_pairs(k)])
            for k in range(N)
        ]

    def sum_everywhere(array):
        for name in (COL, DP, ROW):
            size = mesh.shape[name]
            step = 1
            while step < size:
                other = lax.ppermute(array, name, [(i, i ^ step) for i in range(size)])
                step *= 2
                array = array + other
        return array

    def pair_sum(mine, other, right):
        away = tn(other, right).astype(bf16)
        got = lax.ppermute(away, COL, [(0, 1), (1, 0)])
        return (tn(mine, right) + got.astype(f32)).astype(bf16)

    def body(
        tokens,
        prefix_len,
        norm1_gain,
        norm1_bias,
        query_key_value_weight,
        query_key_value_bias,
        attention_output_weight,
        norm2_gain,
        norm2_bias,
        gate_up_projection_weight,
        down_projection_weight,
        grad_out,
    ):
        r = lax.axis_index(ROW)
        c = lax.axis_index(COL)
        block = tokens.shape[1]
        width = tokens.shape[2]
        head_cols = query_key_value_weight.shape[2]
        pairs = head_cols // (2 * HD)
        places = (jnp.arange(R)[:, None] ^ r) * block + jnp.arange(block)[None, :]
        table = rotary_tables(places.reshape(-1))
        w_rows, _, ff_local = gate_up_projection_weight.shape
        ff_slice = ff_local // R
        ff = ff_slice * C
        q_rows = max(1, C // R)
        u = source_place(r, c)
        v = r if C <= R else r * q_rows + c % q_rows
        info = jnp.stack([r, prefix_len[0], u, v, c]).astype(jnp.int32)
        rows = w_rows // q_rows
        a_rows = N // C * rows
        piece = (3 * ff_slice + 127) // 128 * 128

        gain1 = norm1_gain.astype(f32)
        gain2 = norm2_gain.astype(f32)
        inputs = tokens[0].astype(f32)
        first, first_std, first_inv = layer_norm_forward(inputs, gain1, norm1_bias.astype(f32))
        seq_in = jnp.concatenate(gather_rel(first.astype(bf16)), axis=0)

        (attn_shard,) = whole_call(
            prepare_kernel,
            info,
            [query_key_value_weight.transpose(1, 0, 2), attention_output_weight],
            [jax.ShapeDtypeStruct((attention_output_weight.shape[0], 4 * head_cols), bf16)],
        )
        w_attn = lax.all_gather(attn_shard, (DP, COL), axis=0, tiled=True)
        (packed,) = whole_call(
            functools.partial(pack_kernel, R, q_rows),
            info,
            [gate_up_projection_weight.transpose(1, 0, 2), down_projection_weight],
            [jax.ShapeDtypeStruct((N, rows, piece), bf16)],
        )
        packed, seq_in = lax.optimization_barrier((packed, seq_in))
        held = pltpu.VMEM((N, rows, piece), bf16)
        gu_shard, down_shard = whole_call(
            functools.partial(unpack_kernel, C),
            info,
            spread(packed),
            [
                jax.ShapeDtypeStruct((a_rows, 2 * ff), bf16),
                jax.ShapeDtypeStruct((a_rows, ff), bf16),
            ],
            [held],
        )
        w_gu = lax.all_gather(gu_shard, (DP, COL), axis=0, tiled=True)
        w_down = lax.all_gather(down_shard, (DP, COL), axis=0, tiled=True)

        w_attn, _ = lax.optimization_barrier((w_attn, gu_shard))
        w_qkv = w_attn[:, : 3 * head_cols]
        w_out = w_attn[:, 3 * head_cols :]
        dy_rel = jnp.concatenate(gather_rel(grad_out[0], gu_shard), axis=0)
        dy = grad_out[0]
        bias = query_key_value_bias.astype(f32).reshape(3, pairs, 2 * HD).transpose(1, 0, 2)
        projected = nn(seq_in, w_qkv)
        projected = projected + bias.reshape(-1)

        qkv, attended, log_sums = attend_forward(info, projected, table, R)
        own = nt(attended[:block], w_out)
        others = nt(attended[block:], w_out).astype(bf16)
        residual = scatter_rel([own] + [others[k * block : (k + 1) * block] for k in range(R - 1)])
        middle = inputs + residual

        second, second_std, second_inv = layer_norm_forward(
            middle, gain2, norm2_bias.astype(f32)
        )
        second_in = jnp.concatenate(gather_rel(second.astype(bf16)), axis=0)
        gate_up = nn(second_in, w_gu)
        gate_vals = gate_up[:, :ff]
        up_vals = gate_up[:, ff:]
        sig = jax.nn.sigmoid(gate_vals)
        swish = gate_vals * sig
        hidden = (swish * up_vals).astype(bf16)
        if C == 2:
            seq_halves = split_columns(info, seq_in, mesh.shape[DP])
            halves = split_columns(info, dy_rel, mesh.shape[DP])
            grad_down = pair_sum(*halves, hidden)
            _, w_down = lax.optimization_barrier((grad_down, w_down))
            grad_down = lax.psum_scatter(grad_down, DP, scatter_dimension=0, tiled=True)
        else:
            grad_down = tn(dy_rel, hidden).astype(bf16)
            _, w_down = lax.optimization_barrier((grad_down, w_down))
            grad_down = lax.psum_scatter(
                grad_down, (DP, COL), scatter_dimension=0, tiled=True
            )
        grad_hidden = nn(dy_rel, w_down)
        grad_gate = grad_hidden * up_vals * sig * (1.0 + gate_vals * (1.0 - sig))
        grad_up = grad_hidden * swish
        grad_gu_vals = jnp.concatenate([grad_gate.astype(bf16), grad_up.astype(bf16)], axis=1)
        own = nt(grad_gu_vals[:block], w_gu)
        others = nt(grad_gu_vals[block:], w_gu).astype(bf16)
        others, second_in = lax.optimization_barrier((others, second_in))
        grad_second = scatter_rel(
            [own] + [others[k * block : (k + 1) * block] for k in range(R - 1)]
        )
        grad_gu = tn(second_in, grad_gu_vals).astype(bf16)
        grad_gu = lax.psum_scatter(grad_gu, (DP, COL), scatter_dimension=0, tiled=True)

        grad_middle = dy.astype(f32) + layer_norm_backward(
            grad_second, second_std, second_inv, gain2
        )
        gain2_grad = jnp.sum(grad_second * second_std, axis=0)
        bias2_grad = jnp.sum(grad_second, axis=0)

        branch = jnp.concatenate(gather_rel(grad_middle.astype(bf16)), axis=0)
        own = nt(hidden[:block], w_down)
        others = nt(hidden[block:], w_down).astype(bf16)
        others, _ = lax.optimization_barrier((others, branch))
        mixed = scatter_rel(
            [own] + [others[k * block : (k + 1) * block] for k in range(R - 1)]
        )
        layer_out = (middle + mixed).astype(bf16)
        grad_heads = nn(branch, w_out).astype(bf16)
        grad_proj, bias_local = attend_backward(info, qkv, table, log_sums, grad_heads, R)
        bias_local = bias_local[:, 0].reshape(pairs, 3, 2 * HD)
        bias_local = bias_local.transpose(1, 0, 2).reshape(3, head_cols)
        if C == 2:
            outer = tn(branch, attended).astype(bf16).reshape(mesh.shape[DP], C, -1, head_cols)
            away = lax.dynamic_index_in_dim(outer, 1 - c, 1, keepdims=False)
            mine = lax.dynamic_index_in_dim(outer, c, 1, keepdims=False)
            got = lax.ppermute(away.reshape(-1, head_cols), COL, [(0, 1), (1, 0)])
            outer = mine.reshape(-1, head_cols).astype(f32) + got.astype(f32)
            grad_attn = jnp.concatenate(
                [pair_sum(*seq_halves, grad_proj), outer.astype(bf16)], axis=1
            )
            grad_proj, _ = lax.optimization_barrier((grad_proj, grad_attn))
            grad_attn = lax.psum_scatter(grad_attn, DP, scatter_dimension=0, tiled=True)
        else:
            grad_attn = jnp.concatenate(
                [tn(seq_in, grad_proj).astype(bf16), tn(branch, attended).astype(bf16)], axis=1
            )
            grad_attn = lax.psum_scatter(
                grad_attn, (DP, COL), scatter_dimension=0, tiled=True
            )
        own = nt(grad_proj[:block], w_qkv)
        others = nt(grad_proj[block:], w_qkv).astype(bf16)
        grad_first = scatter_rel(
            [own] + [others[k * block : (k + 1) * block] for k in range(R - 1)]
        )
        input_grad = grad_middle + layer_norm_backward(grad_first, first_std, first_inv, gain1)
        gain1_grad = jnp.sum(grad_first * first_std, axis=0)
        bias1_grad = jnp.sum(grad_first, axis=0)

        col_offset = r * head_cols
        bias_full = lax.dynamic_update_slice(
            jnp.zeros((3, width), f32), bias_local, (jnp.int32(0), col_offset)
        )
        sums = jnp.stack([gain1_grad, bias1_grad, gain2_grad, bias2_grad])
        sums = sum_everywhere(jnp.concatenate([sums, bias_full], axis=0))
        grad_bias = lax.dynamic_slice_in_dim(sums[4:], col_offset, head_cols, 1)

        (packed,) = whole_call(
            functools.partial(pack_back_kernel, C),
            info,
            [grad_gu, grad_down],
            [jax.ShapeDtypeStruct((N, rows, piece), bf16)],
        )
        home_gu, home_down = whole_call(
            functools.partial(unpack_back_kernel, R, q_rows),
            info,
            bring_back(packed),
            [
                jax.ShapeDtypeStruct((2, w_rows, ff_local), f32),
                jax.ShapeDtypeStruct((w_rows, ff_local), f32),
            ],
            [held],
        )
        home_qkv, home_out = whole_call(
            finish_kernel,
            info,
            [grad_attn],
            [
                jax.ShapeDtypeStruct((3, grad_attn.shape[0], head_cols), f32),
                jax.ShapeDtypeStruct((grad_attn.shape[0], head_cols), f32),
            ],
        )
        return (
            layer_out[None],
            input_grad[None],
            sums[0],
            sums[1],
            home_qkv.transpose(1, 0, 2),
            grad_bias,
            home_out,
            sums[2],
            sums[3],
            home_gu.transpose(1, 0, 2),
            home_down,
        )

    return body


def solution(mesh):
    in_specs = (
        P((DP, COL), ROW, None),
        P((DP, COL)),
        P(),
        P(),
        P((DP, COL), None, ROW),
        P(None, ROW),
        P((DP, COL), ROW),
        P(),
        P(),
        P((DP, ROW), None, COL),
        P((DP, ROW), COL),
        P((DP, COL), ROW, None),
    )
    out_specs = (
        P((DP, COL), ROW, None),
        P((DP, COL), ROW, None),
        P(),
        P(),
        P((DP, COL), None, ROW),
        P(None, ROW),
        P((DP, COL), ROW),
        P(),
        P(),
        P((DP, ROW), None, COL),
        P((DP, ROW), COL),
    )
    body = make_body(mesh)

    return jax.shard_map(body, mesh=mesh, in_specs=in_specs, out_specs=out_specs, check_vma=False)
```

```python
import functools
import math

import jax
import jax.numpy as jnp
from jax import lax
from jax.experimental import pallas as pl
from jax.experimental.pallas import tpu as pltpu
from jax.sharding import PartitionSpec as P


HD = 64
ROT = 16

norm_eps = 1e-05
rope_base = 10000.0
masked_fill = -1e30

DP, ROW, COL = "dp", "row", "col"

bf16 = jnp.bfloat16
f32 = jnp.float32


def layer_norm_forward(values, norm_gain, norm_shift):
    centre = jnp.mean(values, axis=-1, keepdims=True)
    centred = values - centre
    variance = jnp.mean(centred * centred, axis=-1, keepdims=True)
    inverse = lax.rsqrt(variance + norm_eps)
    normed = centred * inverse
    return (normed * norm_gain + norm_shift, normed, inverse)


def layer_norm_backward(incoming, normed, inverse, norm_gain):
    scaled = incoming * norm_gain
    inner = jnp.mean(scaled, axis=-1, keepdims=True)
    along = jnp.mean(scaled * normed, axis=-1, keepdims=True)
    return inverse * (scaled - inner - normed * along)


def rotary_tables(places):
    half_rot = ROT // 2
    column = jnp.arange(2 * HD) % HD
    freqs = rope_base ** (-(column % half_rot).astype(f32) * 2.0 / ROT)
    angles = places.astype(f32)[:, None] * freqs[None, :]
    sines = jnp.sin(angles)
    cosine = jnp.where(column < ROT, jnp.cos(angles), 1.0)
    left = jnp.where((column >= half_rot) & (column < ROT), sines, 0.0)
    right = jnp.where(column < half_rot, -sines, 0.0)
    return jnp.stack([cosine, left, right])


def dot(left, right, dims):
    return lax.dot_general(left, right, (dims, ((), ())), preferred_element_type=f32)


def nn(left, right):
    return dot(left, right, ((1,), (0,)))


def nt(left, right):
    return dot(left, right, ((1,), (1,)))


def tn(left, right):
    return dot(left, right, ((0,), (0,)))


def key_blocks(jq, blocks):
    return max(jq + 1, blocks // 2)


def block_mask(qpos, kpos, jq, jk, blocks, prefix):
    if jk < jq:
        return None
    causal = kpos <= qpos
    if jk >= blocks // 2:
        return causal
    early = kpos < prefix
    return (causal | early) if jk == jq else early


def head_lane(head):
    lane = lax.broadcasted_iota(jnp.int32, (1, 2 * HD), 1)
    return (lane < HD) if head == 0 else (lane >= HD)


def forward_kernel(blocks, size, info, proj, table, qkv, out, sums):
    w = 2 * HD
    scale = 1.0 / math.sqrt(HD)
    r, prefix = info[0], info[1]
    for j in range(blocks):
        rows = pl.ds(j * size, size)
        cosine, left, right = table[0, rows], table[1, rows], table[2, rows]
        for part in range(2):
            x = proj[rows, part * w : (part + 1) * w]
            x = x * cosine + pltpu.roll(x, 8, 1) * left + pltpu.roll(x, w - 8, 1) * right
            qkv[rows, part * w : (part + 1) * w] = x.astype(bf16)
        qkv[rows, 2 * w : 3 * w] = proj[rows, 2 * w : 3 * w].astype(bf16)
    places = [pl.ds(pl.multiple_of((j ^ r) * size, size), size) for j in range(blocks)]
    for jq in range(blocks):
        count = key_blocks(jq, blocks)
        q = qkv[places[jq], 0:w].astype(f32) * scale
        qpos = jq * size + lax.broadcasted_iota(jnp.int32, (size, size), 0)
        results = []
        tops = []
        for head in range(2):
            qh = jnp.where(head_lane(head), q, 0.0).astype(bf16)
            scores = []
            for jk in range(count):
                s = nt(qh, qkv[places[jk], w : 2 * w])
                kpos = jk * size + lax.broadcasted_iota(jnp.int32, (size, size), 1)
                mask = block_mask(qpos, kpos, jq, jk, blocks, prefix)
                scores.append(s if mask is None else jnp.where(mask, s, masked_fill))
            top = jnp.max(scores[0], axis=1, keepdims=True)
            for s in scores[1:]:
                top = jnp.maximum(top, jnp.max(s, axis=1, keepdims=True))
            total = 0.0
            result = 0.0
            for jk in range(count):
                e = jnp.exp(scores[jk] - top)
                total = total + jnp.sum(e, axis=1, keepdims=True)
                result = result + nn(e.astype(bf16), qkv[places[jk], 2 * w : 3 * w])
            results.append(result / total)
            tops.append(top + jnp.log(total))
        out[places[jq], :] = jnp.where(head_lane(0), results[0], results[1]).astype(bf16)
        both = jnp.where(head_lane(0), tops[0], tops[1])
        flipped = both.T
        sums[0, jq, 0:8, :] = flipped[0:8]
        sums[0, jq, 8:16, :] = flipped[HD : HD + 8]


def backward_kernel(blocks, size, info, qkv, table, sums, grads, out, bias, qm, km, gm, acc):
    w = 2 * HD
    scale = 1.0 / math.sqrt(HD)
    r, prefix = info[0], info[1]
    for head in range(2):
        lanes = head_lane(head)
        for j in range(blocks):
            rows = pl.ds(j * size, size)
            q = qkv[rows, 0:w].astype(f32) * scale
            k = qkv[rows, w : 2 * w].astype(f32) * scale
            qm[head, rows] = jnp.where(lanes, q, 0.0).astype(bf16)
            km[head, rows] = jnp.where(lanes, k, 0.0).astype(bf16)
            gm[head, rows] = jnp.where(lanes, grads[rows, :].astype(f32), 0.0).astype(bf16)
    acc[...] = jnp.zeros_like(acc)
    places = [pl.ds(pl.multiple_of((j ^ r) * size, size), size) for j in range(blocks)]
    for jq in range(blocks):
        count = key_blocks(jq, blocks)
        rq = places[jq]
        qpos = jq * size + lax.broadcasted_iota(jnp.int32, (size, size), 1)
        grad_q = 0.0
        for head in range(2):
            top = sums[0, jq, 8 * head : 8 * head + 1, :]
            probs = []
            products = []
            inner = 0.0
            for jk in range(count):
                s = nt(qkv[places[jk], w : 2 * w], qm[head, rq])
                p = jnp.exp(s - top)
                kpos = jk * size + lax.broadcasted_iota(jnp.int32, (size, size), 0)
                mask = block_mask(qpos, kpos, jq, jk, blocks, prefix)
                if mask is not None:
                    p = jnp.where(mask, p, 0.0)
                t = p * nt(qkv[places[jk], 2 * w : 3 * w], gm[head, rq])
                inner = inner + jnp.sum(t, axis=0, keepdims=True)
                probs.append(p)
                products.append(t)
            for jk in range(count):
                rk = places[jk]
                d = (products[jk] - probs[jk] * inner).astype(bf16)
                acc[1, rk] += nn(probs[jk].astype(bf16), gm[head, rq])
                acc[0, rk] += nn(d, qm[head, rq])
                grad_q = grad_q + tn(d, km[head, rk])
        cosine, left, right = table[0, rq], table[1, rq], table[2, rq]
        x = grad_q
        x = x * cosine - pltpu.roll(x, 8, 1) * left - pltpu.roll(x, w - 8, 1) * right
        out[rq, 0:w] = x.astype(bf16)
    bias_q = 0.0
    bias_k = 0.0
    bias_v = 0.0
    for j in range(blocks):
        rows = pl.ds(j * size, size)
        x = acc[0, rows]
        x = x * table[0, rows]
        x = x - pltpu.roll(acc[0, rows], 8, 1) * table[1, rows]
        x = x - pltpu.roll(acc[0, rows], w - 8, 1) * table[2, rows]
        x = x.astype(bf16)
        y = acc[1, rows].astype(bf16)
        out[rows, w : 2 * w] = x
        out[rows, 2 * w : 3 * w] = y
        bias_q = bias_q + jnp.sum(out[rows, 0:w].astype(f32), axis=0, keepdims=True)
        bias_k = bias_k + jnp.sum(x.astype(f32), axis=0, keepdims=True)
        bias_v = bias_v + jnp.sum(y.astype(f32), axis=0, keepdims=True)
    row = jnp.concatenate([bias_q, bias_k, bias_v], axis=1)
    bias[0] = jnp.broadcast_to(row, (8, 3 * w))


def attend_forward(info, projected, table, blocks):
    length = projected.shape[0]
    w = 2 * HD
    pairs = projected.shape[1] // (3 * w)
    size = length // blocks
    spec = pltpu.PrefetchScalarGridSpec(
        num_scalar_prefetch=1,
        grid=(pairs,),
        in_specs=[
            pl.BlockSpec((length, 3 * w), lambda p, i: (0, p)),
            pl.BlockSpec((3, length, w), lambda p, i: (0, 0, 0)),
        ],
        out_specs=[
            pl.BlockSpec((length, 3 * w), lambda p, i: (0, p)),
            pl.BlockSpec((length, w), lambda p, i: (0, p)),
            pl.BlockSpec((1, blocks, 16, size), lambda p, i: (p, 0, 0, 0)),
        ],
    )
    return pl.pallas_call(
        lambda *refs: forward_kernel(blocks, size, *refs),
        grid_spec=spec,
        out_shape=[
            jax.ShapeDtypeStruct((length, 3 * w * pairs), bf16),
            jax.ShapeDtypeStruct((length, w * pairs), bf16),
            jax.ShapeDtypeStruct((pairs, blocks, 16, size), f32),
        ],
        name="attn_f",
        compiler_params=pltpu.CompilerParams(vmem_limit_bytes=48 << 20),
    )(info, projected, table)


def attend_backward(info, qkv, table, sums, grads, blocks):
    length = qkv.shape[0]
    w = 2 * HD
    pairs = qkv.shape[1] // (3 * w)
    size = length // blocks
    spec = pltpu.PrefetchScalarGridSpec(
        num_scalar_prefetch=1,
        grid=(pairs,),
        in_specs=[
            pl.BlockSpec((length, 3 * w), lambda p, i: (0, p)),
            pl.BlockSpec((3, length, w), lambda p, i: (0, 0, 0)),
            pl.BlockSpec((1, blocks, 16, size), lambda p, i: (p, 0, 0, 0)),
            pl.BlockSpec((length, w), lambda p, i: (0, p)),
        ],
        out_specs=[
            pl.BlockSpec((length, 3 * w), lambda p, i: (0, p)),
            pl.BlockSpec((1, 8, 3 * w), lambda p, i: (p, 0, 0)),
        ],
        scratch_shapes=[
            pltpu.VMEM((2, length, w), bf16),
            pltpu.VMEM((2, length, w), bf16),
            pltpu.VMEM((2, length, w), bf16),
            pltpu.VMEM((2, length, w), f32),
        ],
    )
    return pl.pallas_call(
        lambda *refs: backward_kernel(blocks, size, *refs),
        grid_spec=spec,
        out_shape=[
            jax.ShapeDtypeStruct((length, 3 * w * pairs), bf16),
            jax.ShapeDtypeStruct((pairs, 8, 3 * w), f32),
        ],
        name="attn_b",
        compiler_params=pltpu.CompilerParams(vmem_limit_bytes=48 << 20),
    )(info, qkv, table, sums, grads)


def pack_kernel(R, q, info, gate_up, down, out):
    fs = down.shape[1] // R
    rows = down.shape[0] // q
    for slot in range(R * q):
        span = pl.ds((slot % q) * rows, rows)
        lo = (slot // q) * fs
        k = slot ^ info[2]
        out[k, :, 0:fs] = gate_up[0, span, lo : lo + fs]
        out[k, :, fs : 2 * fs] = gate_up[1, span, lo : lo + fs]
        out[k, :, 2 * fs : 3 * fs] = down[span, lo : lo + fs]


def unpack_kernel(C, info, *refs):
    pieces, (gate_up, down, held) = refs[:-3], refs[-3:]
    rows = held.shape[1]
    ff = down.shape[1]
    fs = ff // C
    for k, piece in enumerate(pieces):
        held[k ^ info[3]] = piece[...]
    for place in range(len(pieces)):
        span = pl.ds((place // C) * rows, rows)
        lo = (place % C) * fs
        gate_up[span, lo : lo + fs] = held[place, :, 0:fs]
        gate_up[span, ff + lo : ff + lo + fs] = held[place, :, fs : 2 * fs]
        down[span, lo : lo + fs] = held[place, :, 2 * fs : 3 * fs]


def pack_back_kernel(C, info, gate_up, down, out):
    rows = out.shape[1]
    ff = down.shape[1]
    fs = ff // C
    for place in range(out.shape[0]):
        span = pl.ds((place // C) * rows, rows)
        lo = (place % C) * fs
        k = place ^ info[3]
        out[k, :, 0:fs] = gate_up[span, lo : lo + fs]
        out[k, :, fs : 2 * fs] = gate_up[span, ff + lo : ff + lo + fs]
        out[k, :, 2 * fs : 3 * fs] = down[span, lo : lo + fs]


def unpack_back_kernel(R, q, info, *refs):
    pieces, (gate_up, down, held) = refs[:-3], refs[-3:]
    rows = held.shape[1]
    fs = down.shape[1] // R
    for k, piece in enumerate(pieces):
        held[k ^ info[2]] = piece[...]
    for slot in range(len(pieces)):
        span = pl.ds((slot % q) * rows, rows)
        lo = (slot // q) * fs
        gate_up[0, span, lo : lo + fs] = held[slot, :, 0:fs].astype(f32)
        gate_up[1, span, lo : lo + fs] = held[slot, :, fs : 2 * fs].astype(f32)
        down[span, lo : lo + fs] = held[slot, :, 2 * fs : 3 * fs].astype(f32)


def prepare_kernel(info, qkv, outer, out):
    w = 2 * HD
    cols = outer.shape[1]
    for pair in range(cols // w):
        for part in range(3):
            lo = (3 * pair + part) * w
            out[:, lo : lo + w] = qkv[part, :, pair * w : (pair + 1) * w]
    out[:, 3 * cols :] = outer[...]


def finish_kernel(info, grads, qkv, outer):
    w = 2 * HD
    cols = outer.shape[1]
    for pair in range(cols // w):
        for part in range(3):
            lo = (3 * pair + part) * w
            qkv[part, :, pair * w : (pair + 1) * w] = grads[:, lo : lo + w].astype(f32)
    outer[...] = grads[:, 3 * cols :].astype(f32)


def whole_call(kernel, info, arrays, shapes, scratch=()):
    def spec(shape):
        return pl.BlockSpec(shape, lambda i, s: (0,) * len(shape))

    return pl.pallas_call(
        kernel,
        grid_spec=pltpu.PrefetchScalarGridSpec(
            num_scalar_prefetch=1,
            grid=(1,),
            in_specs=[spec(a.shape) for a in arrays],
            out_specs=[spec(a.shape) for a in shapes],
            scratch_shapes=list(scratch),
        ),
        out_shape=shapes,
        compiler_params=pltpu.CompilerParams(vmem_limit_bytes=48 << 20),
    )(info, *arrays)


def split_kernel(info, mine, other, mine_out, other_out):
    mine_out[...] = mine[...]
    other_out[...] = other[...]


def split_columns(info, array, parts):
    length, width = array.shape
    block = width // (2 * parts)
    shape = jax.ShapeDtypeStruct((length, width // 2), array.dtype)
    return pl.pallas_call(
        split_kernel,
        grid_spec=pltpu.PrefetchScalarGridSpec(
            num_scalar_prefetch=1,
            grid=(parts,),
            in_specs=[
                pl.BlockSpec((length, block), lambda j, s: (0, 2 * j + s[4])),
                pl.BlockSpec((length, block), lambda j, s: (0, 2 * j + 1 - s[4])),
            ],
            out_specs=[pl.BlockSpec((length, block), lambda j, s: (0, j))] * 2,
        ),
        out_shape=[shape, shape],
    )(info, array, array)


def make_body(mesh):
    R = mesh.shape[ROW]
    C = mesh.shape[COL]
    N = max(R, C)

    def row_permute(block, k):
        return lax.ppermute(block, ROW, [(i, i ^ k) for i in range(R)])

    def gather_rel(block, after=None):
        if R != 4:
            return [block] + [row_permute(block, k) for k in range(1, R)]
        half = block.shape[0] // 2
        if after is not None:
            block, _ = lax.optimization_barrier((block, after))
        one = row_permute(block, 1)
        two = row_permute(block, 2)
        top = row_permute(one[:half], 2)
        low = row_permute(two[half:], 1)
        return [block, one, two, jnp.concatenate([top, low], axis=0)]

    def scatter_rel(blocks):
        if R != 4:
            total = blocks[0]
            for k in range(1, R):
                total = total + row_permute(blocks[k].astype(bf16), k).astype(f32)
            return total
        half = blocks[0].shape[0] // 2
        b = [(x[:half], x[half:]) for x in blocks]
        top = row_permute(jnp.concatenate([b[1][0], b[3][0]]).astype(bf16), 1).astype(f32)
        low = row_permute(jnp.concatenate([b[2][1], b[3][1]]).astype(bf16), 2).astype(f32)
        top2 = row_permute((b[2][0].astype(f32) + top[half:]).astype(bf16), 2)
        low1 = row_permute((b[1][1].astype(f32) + low[half:]).astype(bf16), 1)
        top = b[0][0].astype(f32) + top[:half] + top2.astype(f32)
        low = b[0][1].astype(f32) + low[:half] + low1.astype(f32)
        return jnp.concatenate([top, low], axis=0)

    def source_place(s, c):
        return (s % (R // C)) * C + c if C <= R else c

    def source_dest(s, c, k):
        slot = source_place(s, c) ^ k
        if C <= R:
            return slot, s // (R // C)
        q = C // R
        return slot // q, s * q + slot % q

    def exchange_pairs(k):
        pairs = []
        for s in range(R):
            for c in range(C):
                dr, dc = source_dest(s, c, k)
                pairs.append((s * C + c, dr * C + dc))
        return pairs

    def spread(packed):
        return [lax.ppermute(packed[k], (ROW, COL), exchange_pairs(k)) for k in range(N)]

    def bring_back(packed):
        return [
            lax.ppermute(packed[k], (ROW, COL), [(b, a) for a, b in exchange_pairs(k)])
            for k in range(N)
        ]

    def sum_everywhere(array):
        for name in (COL, DP, ROW):
            size = mesh.shape[name]
            step = 1
            while step < size:
                other = lax.ppermute(array, name, [(i, i ^ step) for i in range(size)])
                step *= 2
                array = array + other
        return array

    def pair_sum(mine, other, right):
        away = tn(other, right).astype(bf16)
        got = lax.ppermute(away, COL, [(0, 1), (1, 0)])
        return (tn(mine, right) + got.astype(f32)).astype(bf16)

    def body(
        tokens,
        prefix_len,
        norm1_gain,
        norm1_bias,
        query_key_value_weight,
        query_key_value_bias,
        attention_output_weight,
        norm2_gain,
        norm2_bias,
        gate_up_projection_weight,
        down_projection_weight,
        grad_out,
    ):
        r = lax.axis_index(ROW)
        c = lax.axis_index(COL)
        block = tokens.shape[1]
        width = tokens.shape[2]
        head_cols = query_key_value_weight.shape[2]
        pairs = head_cols // (2 * HD)
        places = (jnp.arange(R)[:, None] ^ r) * block + jnp.arange(block)[None, :]
        table = rotary_tables(places.reshape(-1))
        w_rows, _, ff_local = gate_up_projection_weight.shape
        ff_slice = ff_local // R
        ff = ff_slice * C
        q_rows = max(1, C // R)
        u = source_place(r, c)
        v = r if C <= R else r * q_rows + c % q_rows
        info = jnp.stack([r, prefix_len[0], u, v, c]).astype(jnp.int32)
        rows = w_rows // q_rows
        a_rows = N // C * rows
        piece = (3 * ff_slice + 127) // 128 * 128

        gain1 = norm1_gain.astype(f32)
        gain2 = norm2_gain.astype(f32)
        inputs = tokens[0].astype(f32)
        first, first_std, first_inv = layer_norm_forward(inputs, gain1, norm1_bias.astype(f32))
        seq_in = jnp.concatenate(gather_rel(first.astype(bf16)), axis=0)

        (attn_shard,) = whole_call(
            prepare_kernel,
            info,
            [query_key_value_weight.transpose(1, 0, 2), attention_output_weight],
            [jax.ShapeDtypeStruct((attention_output_weight.shape[0], 4 * head_cols), bf16)],
        )
        w_attn = lax.all_gather(attn_shard, (DP, COL), axis=0, tiled=True)
        (packed,) = whole_call(
            functools.partial(pack_kernel, R, q_rows),
            info,
            [gate_up_projection_weight.transpose(1, 0, 2), down_projection_weight],
            [jax.ShapeDtypeStruct((N, rows, piece), bf16)],
        )
        packed, seq_in = lax.optimization_barrier((packed, seq_in))
        held = pltpu.VMEM((N, rows, piece), bf16)
        gu_shard, down_shard = whole_call(
            functools.partial(unpack_kernel, C),
            info,
            spread(packed),
            [
                jax.ShapeDtypeStruct((a_rows, 2 * ff), bf16),
                jax.ShapeDtypeStruct((a_rows, ff), bf16),
            ],
            [held],
        )
        w_gu = lax.all_gather(gu_shard, (DP, COL), axis=0, tiled=True)
        w_down = lax.all_gather(down_shard, (DP, COL), axis=0, tiled=True)

        w_attn, _ = lax.optimization_barrier((w_attn, gu_shard))
        w_qkv = w_attn[:, : 3 * head_cols]
        w_out = w_attn[:, 3 * head_cols :]
        dy_rel = jnp.concatenate(gather_rel(grad_out[0], gu_shard), axis=0)
        dy = grad_out[0]
        bias = query_key_value_bias.astype(f32).reshape(3, pairs, 2 * HD).transpose(1, 0, 2)
        projected = nn(seq_in, w_qkv)
        projected = projected + bias.reshape(-1)

        qkv, attended, log_sums = attend_forward(info, projected, table, R)
        own = nt(attended[:block], w_out)
        others = nt(attended[block:], w_out).astype(bf16)
        residual = scatter_rel([own] + [others[k * block : (k + 1) * block] for k in range(R - 1)])
        middle = inputs + residual

        second, second_std, second_inv = layer_norm_forward(
            middle, gain2, norm2_bias.astype(f32)
        )
        second_in = jnp.concatenate(gather_rel(second.astype(bf16)), axis=0)
        gate_up = nn(second_in, w_gu)
        gate_vals = gate_up[:, :ff]
        up_vals = gate_up[:, ff:]
        sig = jax.nn.sigmoid(gate_vals)
        swish = gate_vals * sig
        hidden = (swish * up_vals).astype(bf16)
        if C == 2:
            seq_halves = split_columns(info, seq_in, mesh.shape[DP])
            halves = split_columns(info, dy_rel, mesh.shape[DP])
            grad_down = pair_sum(*halves, hidden)
            _, w_down = lax.optimization_barrier((grad_down, w_down))
            grad_down = lax.psum_scatter(grad_down, DP, scatter_dimension=0, tiled=True)
        else:
            grad_down = tn(dy_rel, hidden).astype(bf16)
            _, w_down = lax.optimization_barrier((grad_down, w_down))
            grad_down = lax.psum_scatter(
                grad_down, (DP, COL), scatter_dimension=0, tiled=True
            )
        grad_hidden = nn(dy_rel, w_down)
        grad_gate = grad_hidden * up_vals * sig * (1.0 + gate_vals * (1.0 - sig))
        grad_up = grad_hidden * swish
        grad_gu_vals = jnp.concatenate([grad_gate.astype(bf16), grad_up.astype(bf16)], axis=1)
        if C == 2:
            halves = split_columns(info, second_in, mesh.shape[DP])
            away = tn(halves[1], grad_gu_vals).astype(bf16)
            got = lax.ppermute(away, COL, [(0, 1), (1, 0)])
            second_vals, _ = lax.optimization_barrier((grad_gu_vals, away))
        else:
            second_vals = grad_gu_vals
        own = nt(second_vals[:block], w_gu)
        others = nt(second_vals[block:], w_gu).astype(bf16)
        others, grad_gu_vals = lax.optimization_barrier((others, grad_gu_vals))
        grad_second = scatter_rel(
            [own] + [others[k * block : (k + 1) * block] for k in range(R - 1)]
        )
        if C == 2:
            grad_gu = (tn(halves[0], grad_gu_vals) + got.astype(f32)).astype(bf16)
            grad_gu = lax.psum_scatter(grad_gu, DP, scatter_dimension=0, tiled=True)
        else:
            grad_gu = tn(second_in, grad_gu_vals).astype(bf16)
            grad_gu = lax.psum_scatter(grad_gu, (DP, COL), scatter_dimension=0, tiled=True)

        grad_middle = dy.astype(f32) + layer_norm_backward(
            grad_second, second_std, second_inv, gain2
        )
        gain2_grad = jnp.sum(grad_second * second_std, axis=0)
        bias2_grad = jnp.sum(grad_second, axis=0)

        branch = jnp.concatenate(gather_rel(grad_middle.astype(bf16)), axis=0)
        own = nt(hidden[:block], w_down)
        others = nt(hidden[block:], w_down).astype(bf16)
        others, _ = lax.optimization_barrier((others, branch))
        mixed = scatter_rel(
            [own] + [others[k * block : (k + 1) * block] for k in range(R - 1)]
        )
        layer_out = (middle + mixed).astype(bf16)
        grad_heads = nn(branch, w_out).astype(bf16)
        grad_proj, bias_local = attend_backward(info, qkv, table, log_sums, grad_heads, R)
        bias_local = bias_local[:, 0].reshape(pairs, 3, 2 * HD)
        bias_local = bias_local.transpose(1, 0, 2).reshape(3, head_cols)
        if C == 2:
            outer = tn(branch, attended).astype(bf16).reshape(mesh.shape[DP], C, -1, head_cols)
            away = lax.dynamic_index_in_dim(outer, 1 - c, 1, keepdims=False)
            mine = lax.dynamic_index_in_dim(outer, c, 1, keepdims=False)
            got = lax.ppermute(away.reshape(-1, head_cols), COL, [(0, 1), (1, 0)])
            outer = mine.reshape(-1, head_cols).astype(f32) + got.astype(f32)
            grad_attn = jnp.concatenate(
                [pair_sum(*seq_halves, grad_proj), outer.astype(bf16)], axis=1
            )
            grad_proj, _ = lax.optimization_barrier((grad_proj, grad_attn))
            grad_attn = lax.psum_scatter(grad_attn, DP, scatter_dimension=0, tiled=True)
        else:
            grad_attn = jnp.concatenate(
                [tn(seq_in, grad_proj).astype(bf16), tn(branch, attended).astype(bf16)], axis=1
            )
            grad_attn = lax.psum_scatter(
                grad_attn, (DP, COL), scatter_dimension=0, tiled=True
            )
        own = nt(grad_proj[:block], w_qkv)
        others = nt(grad_proj[block:], w_qkv).astype(bf16)
        grad_first = scatter_rel(
            [own] + [others[k * block : (k + 1) * block] for k in range(R - 1)]
        )
        input_grad = grad_middle + layer_norm_backward(grad_first, first_std, first_inv, gain1)
        gain1_grad = jnp.sum(grad_first * first_std, axis=0)
        bias1_grad = jnp.sum(grad_first, axis=0)

        col_offset = r * head_cols
        bias_full = lax.dynamic_update_slice(
            jnp.zeros((3, width), f32), bias_local, (jnp.int32(0), col_offset)
        )
        sums = jnp.stack([gain1_grad, bias1_grad, gain2_grad, bias2_grad])
        sums = sum_everywhere(jnp.concatenate([sums, bias_full], axis=0))
        grad_bias = lax.dynamic_slice_in_dim(sums[4:], col_offset, head_cols, 1)

        (packed,) = whole_call(
            functools.partial(pack_back_kernel, C),
            info,
            [grad_gu, grad_down],
            [jax.ShapeDtypeStruct((N, rows, piece), bf16)],
        )
        home_gu, home_down = whole_call(
            functools.partial(unpack_back_kernel, R, q_rows),
            info,
            bring_back(packed),
            [
                jax.ShapeDtypeStruct((2, w_rows, ff_local), f32),
                jax.ShapeDtypeStruct((w_rows, ff_local), f32),
            ],
            [held],
        )
        home_qkv, home_out = whole_call(
            finish_kernel,
            info,
            [grad_attn],
            [
                jax.ShapeDtypeStruct((3, grad_attn.shape[0], head_cols), f32),
                jax.ShapeDtypeStruct((grad_attn.shape[0], head_cols), f32),
            ],
        )
        return (
            layer_out[None],
            input_grad[None],
            sums[0],
            sums[1],
            home_qkv.transpose(1, 0, 2),
            grad_bias,
            home_out,
            sums[2],
            sums[3],
            home_gu.transpose(1, 0, 2),
            home_down,
        )

    return body


def solution(mesh):
    in_specs = (
        P((DP, COL), ROW, None),
        P((DP, COL)),
        P(),
        P(),
        P((DP, COL), None, ROW),
        P(None, ROW),
        P((DP, COL), ROW),
        P(),
        P(),
        P((DP, ROW), None, COL),
        P((DP, ROW), COL),
        P((DP, COL), ROW, None),
    )
    out_specs = (
        P((DP, COL), ROW, None),
        P((DP, COL), ROW, None),
        P(),
        P(),
        P((DP, COL), None, ROW),
        P(None, ROW),
        P((DP, COL), ROW),
        P(),
        P(),
        P((DP, ROW), None, COL),
        P((DP, ROW), COL),
    )
    body = make_body(mesh)

    return jax.shard_map(body, mesh=mesh, in_specs=in_specs, out_specs=out_specs, check_vma=False)
```

```python
import functools
import math

import jax
import jax.numpy as jnp
from jax import lax
from jax.experimental import pallas as pl
from jax.experimental.pallas import tpu as pltpu
from jax.sharding import PartitionSpec as P


HD = 64
ROT = 16

norm_eps = 1e-05
rope_base = 10000.0
masked_fill = -1e30

DP, ROW, COL = "dp", "row", "col"

bf16 = jnp.bfloat16
f32 = jnp.float32


def layer_norm_forward(values, norm_gain, norm_shift):
    centre = jnp.mean(values, axis=-1, keepdims=True)
    centred = values - centre
    variance = jnp.mean(centred * centred, axis=-1, keepdims=True)
    inverse = lax.rsqrt(variance + norm_eps)
    normed = centred * inverse
    return (normed * norm_gain + norm_shift, normed, inverse)


def layer_norm_backward(incoming, normed, inverse, norm_gain):
    scaled = incoming * norm_gain
    inner = jnp.mean(scaled, axis=-1, keepdims=True)
    along = jnp.mean(scaled * normed, axis=-1, keepdims=True)
    return inverse * (scaled - inner - normed * along)


def rotary_tables(places):
    half_rot = ROT // 2
    column = jnp.arange(2 * HD) % HD
    freqs = rope_base ** (-(column % half_rot).astype(f32) * 2.0 / ROT)
    angles = places.astype(f32)[:, None] * freqs[None, :]
    sines = jnp.sin(angles)
    cosine = jnp.where(column < ROT, jnp.cos(angles), 1.0)
    left = jnp.where((column >= half_rot) & (column < ROT), sines, 0.0)
    right = jnp.where(column < half_rot, -sines, 0.0)
    return jnp.stack([cosine, left, right])


def dot(left, right, dims):
    return lax.dot_general(left, right, (dims, ((), ())), preferred_element_type=f32)


def nn(left, right):
    return dot(left, right, ((1,), (0,)))


def nt(left, right):
    return dot(left, right, ((1,), (1,)))


def tn(left, right):
    return dot(left, right, ((0,), (0,)))


def key_blocks(jq, blocks):
    return max(jq + 1, blocks // 2)


def block_mask(qpos, kpos, jq, jk, blocks, prefix):
    if jk < jq:
        return None
    causal = kpos <= qpos
    if jk >= blocks // 2:
        return causal
    early = kpos < prefix
    return (causal | early) if jk == jq else early


def head_lane(head):
    lane = lax.broadcasted_iota(jnp.int32, (1, 2 * HD), 1)
    return (lane < HD) if head == 0 else (lane >= HD)


def forward_kernel(blocks, size, info, proj, table, qkv, out, sums):
    w = 2 * HD
    scale = 1.0 / math.sqrt(HD)
    r, prefix = info[0], info[1]
    for j in range(blocks):
        rows = pl.ds(j * size, size)
        cosine, left, right = table[0, rows], table[1, rows], table[2, rows]
        for part in range(2):
            x = proj[rows, part * w : (part + 1) * w]
            x = x * cosine + pltpu.roll(x, 8, 1) * left + pltpu.roll(x, w - 8, 1) * right
            qkv[rows, part * w : (part + 1) * w] = x.astype(bf16)
        qkv[rows, 2 * w : 3 * w] = proj[rows, 2 * w : 3 * w].astype(bf16)
    places = [pl.ds(pl.multiple_of((j ^ r) * size, size), size) for j in range(blocks)]
    for jq in range(blocks):
        count = key_blocks(jq, blocks)
        q = qkv[places[jq], 0:w].astype(f32) * scale
        qpos = jq * size + lax.broadcasted_iota(jnp.int32, (size, size), 0)
        results = []
        tops = []
        for head in range(2):
            qh = jnp.where(head_lane(head), q, 0.0).astype(bf16)
            scores = []
            for jk in range(count):
                s = nt(qh, qkv[places[jk], w : 2 * w])
                kpos = jk * size + lax.broadcasted_iota(jnp.int32, (size, size), 1)
                mask = block_mask(qpos, kpos, jq, jk, blocks, prefix)
                scores.append(s if mask is None else jnp.where(mask, s, masked_fill))
            top = jnp.max(scores[0], axis=1, keepdims=True)
            for s in scores[1:]:
                top = jnp.maximum(top, jnp.max(s, axis=1, keepdims=True))
            total = 0.0
            result = 0.0
            for jk in range(count):
                e = jnp.exp(scores[jk] - top)
                total = total + jnp.sum(e, axis=1, keepdims=True)
                result = result + nn(e.astype(bf16), qkv[places[jk], 2 * w : 3 * w])
            results.append(result / total)
            tops.append(top + jnp.log(total))
        out[places[jq], :] = jnp.where(head_lane(0), results[0], results[1]).astype(bf16)
        both = jnp.where(head_lane(0), tops[0], tops[1])
        flipped = both.T
        sums[0, jq, 0:8, :] = flipped[0:8]
        sums[0, jq, 8:16, :] = flipped[HD : HD + 8]


def backward_kernel(blocks, size, info, qkv, table, sums, grads, out, bias, qm, km, gm, acc):
    w = 2 * HD
    scale = 1.0 / math.sqrt(HD)
    r, prefix = info[0], info[1]
    for head in range(2):
        lanes = head_lane(head)
        for j in range(blocks):
            rows = pl.ds(j * size, size)
            q = qkv[rows, 0:w].astype(f32) * scale
            k = qkv[rows, w : 2 * w].astype(f32) * scale
            qm[head, rows] = jnp.where(lanes, q, 0.0).astype(bf16)
            km[head, rows] = jnp.where(lanes, k, 0.0).astype(bf16)
            gm[head, rows] = jnp.where(lanes, grads[rows, :].astype(f32), 0.0).astype(bf16)
    acc[...] = jnp.zeros_like(acc)
    places = [pl.ds(pl.multiple_of((j ^ r) * size, size), size) for j in range(blocks)]
    for jq in range(blocks):
        count = key_blocks(jq, blocks)
        rq = places[jq]
        qpos = jq * size + lax.broadcasted_iota(jnp.int32, (size, size), 1)
        grad_q = 0.0
        for head in range(2):
            top = sums[0, jq, 8 * head : 8 * head + 1, :]
            probs = []
            products = []
            inner = 0.0
            for jk in range(count):
                s = nt(qkv[places[jk], w : 2 * w], qm[head, rq])
                p = jnp.exp(s - top)
                kpos = jk * size + lax.broadcasted_iota(jnp.int32, (size, size), 0)
                mask = block_mask(qpos, kpos, jq, jk, blocks, prefix)
                if mask is not None:
                    p = jnp.where(mask, p, 0.0)
                t = p * nt(qkv[places[jk], 2 * w : 3 * w], gm[head, rq])
                inner = inner + jnp.sum(t, axis=0, keepdims=True)
                probs.append(p)
                products.append(t)
            for jk in range(count):
                rk = places[jk]
                d = (products[jk] - probs[jk] * inner).astype(bf16)
                acc[1, rk] += nn(probs[jk].astype(bf16), gm[head, rq])
                acc[0, rk] += nn(d, qm[head, rq])
                grad_q = grad_q + tn(d, km[head, rk])
        cosine, left, right = table[0, rq], table[1, rq], table[2, rq]
        x = grad_q
        x = x * cosine - pltpu.roll(x, 8, 1) * left - pltpu.roll(x, w - 8, 1) * right
        out[rq, 0:w] = x.astype(bf16)
    bias_q = 0.0
    bias_k = 0.0
    bias_v = 0.0
    for j in range(blocks):
        rows = pl.ds(j * size, size)
        x = acc[0, rows]
        x = x * table[0, rows]
        x = x - pltpu.roll(acc[0, rows], 8, 1) * table[1, rows]
        x = x - pltpu.roll(acc[0, rows], w - 8, 1) * table[2, rows]
        x = x.astype(bf16)
        y = acc[1, rows].astype(bf16)
        out[rows, w : 2 * w] = x
        out[rows, 2 * w : 3 * w] = y
        bias_q = bias_q + jnp.sum(out[rows, 0:w].astype(f32), axis=0, keepdims=True)
        bias_k = bias_k + jnp.sum(x.astype(f32), axis=0, keepdims=True)
        bias_v = bias_v + jnp.sum(y.astype(f32), axis=0, keepdims=True)
    row = jnp.concatenate([bias_q, bias_k, bias_v], axis=1)
    bias[0] = jnp.broadcast_to(row, (8, 3 * w))


def attend_forward(info, projected, table, blocks):
    length = projected.shape[0]
    w = 2 * HD
    pairs = projected.shape[1] // (3 * w)
    size = length // blocks
    spec = pltpu.PrefetchScalarGridSpec(
        num_scalar_prefetch=1,
        grid=(pairs,),
        in_specs=[
            pl.BlockSpec((length, 3 * w), lambda p, i: (0, p)),
            pl.BlockSpec((3, length, w), lambda p, i: (0, 0, 0)),
        ],
        out_specs=[
            pl.BlockSpec((length, 3 * w), lambda p, i: (0, p)),
            pl.BlockSpec((length, w), lambda p, i: (0, p)),
            pl.BlockSpec((1, blocks, 16, size), lambda p, i: (p, 0, 0, 0)),
        ],
    )
    return pl.pallas_call(
        lambda *refs: forward_kernel(blocks, size, *refs),
        grid_spec=spec,
        out_shape=[
            jax.ShapeDtypeStruct((length, 3 * w * pairs), bf16),
            jax.ShapeDtypeStruct((length, w * pairs), bf16),
            jax.ShapeDtypeStruct((pairs, blocks, 16, size), f32),
        ],
        name="attn_f",
        compiler_params=pltpu.CompilerParams(vmem_limit_bytes=48 << 20),
    )(info, projected, table)


def attend_backward(info, qkv, table, sums, grads, blocks):
    length = qkv.shape[0]
    w = 2 * HD
    pairs = qkv.shape[1] // (3 * w)
    size = length // blocks
    spec = pltpu.PrefetchScalarGridSpec(
        num_scalar_prefetch=1,
        grid=(pairs,),
        in_specs=[
            pl.BlockSpec((length, 3 * w), lambda p, i: (0, p)),
            pl.BlockSpec((3, length, w), lambda p, i: (0, 0, 0)),
            pl.BlockSpec((1, blocks, 16, size), lambda p, i: (p, 0, 0, 0)),
            pl.BlockSpec((length, w), lambda p, i: (0, p)),
        ],
        out_specs=[
            pl.BlockSpec((length, 3 * w), lambda p, i: (0, p)),
            pl.BlockSpec((1, 8, 3 * w), lambda p, i: (p, 0, 0)),
        ],
        scratch_shapes=[
            pltpu.VMEM((2, length, w), bf16),
            pltpu.VMEM((2, length, w), bf16),
            pltpu.VMEM((2, length, w), bf16),
            pltpu.VMEM((2, length, w), f32),
        ],
    )
    return pl.pallas_call(
        lambda *refs: backward_kernel(blocks, size, *refs),
        grid_spec=spec,
        out_shape=[
            jax.ShapeDtypeStruct((length, 3 * w * pairs), bf16),
            jax.ShapeDtypeStruct((pairs, 8, 3 * w), f32),
        ],
        name="attn_b",
        compiler_params=pltpu.CompilerParams(vmem_limit_bytes=48 << 20),
    )(info, qkv, table, sums, grads)


def pack_kernel(R, q, info, gate_up, down, out):
    fs = down.shape[1] // R
    rows = down.shape[0] // q
    for slot in range(R * q):
        span = pl.ds((slot % q) * rows, rows)
        lo = (slot // q) * fs
        k = slot ^ info[2]
        out[k, :, 0:fs] = gate_up[0, span, lo : lo + fs]
        out[k, :, fs : 2 * fs] = gate_up[1, span, lo : lo + fs]
        out[k, :, 2 * fs : 3 * fs] = down[span, lo : lo + fs]


def unpack_kernel(C, info, *refs):
    pieces, (gate_up, down, held) = refs[:-3], refs[-3:]
    rows = held.shape[1]
    ff = down.shape[1]
    fs = ff // C
    for k, piece in enumerate(pieces):
        held[k ^ info[3]] = piece[...]
    for place in range(len(pieces)):
        span = pl.ds((place // C) * rows, rows)
        lo = (place % C) * fs
        gate_up[span, lo : lo + fs] = held[place, :, 0:fs]
        gate_up[span, ff + lo : ff + lo + fs] = held[place, :, fs : 2 * fs]
        down[span, lo : lo + fs] = held[place, :, 2 * fs : 3 * fs]


def pack_back_kernel(C, info, gate_up, down, out):
    rows = out.shape[1]
    ff = down.shape[1]
    fs = ff // C
    for place in range(out.shape[0]):
        span = pl.ds((place // C) * rows, rows)
        lo = (place % C) * fs
        k = place ^ info[3]
        out[k, :, 0:fs] = gate_up[span, lo : lo + fs]
        out[k, :, fs : 2 * fs] = gate_up[span, ff + lo : ff + lo + fs]
        out[k, :, 2 * fs : 3 * fs] = down[span, lo : lo + fs]


def unpack_back_kernel(R, q, info, *refs):
    pieces, (gate_up, down, held) = refs[:-3], refs[-3:]
    rows = held.shape[1]
    fs = down.shape[1] // R
    for k, piece in enumerate(pieces):
        held[k ^ info[2]] = piece[...]
    for slot in range(len(pieces)):
        span = pl.ds((slot % q) * rows, rows)
        lo = (slot // q) * fs
        gate_up[span, 0, lo : lo + fs] = held[slot, :, 0:fs].astype(f32)
        gate_up[span, 1, lo : lo + fs] = held[slot, :, fs : 2 * fs].astype(f32)
        down[span, lo : lo + fs] = held[slot, :, 2 * fs : 3 * fs].astype(f32)


def prepare_kernel(info, qkv, outer, out):
    w = 2 * HD
    cols = outer.shape[1]
    for pair in range(cols // w):
        for part in range(3):
            lo = (3 * pair + part) * w
            out[:, lo : lo + w] = qkv[part, :, pair * w : (pair + 1) * w]
    out[:, 3 * cols :] = outer[...]


def finish_kernel(info, grads, qkv, outer):
    w = 2 * HD
    cols = outer.shape[1]
    for pair in range(cols // w):
        for part in range(3):
            lo = (3 * pair + part) * w
            qkv[part, :, pair * w : (pair + 1) * w] = grads[:, lo : lo + w].astype(f32)
    outer[...] = grads[:, 3 * cols :].astype(f32)


def whole_call(kernel, info, arrays, shapes, scratch=()):
    def spec(shape):
        return pl.BlockSpec(shape, lambda i, s: (0,) * len(shape))

    return pl.pallas_call(
        kernel,
        grid_spec=pltpu.PrefetchScalarGridSpec(
            num_scalar_prefetch=1,
            grid=(1,),
            in_specs=[spec(a.shape) for a in arrays],
            out_specs=[spec(a.shape) for a in shapes],
            scratch_shapes=list(scratch),
        ),
        out_shape=shapes,
        compiler_params=pltpu.CompilerParams(vmem_limit_bytes=48 << 20),
    )(info, *arrays)


def split_kernel(info, mine, other, mine_out, other_out):
    mine_out[...] = mine[...]
    other_out[...] = other[...]


def split_columns(info, array, parts):
    length, width = array.shape
    block = width // (2 * parts)
    shape = jax.ShapeDtypeStruct((length, width // 2), array.dtype)
    return pl.pallas_call(
        split_kernel,
        grid_spec=pltpu.PrefetchScalarGridSpec(
            num_scalar_prefetch=1,
            grid=(parts,),
            in_specs=[
                pl.BlockSpec((length, block), lambda j, s: (0, 2 * j + s[4])),
                pl.BlockSpec((length, block), lambda j, s: (0, 2 * j + 1 - s[4])),
            ],
            out_specs=[pl.BlockSpec((length, block), lambda j, s: (0, j))] * 2,
        ),
        out_shape=[shape, shape],
    )(info, array, array)


def make_body(mesh):
    R = mesh.shape[ROW]
    C = mesh.shape[COL]
    N = max(R, C)

    def row_permute(block, k):
        return lax.ppermute(block, ROW, [(i, i ^ k) for i in range(R)])

    def gather_rel(block, after=None):
        if R != 4:
            return [block] + [row_permute(block, k) for k in range(1, R)]
        half = block.shape[0] // 2
        if after is not None:
            block, _ = lax.optimization_barrier((block, after))
        one = row_permute(block, 1)
        two = row_permute(block, 2)
        top = row_permute(one[:half], 2)
        low = row_permute(two[half:], 1)
        return [block, one, two, jnp.concatenate([top, low], axis=0)]

    def scatter_rel(blocks):
        if R != 4:
            total = blocks[0]
            for k in range(1, R):
                total = total + row_permute(blocks[k].astype(bf16), k).astype(f32)
            return total
        half = blocks[0].shape[0] // 2
        b = [(x[:half], x[half:]) for x in blocks]
        top2 = row_permute(b[3][0].astype(bf16), 1)
        low1 = row_permute(b[3][1].astype(bf16), 2)
        top0 = row_permute(b[1][0].astype(bf16), 1)
        low0 = row_permute(b[2][1].astype(bf16), 2)
        top2 = row_permute((b[2][0].astype(f32) + top2.astype(f32)).astype(bf16), 2)
        low1 = row_permute((b[1][1].astype(f32) + low1.astype(f32)).astype(bf16), 1)
        top = b[0][0].astype(f32) + top0.astype(f32) + top2.astype(f32)
        low = b[0][1].astype(f32) + low0.astype(f32) + low1.astype(f32)
        return jnp.concatenate([top, low], axis=0)

    def source_place(s, c):
        return (s % (R // C)) * C + c if C <= R else c

    def source_dest(s, c, k):
        slot = source_place(s, c) ^ k
        if C <= R:
            return slot, s // (R // C)
        q = C // R
        return slot // q, s * q + slot % q

    def exchange_pairs(k):
        pairs = []
        for s in range(R):
            for c in range(C):
                dr, dc = source_dest(s, c, k)
                pairs.append((s * C + c, dr * C + dc))
        return pairs

    def spread(packed):
        return [lax.ppermute(packed[k], (ROW, COL), exchange_pairs(k)) for k in range(N)]

    def bring_back(packed):
        return [
            lax.ppermute(packed[k], (ROW, COL), [(b, a) for a, b in exchange_pairs(k)])
            for k in range(N)
        ]

    def sum_everywhere(array):
        for name in (COL, DP, ROW):
            size = mesh.shape[name]
            step = 1
            while step < size:
                other = lax.ppermute(array, name, [(i, i ^ step) for i in range(size)])
                step *= 2
                array = array + other
        return array

    def pair_sum(mine, other, right):
        away = tn(other, right).astype(bf16)
        got = lax.ppermute(away, COL, [(0, 1), (1, 0)])
        return (tn(mine, right) + got.astype(f32)).astype(bf16)

    def body(
        tokens,
        prefix_len,
        norm1_gain,
        norm1_bias,
        query_key_value_weight,
        query_key_value_bias,
        attention_output_weight,
        norm2_gain,
        norm2_bias,
        gate_up_projection_weight,
        down_projection_weight,
        grad_out,
    ):
        r = lax.axis_index(ROW)
        c = lax.axis_index(COL)
        block = tokens.shape[1]
        width = tokens.shape[2]
        head_cols = query_key_value_weight.shape[2]
        pairs = head_cols // (2 * HD)
        places = (jnp.arange(R)[:, None] ^ r) * block + jnp.arange(block)[None, :]
        table = rotary_tables(places.reshape(-1))
        w_rows, _, ff_local = gate_up_projection_weight.shape
        ff_slice = ff_local // R
        ff = ff_slice * C
        q_rows = max(1, C // R)
        u = source_place(r, c)
        v = r if C <= R else r * q_rows + c % q_rows
        info = jnp.stack([r, prefix_len[0], u, v, c]).astype(jnp.int32)
        rows = w_rows // q_rows
        a_rows = N // C * rows
        piece = (3 * ff_slice + 127) // 128 * 128

        gain1 = norm1_gain.astype(f32)
        gain2 = norm2_gain.astype(f32)
        inputs = tokens[0].astype(f32)
        first, first_std, first_inv = layer_norm_forward(inputs, gain1, norm1_bias.astype(f32))
        seq_in = jnp.concatenate(gather_rel(first.astype(bf16)), axis=0)

        (attn_shard,) = whole_call(
            prepare_kernel,
            info,
            [query_key_value_weight.transpose(1, 0, 2), attention_output_weight],
            [jax.ShapeDtypeStruct((attention_output_weight.shape[0], 4 * head_cols), bf16)],
        )
        w_attn = lax.all_gather(attn_shard, (DP, COL), axis=0, tiled=True)
        (packed,) = whole_call(
            functools.partial(pack_kernel, R, q_rows),
            info,
            [gate_up_projection_weight.transpose(1, 0, 2), down_projection_weight],
            [jax.ShapeDtypeStruct((N, rows, piece), bf16)],
        )
        packed, seq_in = lax.optimization_barrier((packed, seq_in))
        held = pltpu.VMEM((N, rows, piece), bf16)
        gu_shard, down_shard = whole_call(
            functools.partial(unpack_kernel, C),
            info,
            spread(packed),
            [
                jax.ShapeDtypeStruct((a_rows, 2 * ff), bf16),
                jax.ShapeDtypeStruct((a_rows, ff), bf16),
            ],
            [held],
        )
        w_gu = lax.all_gather(gu_shard, (DP, COL), axis=0, tiled=True)
        w_down = lax.all_gather(down_shard, (DP, COL), axis=0, tiled=True)

        w_attn, _ = lax.optimization_barrier((w_attn, gu_shard))
        w_qkv = w_attn[:, : 3 * head_cols]
        w_out = w_attn[:, 3 * head_cols :]
        dy_rel = jnp.concatenate(gather_rel(grad_out[0], gu_shard), axis=0)
        dy = grad_out[0]
        bias = query_key_value_bias.astype(f32).reshape(3, pairs, 2 * HD).transpose(1, 0, 2)
        projected = nn(seq_in, w_qkv)
        projected = projected + bias.reshape(-1)

        qkv, attended, log_sums = attend_forward(info, projected, table, R)
        own = nt(attended[:block], w_out)
        others = nt(attended[block:], w_out).astype(bf16)
        residual = scatter_rel([own] + [others[k * block : (k + 1) * block] for k in range(R - 1)])
        middle = inputs + residual

        second, second_std, second_inv = layer_norm_forward(
            middle, gain2, norm2_bias.astype(f32)
        )
        second_in = jnp.concatenate(gather_rel(second.astype(bf16)), axis=0)
        gate_up = nn(second_in, w_gu)
        gate_vals = gate_up[:, :ff]
        up_vals = gate_up[:, ff:]
        sig = jax.nn.sigmoid(gate_vals)
        swish = gate_vals * sig
        hidden = (swish * up_vals).astype(bf16)
        if C == 2:
            seq_halves = split_columns(info, seq_in, mesh.shape[DP])
            halves = split_columns(info, dy_rel, mesh.shape[DP])
            grad_down = pair_sum(*halves, hidden)
            _, w_down = lax.optimization_barrier((grad_down, w_down))
            grad_down = lax.psum_scatter(grad_down, DP, scatter_dimension=0, tiled=True)
        else:
            grad_down = tn(dy_rel, hidden).astype(bf16)
            _, w_down = lax.optimization_barrier((grad_down, w_down))
            grad_down = lax.psum_scatter(
                grad_down, (DP, COL), scatter_dimension=0, tiled=True
            )
        grad_hidden = nn(dy_rel, w_down)
        grad_gate = grad_hidden * up_vals * sig * (1.0 + gate_vals * (1.0 - sig))
        grad_up = grad_hidden * swish
        grad_gu_vals = jnp.concatenate([grad_gate.astype(bf16), grad_up.astype(bf16)], axis=1)
        own = nt(grad_gu_vals[:block], w_gu)
        others = nt(grad_gu_vals[block:], w_gu).astype(bf16)
        others, second_in = lax.optimization_barrier((others, second_in))
        grad_second = scatter_rel(
            [own] + [others[k * block : (k + 1) * block] for k in range(R - 1)]
        )
        grad_gu = tn(second_in, grad_gu_vals).astype(bf16)
        grad_gu = lax.psum_scatter(grad_gu, (DP, COL), scatter_dimension=0, tiled=True)

        grad_middle = dy.astype(f32) + layer_norm_backward(
            grad_second, second_std, second_inv, gain2
        )
        gain2_grad = jnp.sum(grad_second * second_std, axis=0)
        bias2_grad = jnp.sum(grad_second, axis=0)

        branch = jnp.concatenate(gather_rel(grad_middle.astype(bf16)), axis=0)
        own = nt(hidden[:block], w_down)
        others = nt(hidden[block:], w_down).astype(bf16)
        others, _ = lax.optimization_barrier((others, branch))
        mixed = scatter_rel(
            [own] + [others[k * block : (k + 1) * block] for k in range(R - 1)]
        )
        layer_out = (middle + mixed).astype(bf16)
        grad_heads = nn(branch, w_out).astype(bf16)
        grad_proj, bias_local = attend_backward(info, qkv, table, log_sums, grad_heads, R)
        bias_local = bias_local[:, 0].reshape(pairs, 3, 2 * HD)
        bias_local = bias_local.transpose(1, 0, 2).reshape(3, head_cols)
        if C == 2:
            outer = tn(branch, attended).astype(bf16).reshape(mesh.shape[DP], C, -1, head_cols)
            away = lax.dynamic_index_in_dim(outer, 1 - c, 1, keepdims=False)
            mine = lax.dynamic_index_in_dim(outer, c, 1, keepdims=False)
            got = lax.ppermute(away.reshape(-1, head_cols), COL, [(0, 1), (1, 0)])
            outer = mine.reshape(-1, head_cols).astype(f32) + got.astype(f32)
            grad_attn = jnp.concatenate(
                [pair_sum(*seq_halves, grad_proj), outer.astype(bf16)], axis=1
            )
            grad_proj, _ = lax.optimization_barrier((grad_proj, grad_attn))
            grad_attn = lax.psum_scatter(grad_attn, DP, scatter_dimension=0, tiled=True)
        else:
            grad_attn = jnp.concatenate(
                [tn(seq_in, grad_proj).astype(bf16), tn(branch, attended).astype(bf16)], axis=1
            )
            grad_attn = lax.psum_scatter(
                grad_attn, (DP, COL), scatter_dimension=0, tiled=True
            )
        own = nt(grad_proj[:block], w_qkv)
        others = nt(grad_proj[block:], w_qkv).astype(bf16)
        grad_first = scatter_rel(
            [own] + [others[k * block : (k + 1) * block] for k in range(R - 1)]
        )
        input_grad = grad_middle + layer_norm_backward(grad_first, first_std, first_inv, gain1)
        gain1_grad = jnp.sum(grad_first * first_std, axis=0)
        bias1_grad = jnp.sum(grad_first, axis=0)

        col_offset = r * head_cols
        bias_full = lax.dynamic_update_slice(
            jnp.zeros((3, width), f32), bias_local, (jnp.int32(0), col_offset)
        )
        sums = jnp.stack([gain1_grad, bias1_grad, gain2_grad, bias2_grad])
        sums = sum_everywhere(jnp.concatenate([sums, bias_full], axis=0))
        grad_bias = lax.dynamic_slice_in_dim(sums[4:], col_offset, head_cols, 1)

        (packed,) = whole_call(
            functools.partial(pack_back_kernel, C),
            info,
            [grad_gu, grad_down],
            [jax.ShapeDtypeStruct((N, rows, piece), bf16)],
        )
        home_gu, home_down = whole_call(
            functools.partial(unpack_back_kernel, R, q_rows),
            info,
            bring_back(packed),
            [
                jax.ShapeDtypeStruct((w_rows, 2, ff_local), f32),
                jax.ShapeDtypeStruct((w_rows, ff_local), f32),
            ],
            [held],
        )
        home_qkv, home_out = whole_call(
            finish_kernel,
            info,
            [grad_attn],
            [
                jax.ShapeDtypeStruct((3, grad_attn.shape[0], head_cols), f32),
                jax.ShapeDtypeStruct((grad_attn.shape[0], head_cols), f32),
            ],
        )
        return (
            layer_out[None],
            input_grad[None],
            sums[0],
            sums[1],
            home_qkv.transpose(1, 0, 2),
            grad_bias,
            home_out,
            sums[2],
            sums[3],
            home_gu,
            home_down,
        )

    return body


def solution(mesh):
    in_specs = (
        P((DP, COL), ROW, None),
        P((DP, COL)),
        P(),
        P(),
        P((DP, COL), None, ROW),
        P(None, ROW),
        P((DP, COL), ROW),
        P(),
        P(),
        P((DP, ROW), None, COL),
        P((DP, ROW), COL),
        P((DP, COL), ROW, None),
    )
    out_specs = (
        P((DP, COL), ROW, None),
        P((DP, COL), ROW, None),
        P(),
        P(),
        P((DP, COL), None, ROW),
        P(None, ROW),
        P((DP, COL), ROW),
        P(),
        P(),
        P((DP, ROW), None, COL),
        P((DP, ROW), COL),
    )
    body = make_body(mesh)

    return jax.shard_map(body, mesh=mesh, in_specs=in_specs, out_specs=out_specs, check_vma=False)
```

```python
import functools
import math

import jax
import jax.numpy as jnp
from jax import lax
from jax.experimental import pallas as pl
from jax.experimental.pallas import tpu as pltpu
from jax.sharding import PartitionSpec as P


HD = 64
ROT = 16

norm_eps = 1e-05
rope_base = 10000.0
masked_fill = -1e30

DP, ROW, COL = "dp", "row", "col"

bf16 = jnp.bfloat16
f32 = jnp.float32


def layer_norm_forward(values, norm_gain, norm_shift):
    centre = jnp.mean(values, axis=-1, keepdims=True)
    centred = values - centre
    variance = jnp.mean(centred * centred, axis=-1, keepdims=True)
    inverse = lax.rsqrt(variance + norm_eps)
    normed = centred * inverse
    return (normed * norm_gain + norm_shift, normed, inverse)


def layer_norm_backward(incoming, normed, inverse, norm_gain):
    scaled = incoming * norm_gain
    inner = jnp.mean(scaled, axis=-1, keepdims=True)
    along = jnp.mean(scaled * normed, axis=-1, keepdims=True)
    return inverse * (scaled - inner - normed * along)


def rotary_tables(places):
    half_rot = ROT // 2
    column = jnp.arange(2 * HD) % HD
    freqs = rope_base ** (-(column % half_rot).astype(f32) * 2.0 / ROT)
    angles = places.astype(f32)[:, None] * freqs[None, :]
    sines = jnp.sin(angles)
    cosine = jnp.where(column < ROT, jnp.cos(angles), 1.0)
    left = jnp.where((column >= half_rot) & (column < ROT), sines, 0.0)
    right = jnp.where(column < half_rot, -sines, 0.0)
    return jnp.stack([cosine, left, right])


def dot(left, right, dims):
    return lax.dot_general(left, right, (dims, ((), ())), preferred_element_type=f32)


def nn(left, right):
    return dot(left, right, ((1,), (0,)))


def nt(left, right):
    return dot(left, right, ((1,), (1,)))


def tn(left, right):
    return dot(left, right, ((0,), (0,)))


def key_blocks(jq, blocks):
    return max(jq + 1, blocks // 2)


def block_mask(qpos, kpos, jq, jk, blocks, prefix):
    if jk < jq:
        return None
    causal = kpos <= qpos
    if jk >= blocks // 2:
        return causal
    early = kpos < prefix
    return (causal | early) if jk == jq else early


def head_lane(head):
    lane = lax.broadcasted_iota(jnp.int32, (1, 2 * HD), 1)
    return (lane < HD) if head == 0 else (lane >= HD)


def forward_kernel(blocks, size, info, proj, table, qkv, out, sums):
    w = 2 * HD
    scale = 1.0 / math.sqrt(HD)
    r, prefix = info[0], info[1]
    for j in range(blocks):
        rows = pl.ds(j * size, size)
        cosine, left, right = table[0, rows], table[1, rows], table[2, rows]
        for part in range(2):
            x = proj[rows, part * w : (part + 1) * w]
            x = x * cosine + pltpu.roll(x, 8, 1) * left + pltpu.roll(x, w - 8, 1) * right
            qkv[rows, part * w : (part + 1) * w] = x.astype(bf16)
        qkv[rows, 2 * w : 3 * w] = proj[rows, 2 * w : 3 * w].astype(bf16)
    places = [pl.ds(pl.multiple_of((j ^ r) * size, size), size) for j in range(blocks)]
    for jq in range(blocks):
        count = key_blocks(jq, blocks)
        q = qkv[places[jq], 0:w].astype(f32) * scale
        qpos = jq * size + lax.broadcasted_iota(jnp.int32, (size, size), 0)
        results = []
        tops = []
        for head in range(2):
            qh = jnp.where(head_lane(head), q, 0.0).astype(bf16)
            scores = []
            for jk in range(count):
                s = nt(qh, qkv[places[jk], w : 2 * w])
                kpos = jk * size + lax.broadcasted_iota(jnp.int32, (size, size), 1)
                mask = block_mask(qpos, kpos, jq, jk, blocks, prefix)
                scores.append(s if mask is None else jnp.where(mask, s, masked_fill))
            top = jnp.max(scores[0], axis=1, keepdims=True)
            for s in scores[1:]:
                top = jnp.maximum(top, jnp.max(s, axis=1, keepdims=True))
            total = 0.0
            result = 0.0
            for jk in range(count):
                e = jnp.exp(scores[jk] - top)
                total = total + jnp.sum(e, axis=1, keepdims=True)
                result = result + nn(e.astype(bf16), qkv[places[jk], 2 * w : 3 * w])
            results.append(result / total)
            tops.append(top + jnp.log(total))
        out[places[jq], :] = jnp.where(head_lane(0), results[0], results[1]).astype(bf16)
        both = jnp.where(head_lane(0), tops[0], tops[1])
        flipped = both.T
        sums[0, jq, 0:8, :] = flipped[0:8]
        sums[0, jq, 8:16, :] = flipped[HD : HD + 8]


def backward_kernel(blocks, size, info, qkv, table, sums, grads, out, bias, qm, km, gm, acc):
    w = 2 * HD
    scale = 1.0 / math.sqrt(HD)
    r, prefix = info[0], info[1]
    for head in range(2):
        lanes = head_lane(head)
        for j in range(blocks):
            rows = pl.ds(j * size, size)
            q = qkv[rows, 0:w].astype(f32) * scale
            k = qkv[rows, w : 2 * w].astype(f32) * scale
            qm[head, rows] = jnp.where(lanes, q, 0.0).astype(bf16)
            km[head, rows] = jnp.where(lanes, k, 0.0).astype(bf16)
            gm[head, rows] = jnp.where(lanes, grads[rows, :].astype(f32), 0.0).astype(bf16)
    acc[...] = jnp.zeros_like(acc)
    places = [pl.ds(pl.multiple_of((j ^ r) * size, size), size) for j in range(blocks)]
    for jq in range(blocks):
        count = key_blocks(jq, blocks)
        rq = places[jq]
        qpos = jq * size + lax.broadcasted_iota(jnp.int32, (size, size), 1)
        grad_q = 0.0
        for head in range(2):
            top = sums[0, jq, 8 * head : 8 * head + 1, :]
            probs = []
            products = []
            inner = 0.0
            for jk in range(count):
                s = nt(qkv[places[jk], w : 2 * w], qm[head, rq])
                p = jnp.exp(s - top)
                kpos = jk * size + lax.broadcasted_iota(jnp.int32, (size, size), 0)
                mask = block_mask(qpos, kpos, jq, jk, blocks, prefix)
                if mask is not None:
                    p = jnp.where(mask, p, 0.0)
                t = p * nt(qkv[places[jk], 2 * w : 3 * w], gm[head, rq])
                inner = inner + jnp.sum(t, axis=0, keepdims=True)
                probs.append(p)
                products.append(t)
            for jk in range(count):
                rk = places[jk]
                d = (products[jk] - probs[jk] * inner).astype(bf16)
                acc[1, rk] += nn(probs[jk].astype(bf16), gm[head, rq])
                acc[0, rk] += nn(d, qm[head, rq])
                grad_q = grad_q + tn(d, km[head, rk])
        cosine, left, right = table[0, rq], table[1, rq], table[2, rq]
        x = grad_q
        x = x * cosine - pltpu.roll(x, 8, 1) * left - pltpu.roll(x, w - 8, 1) * right
        out[rq, 0:w] = x.astype(bf16)
    bias_q = 0.0
    bias_k = 0.0
    bias_v = 0.0
    for j in range(blocks):
        rows = pl.ds(j * size, size)
        x = acc[0, rows]
        x = x * table[0, rows]
        x = x - pltpu.roll(acc[0, rows], 8, 1) * table[1, rows]
        x = x - pltpu.roll(acc[0, rows], w - 8, 1) * table[2, rows]
        x = x.astype(bf16)
        y = acc[1, rows].astype(bf16)
        out[rows, w : 2 * w] = x
        out[rows, 2 * w : 3 * w] = y
        bias_q = bias_q + jnp.sum(out[rows, 0:w].astype(f32), axis=0, keepdims=True)
        bias_k = bias_k + jnp.sum(x.astype(f32), axis=0, keepdims=True)
        bias_v = bias_v + jnp.sum(y.astype(f32), axis=0, keepdims=True)
    row = jnp.concatenate([bias_q, bias_k, bias_v], axis=1)
    bias[0] = jnp.broadcast_to(row, (8, 3 * w))


def attend_forward(info, projected, table, blocks):
    length = projected.shape[0]
    w = 2 * HD
    pairs = projected.shape[1] // (3 * w)
    size = length // blocks
    spec = pltpu.PrefetchScalarGridSpec(
        num_scalar_prefetch=1,
        grid=(pairs,),
        in_specs=[
            pl.BlockSpec((length, 3 * w), lambda p, i: (0, p)),
            pl.BlockSpec((3, length, w), lambda p, i: (0, 0, 0)),
        ],
        out_specs=[
            pl.BlockSpec((length, 3 * w), lambda p, i: (0, p)),
            pl.BlockSpec((length, w), lambda p, i: (0, p)),
            pl.BlockSpec((1, blocks, 16, size), lambda p, i: (p, 0, 0, 0)),
        ],
    )
    return pl.pallas_call(
        lambda *refs: forward_kernel(blocks, size, *refs),
        grid_spec=spec,
        out_shape=[
            jax.ShapeDtypeStruct((length, 3 * w * pairs), bf16),
            jax.ShapeDtypeStruct((length, w * pairs), bf16),
            jax.ShapeDtypeStruct((pairs, blocks, 16, size), f32),
        ],
        name="attn_f",
        compiler_params=pltpu.CompilerParams(vmem_limit_bytes=48 << 20),
    )(info, projected, table)


def attend_backward(info, qkv, table, sums, grads, blocks):
    length = qkv.shape[0]
    w = 2 * HD
    pairs = qkv.shape[1] // (3 * w)
    size = length // blocks
    spec = pltpu.PrefetchScalarGridSpec(
        num_scalar_prefetch=1,
        grid=(pairs,),
        in_specs=[
            pl.BlockSpec((length, 3 * w), lambda p, i: (0, p)),
            pl.BlockSpec((3, length, w), lambda p, i: (0, 0, 0)),
            pl.BlockSpec((1, blocks, 16, size), lambda p, i: (p, 0, 0, 0)),
            pl.BlockSpec((length, w), lambda p, i: (0, p)),
        ],
        out_specs=[
            pl.BlockSpec((length, 3 * w), lambda p, i: (0, p)),
            pl.BlockSpec((1, 8, 3 * w), lambda p, i: (p, 0, 0)),
        ],
        scratch_shapes=[
            pltpu.VMEM((2, length, w), bf16),
            pltpu.VMEM((2, length, w), bf16),
            pltpu.VMEM((2, length, w), bf16),
            pltpu.VMEM((2, length, w), f32),
        ],
    )
    return pl.pallas_call(
        lambda *refs: backward_kernel(blocks, size, *refs),
        grid_spec=spec,
        out_shape=[
            jax.ShapeDtypeStruct((length, 3 * w * pairs), bf16),
            jax.ShapeDtypeStruct((pairs, 8, 3 * w), f32),
        ],
        name="attn_b",
        compiler_params=pltpu.CompilerParams(vmem_limit_bytes=48 << 20),
    )(info, qkv, table, sums, grads)


def pack_kernel(R, q, info, gate_up, down, out):
    fs = down.shape[1] // R
    rows = down.shape[0] // q
    for slot in range(R * q):
        span = pl.ds((slot % q) * rows, rows)
        lo = (slot // q) * fs
        k = slot ^ info[2]
        out[k, :, 0:fs] = gate_up[0, span, lo : lo + fs]
        out[k, :, fs : 2 * fs] = gate_up[1, span, lo : lo + fs]
        out[k, :, 2 * fs : 3 * fs] = down[span, lo : lo + fs]


def unpack_kernel(C, info, *refs):
    pieces, (gate_up, down, held) = refs[:-3], refs[-3:]
    rows = held.shape[1]
    ff = down.shape[1]
    fs = ff // C
    for k, piece in enumerate(pieces):
        held[k ^ info[3]] = piece[...]
    for place in range(len(pieces)):
        span = pl.ds((place // C) * rows, rows)
        lo = (place % C) * fs
        gate_up[span, lo : lo + fs] = held[place, :, 0:fs]
        gate_up[span, ff + lo : ff + lo + fs] = held[place, :, fs : 2 * fs]
        down[span, lo : lo + fs] = held[place, :, 2 * fs : 3 * fs]


def pack_back_kernel(C, info, gate_up, down, out):
    rows = out.shape[1]
    ff = down.shape[1]
    fs = ff // C
    for place in range(out.shape[0]):
        span = pl.ds((place // C) * rows, rows)
        lo = (place % C) * fs
        k = place ^ info[3]
        out[k, :, 0:fs] = gate_up[span, lo : lo + fs]
        out[k, :, fs : 2 * fs] = gate_up[span, ff + lo : ff + lo + fs]
        out[k, :, 2 * fs : 3 * fs] = down[span, lo : lo + fs]


def unpack_back_kernel(R, q, info, *refs):
    pieces, (gate_up, down, held) = refs[:-3], refs[-3:]
    rows = held.shape[1]
    fs = down.shape[1] // R
    for k, piece in enumerate(pieces):
        held[k ^ info[2]] = piece[...]
    for slot in range(len(pieces)):
        span = pl.ds((slot % q) * rows, rows)
        lo = (slot // q) * fs
        gate_up[span, 0, lo : lo + fs] = held[slot, :, 0:fs].astype(f32)
        gate_up[span, 1, lo : lo + fs] = held[slot, :, fs : 2 * fs].astype(f32)
        down[span, lo : lo + fs] = held[slot, :, 2 * fs : 3 * fs].astype(f32)


def prepare_kernel(info, qkv, outer, out):
    w = 2 * HD
    cols = outer.shape[1]
    for pair in range(cols // w):
        for part in range(3):
            lo = (3 * pair + part) * w
            out[:, lo : lo + w] = qkv[part, :, pair * w : (pair + 1) * w]
    out[:, 3 * cols :] = outer[...]


def finish_kernel(info, grads, qkv, outer):
    w = 2 * HD
    cols = outer.shape[1]
    for pair in range(cols // w):
        for part in range(3):
            lo = (3 * pair + part) * w
            qkv[part, :, pair * w : (pair + 1) * w] = grads[:, lo : lo + w].astype(f32)
    outer[...] = grads[:, 3 * cols :].astype(f32)


def whole_call(kernel, info, arrays, shapes, scratch=()):
    def spec(shape):
        return pl.BlockSpec(shape, lambda i, s: (0,) * len(shape))

    return pl.pallas_call(
        kernel,
        grid_spec=pltpu.PrefetchScalarGridSpec(
            num_scalar_prefetch=1,
            grid=(1,),
            in_specs=[spec(a.shape) for a in arrays],
            out_specs=[spec(a.shape) for a in shapes],
            scratch_shapes=list(scratch),
        ),
        out_shape=shapes,
        compiler_params=pltpu.CompilerParams(vmem_limit_bytes=48 << 20),
    )(info, *arrays)


def split_kernel(info, mine, other, mine_out, other_out):
    mine_out[...] = mine[...]
    other_out[...] = other[...]


def split_columns(info, array, parts):
    length, width = array.shape
    block = width // (2 * parts)
    shape = jax.ShapeDtypeStruct((length, width // 2), array.dtype)
    return pl.pallas_call(
        split_kernel,
        grid_spec=pltpu.PrefetchScalarGridSpec(
            num_scalar_prefetch=1,
            grid=(parts,),
            in_specs=[
                pl.BlockSpec((length, block), lambda j, s: (0, 2 * j + s[4])),
                pl.BlockSpec((length, block), lambda j, s: (0, 2 * j + 1 - s[4])),
            ],
            out_specs=[pl.BlockSpec((length, block), lambda j, s: (0, j))] * 2,
        ),
        out_shape=[shape, shape],
    )(info, array, array)


def make_body(mesh):
    R = mesh.shape[ROW]
    C = mesh.shape[COL]
    N = max(R, C)

    def row_permute(block, k):
        return lax.ppermute(block, ROW, [(i, i ^ k) for i in range(R)])

    def gather_rel(block, after=None):
        if R != 4:
            return [block] + [row_permute(block, k) for k in range(1, R)]
        half = block.shape[0] // 2
        if after is not None:
            block, _ = lax.optimization_barrier((block, after))
        one = row_permute(block, 1)
        two = row_permute(block, 2)
        top = row_permute(one[:half], 2)
        low = row_permute(two[half:], 1)
        return [block, one, two, jnp.concatenate([top, low], axis=0)]

    def scatter_rel(blocks):
        if R != 4:
            total = blocks[0]
            for k in range(1, R):
                total = total + row_permute(blocks[k].astype(bf16), k).astype(f32)
            return total
        half = blocks[0].shape[0] // 2
        b = [(x[:half], x[half:]) for x in blocks]
        top2 = row_permute(b[3][0].astype(bf16), 1)
        low1 = row_permute(b[3][1].astype(bf16), 2)
        top0 = row_permute(b[1][0].astype(bf16), 1)
        low0 = row_permute(b[2][1].astype(bf16), 2)
        top2 = row_permute((b[2][0].astype(f32) + top2.astype(f32)).astype(bf16), 2)
        low1 = row_permute((b[1][1].astype(f32) + low1.astype(f32)).astype(bf16), 1)
        top = b[0][0].astype(f32) + top0.astype(f32) + top2.astype(f32)
        low = b[0][1].astype(f32) + low0.astype(f32) + low1.astype(f32)
        return jnp.concatenate([top, low], axis=0)

    def source_place(s, c):
        return (s % (R // C)) * C + c if C <= R else c

    def source_dest(s, c, k):
        slot = source_place(s, c) ^ k
        if C <= R:
            return slot, s // (R // C)
        q = C // R
        return slot // q, s * q + slot % q

    def exchange_pairs(k):
        pairs = []
        for s in range(R):
            for c in range(C):
                dr, dc = source_dest(s, c, k)
                pairs.append((s * C + c, dr * C + dc))
        return pairs

    def spread(packed):
        return [lax.ppermute(packed[k], (ROW, COL), exchange_pairs(k)) for k in range(N)]

    def bring_back(packed):
        return [
            lax.ppermute(packed[k], (ROW, COL), [(b, a) for a, b in exchange_pairs(k)])
            for k in range(N)
        ]

    def sum_everywhere(array):
        for name in (COL, DP, ROW):
            size = mesh.shape[name]
            step = 1
            while step < size:
                other = lax.ppermute(array, name, [(i, i ^ step) for i in range(size)])
                step *= 2
                array = array + other
        return array

    def pair_sum(mine, other, right):
        away = tn(other, right).astype(bf16)
        got = lax.ppermute(away, COL, [(0, 1), (1, 0)])
        return (tn(mine, right) + got.astype(f32)).astype(bf16)

    def body(
        tokens,
        prefix_len,
        norm1_gain,
        norm1_bias,
        query_key_value_weight,
        query_key_value_bias,
        attention_output_weight,
        norm2_gain,
        norm2_bias,
        gate_up_projection_weight,
        down_projection_weight,
        grad_out,
    ):
        r = lax.axis_index(ROW)
        c = lax.axis_index(COL)
        block = tokens.shape[1]
        width = tokens.shape[2]
        head_cols = query_key_value_weight.shape[2]
        pairs = head_cols // (2 * HD)
        places = (jnp.arange(R)[:, None] ^ r) * block + jnp.arange(block)[None, :]
        table = rotary_tables(places.reshape(-1))
        w_rows, _, ff_local = gate_up_projection_weight.shape
        ff_slice = ff_local // R
        ff = ff_slice * C
        q_rows = max(1, C // R)
        u = source_place(r, c)
        v = r if C <= R else r * q_rows + c % q_rows
        info = jnp.stack([r, prefix_len[0], u, v, c]).astype(jnp.int32)
        rows = w_rows // q_rows
        a_rows = N // C * rows
        piece = (3 * ff_slice + 127) // 128 * 128

        gain1 = norm1_gain.astype(f32)
        gain2 = norm2_gain.astype(f32)
        inputs = tokens[0].astype(f32)
        first, first_std, first_inv = layer_norm_forward(inputs, gain1, norm1_bias.astype(f32))
        seq_in = jnp.concatenate(gather_rel(first.astype(bf16)), axis=0)

        (attn_shard,) = whole_call(
            prepare_kernel,
            info,
            [query_key_value_weight.transpose(1, 0, 2), attention_output_weight],
            [jax.ShapeDtypeStruct((attention_output_weight.shape[0], 4 * head_cols), bf16)],
        )
        w_attn = lax.all_gather(attn_shard, (DP, COL), axis=0, tiled=True)
        (packed,) = whole_call(
            functools.partial(pack_kernel, R, q_rows),
            info,
            [gate_up_projection_weight.transpose(1, 0, 2), down_projection_weight],
            [jax.ShapeDtypeStruct((N, rows, piece), bf16)],
        )
        packed, seq_in = lax.optimization_barrier((packed, seq_in))
        held = pltpu.VMEM((N, rows, piece), bf16)
        gu_shard, down_shard = whole_call(
            functools.partial(unpack_kernel, C),
            info,
            spread(packed),
            [
                jax.ShapeDtypeStruct((a_rows, 2 * ff), bf16),
                jax.ShapeDtypeStruct((a_rows, ff), bf16),
            ],
            [held],
        )
        w_gu = lax.all_gather(gu_shard, (DP, COL), axis=0, tiled=True)
        w_down = lax.all_gather(down_shard, (DP, COL), axis=0, tiled=True)

        w_attn, _ = lax.optimization_barrier((w_attn, gu_shard))
        w_qkv = w_attn[:, : 3 * head_cols]
        w_out = w_attn[:, 3 * head_cols :]
        dy_rel = jnp.concatenate(gather_rel(grad_out[0], gu_shard), axis=0)
        dy = grad_out[0]
        bias = query_key_value_bias.astype(f32).reshape(3, pairs, 2 * HD).transpose(1, 0, 2)
        projected = nn(seq_in, w_qkv)
        projected = projected + bias.reshape(-1)

        qkv, attended, log_sums = attend_forward(info, projected, table, R)
        own = nt(attended[:block], w_out)
        others = nt(attended[block:], w_out).astype(bf16)
        residual = scatter_rel([own] + [others[k * block : (k + 1) * block] for k in range(R - 1)])
        middle = inputs + residual

        second, second_std, second_inv = layer_norm_forward(
            middle, gain2, norm2_bias.astype(f32)
        )
        second_in = jnp.concatenate(gather_rel(second.astype(bf16)), axis=0)
        gate_up = nn(second_in, w_gu)
        gate_vals = gate_up[:, :ff]
        up_vals = gate_up[:, ff:]
        sig = jax.nn.sigmoid(gate_vals)
        swish = gate_vals * sig
        hidden = (swish * up_vals).astype(bf16)
        if C == 2:
            seq_halves = split_columns(info, seq_in, mesh.shape[DP])
            halves = split_columns(info, dy_rel, mesh.shape[DP])
            grad_down = pair_sum(*halves, hidden)
            _, w_down = lax.optimization_barrier((grad_down, w_down))
            grad_down = lax.psum_scatter(grad_down, DP, scatter_dimension=0, tiled=True)
        else:
            grad_down = tn(dy_rel, hidden).astype(bf16)
            _, w_down = lax.optimization_barrier((grad_down, w_down))
            grad_down = lax.psum_scatter(
                grad_down, (DP, COL), scatter_dimension=0, tiled=True
            )
        grad_hidden = nn(dy_rel, w_down)
        grad_gate = grad_hidden * up_vals * sig * (1.0 + gate_vals * (1.0 - sig))
        grad_up = grad_hidden * swish
        grad_gu_vals = jnp.concatenate([grad_gate.astype(bf16), grad_up.astype(bf16)], axis=1)
        if C == 2:
            halves = split_columns(info, second_in, mesh.shape[DP])
            away = tn(halves[1], grad_gu_vals).astype(bf16)
            got = lax.ppermute(away, COL, [(0, 1), (1, 0)])
            second_vals, _ = lax.optimization_barrier((grad_gu_vals, away))
        else:
            second_vals = grad_gu_vals
        own = nt(second_vals[:block], w_gu)
        last = (R - 1) * block
        far = nt(second_vals[last:], w_gu).astype(bf16)
        second_vals, _ = lax.optimization_barrier((second_vals, far))
        others = nt(second_vals[block:last], w_gu).astype(bf16)
        _, grad_gu_vals = lax.optimization_barrier((others, grad_gu_vals))
        grad_second = scatter_rel(
            [own] + [others[k * block : (k + 1) * block] for k in range(R - 2)] + [far]
        )
        if C == 2:
            grad_gu = (tn(halves[0], grad_gu_vals) + got.astype(f32)).astype(bf16)
            grad_gu = lax.psum_scatter(grad_gu, DP, scatter_dimension=0, tiled=True)
        else:
            grad_gu = tn(second_in, grad_gu_vals).astype(bf16)
            grad_gu = lax.psum_scatter(grad_gu, (DP, COL), scatter_dimension=0, tiled=True)

        grad_middle = dy.astype(f32) + layer_norm_backward(
            grad_second, second_std, second_inv, gain2
        )
        gain2_grad = jnp.sum(grad_second * second_std, axis=0)
        bias2_grad = jnp.sum(grad_second, axis=0)

        branch = jnp.concatenate(gather_rel(grad_middle.astype(bf16)), axis=0)
        own = nt(hidden[:block], w_down)
        others = nt(hidden[block:], w_down).astype(bf16)
        others, _ = lax.optimization_barrier((others, branch))
        mixed = scatter_rel(
            [own] + [others[k * block : (k + 1) * block] for k in range(R - 1)]
        )
        layer_out = (middle + mixed).astype(bf16)
        grad_heads = nn(branch, w_out).astype(bf16)
        grad_proj, bias_local = attend_backward(info, qkv, table, log_sums, grad_heads, R)
        bias_local = bias_local[:, 0].reshape(pairs, 3, 2 * HD)
        bias_local = bias_local.transpose(1, 0, 2).reshape(3, head_cols)
        if C == 2:
            outer = tn(branch, attended).astype(bf16).reshape(mesh.shape[DP], C, -1, head_cols)
            away = lax.dynamic_index_in_dim(outer, 1 - c, 1, keepdims=False)
            mine = lax.dynamic_index_in_dim(outer, c, 1, keepdims=False)
            got = lax.ppermute(away.reshape(-1, head_cols), COL, [(0, 1), (1, 0)])
            outer = mine.reshape(-1, head_cols).astype(f32) + got.astype(f32)
            grad_attn = jnp.concatenate(
                [pair_sum(*seq_halves, grad_proj), outer.astype(bf16)], axis=1
            )
            grad_proj, _ = lax.optimization_barrier((grad_proj, grad_attn))
            grad_attn = lax.psum_scatter(grad_attn, DP, scatter_dimension=0, tiled=True)
        else:
            grad_attn = jnp.concatenate(
                [tn(seq_in, grad_proj).astype(bf16), tn(branch, attended).astype(bf16)], axis=1
            )
            grad_attn = lax.psum_scatter(
                grad_attn, (DP, COL), scatter_dimension=0, tiled=True
            )
        own = nt(grad_proj[:block], w_qkv)
        others = nt(grad_proj[block:], w_qkv).astype(bf16)
        grad_first = scatter_rel(
            [own] + [others[k * block : (k + 1) * block] for k in range(R - 1)]
        )
        input_grad = grad_middle + layer_norm_backward(grad_first, first_std, first_inv, gain1)
        gain1_grad = jnp.sum(grad_first * first_std, axis=0)
        bias1_grad = jnp.sum(grad_first, axis=0)

        col_offset = r * head_cols
        bias_full = lax.dynamic_update_slice(
            jnp.zeros((3, width), f32), bias_local, (jnp.int32(0), col_offset)
        )
        sums = jnp.stack([gain1_grad, bias1_grad, gain2_grad, bias2_grad])
        sums = sum_everywhere(jnp.concatenate([sums, bias_full], axis=0))
        grad_bias = lax.dynamic_slice_in_dim(sums[4:], col_offset, head_cols, 1)

        (packed,) = whole_call(
            functools.partial(pack_back_kernel, C),
            info,
            [grad_gu, grad_down],
            [jax.ShapeDtypeStruct((N, rows, piece), bf16)],
        )
        home_gu, home_down = whole_call(
            functools.partial(unpack_back_kernel, R, q_rows),
            info,
            bring_back(packed),
            [
                jax.ShapeDtypeStruct((w_rows, 2, ff_local), f32),
                jax.ShapeDtypeStruct((w_rows, ff_local), f32),
            ],
            [held],
        )
        home_qkv, home_out = whole_call(
            finish_kernel,
            info,
            [grad_attn],
            [
                jax.ShapeDtypeStruct((3, grad_attn.shape[0], head_cols), f32),
                jax.ShapeDtypeStruct((grad_attn.shape[0], head_cols), f32),
            ],
        )
        return (
            layer_out[None],
            input_grad[None],
            sums[0],
            sums[1],
            home_qkv.transpose(1, 0, 2),
            grad_bias,
            home_out,
            sums[2],
            sums[3],
            home_gu,
            home_down,
        )

    return body


def solution(mesh):
    in_specs = (
        P((DP, COL), ROW, None),
        P((DP, COL)),
        P(),
        P(),
        P((DP, COL), None, ROW),
        P(None, ROW),
        P((DP, COL), ROW),
        P(),
        P(),
        P((DP, ROW), None, COL),
        P((DP, ROW), COL),
        P((DP, COL), ROW, None),
    )
    out_specs = (
        P((DP, COL), ROW, None),
        P((DP, COL), ROW, None),
        P(),
        P(),
        P((DP, COL), None, ROW),
        P(None, ROW),
        P((DP, COL), ROW),
        P(),
        P(),
        P((DP, ROW), None, COL),
        P((DP, ROW), COL),
    )
    body = make_body(mesh)

    return jax.shard_map(body, mesh=mesh, in_specs=in_specs, out_specs=out_specs, check_vma=False)
```

```python
import functools
import math

import jax
import jax.numpy as jnp
from jax import lax
from jax.experimental import pallas as pl
from jax.experimental.pallas import tpu as pltpu
from jax.sharding import PartitionSpec as P


HD = 64
ROT = 16

norm_eps = 1e-05
rope_base = 10000.0
masked_fill = -1e30

DP, ROW, COL = "dp", "row", "col"

bf16 = jnp.bfloat16
f32 = jnp.float32


def layer_norm_forward(values, norm_gain, norm_shift):
    centre = jnp.mean(values, axis=-1, keepdims=True)
    centred = values - centre
    variance = jnp.mean(centred * centred, axis=-1, keepdims=True)
    inverse = lax.rsqrt(variance + norm_eps)
    normed = centred * inverse
    return (normed * norm_gain + norm_shift, normed, inverse)


def layer_norm_backward(incoming, normed, inverse, norm_gain):
    scaled = incoming * norm_gain
    inner = jnp.mean(scaled, axis=-1, keepdims=True)
    along = jnp.mean(scaled * normed, axis=-1, keepdims=True)
    return inverse * (scaled - inner - normed * along)


def rotary_tables(places):
    half_rot = ROT // 2
    column = jnp.arange(2 * HD) % HD
    freqs = rope_base ** (-(column % half_rot).astype(f32) * 2.0 / ROT)
    angles = places.astype(f32)[:, None] * freqs[None, :]
    sines = jnp.sin(angles)
    cosine = jnp.where(column < ROT, jnp.cos(angles), 1.0)
    left = jnp.where((column >= half_rot) & (column < ROT), sines, 0.0)
    right = jnp.where(column < half_rot, -sines, 0.0)
    return jnp.stack([cosine, left, right])


def dot(left, right, dims):
    return lax.dot_general(left, right, (dims, ((), ())), preferred_element_type=f32)


def nn(left, right):
    return dot(left, right, ((1,), (0,)))


def nt(left, right):
    return dot(left, right, ((1,), (1,)))


def tn(left, right):
    return dot(left, right, ((0,), (0,)))


def key_blocks(jq, blocks):
    return max(jq + 1, blocks // 2)


def block_mask(qpos, kpos, jq, jk, blocks, prefix):
    if jk < jq:
        return None
    causal = kpos <= qpos
    if jk >= blocks // 2:
        return causal
    early = kpos < prefix
    return (causal | early) if jk == jq else early


def head_lane(head):
    lane = lax.broadcasted_iota(jnp.int32, (1, 2 * HD), 1)
    return (lane < HD) if head == 0 else (lane >= HD)


def forward_kernel(blocks, size, info, proj, table, qkv, out, sums):
    w = 2 * HD
    scale = 1.0 / math.sqrt(HD)
    r, prefix = info[0], info[1]
    for j in range(blocks):
        rows = pl.ds(j * size, size)
        cosine, left, right = table[0, rows], table[1, rows], table[2, rows]
        for part in range(2):
            x = proj[rows, part * w : (part + 1) * w]
            x = x * cosine + pltpu.roll(x, 8, 1) * left + pltpu.roll(x, w - 8, 1) * right
            qkv[rows, part * w : (part + 1) * w] = x.astype(bf16)
        qkv[rows, 2 * w : 3 * w] = proj[rows, 2 * w : 3 * w].astype(bf16)
    places = [pl.ds(pl.multiple_of((j ^ r) * size, size), size) for j in range(blocks)]
    for jq in range(blocks):
        count = key_blocks(jq, blocks)
        q = qkv[places[jq], 0:w].astype(f32) * scale
        qpos = jq * size + lax.broadcasted_iota(jnp.int32, (size, size), 0)
        results = []
        tops = []
        for head in range(2):
            qh = jnp.where(head_lane(head), q, 0.0).astype(bf16)
            scores = []
            for jk in range(count):
                s = nt(qh, qkv[places[jk], w : 2 * w])
                kpos = jk * size + lax.broadcasted_iota(jnp.int32, (size, size), 1)
                mask = block_mask(qpos, kpos, jq, jk, blocks, prefix)
                scores.append(s if mask is None else jnp.where(mask, s, masked_fill))
            top = jnp.max(scores[0], axis=1, keepdims=True)
            for s in scores[1:]:
                top = jnp.maximum(top, jnp.max(s, axis=1, keepdims=True))
            total = 0.0
            result = 0.0
            for jk in range(count):
                e = jnp.exp(scores[jk] - top)
                total = total + jnp.sum(e, axis=1, keepdims=True)
                result = result + nn(e.astype(bf16), qkv[places[jk], 2 * w : 3 * w])
            results.append(result / total)
            tops.append(top + jnp.log(total))
        out[places[jq], :] = jnp.where(head_lane(0), results[0], results[1]).astype(bf16)
        both = jnp.where(head_lane(0), tops[0], tops[1])
        flipped = both.T
        sums[0, jq, 0:8, :] = flipped[0:8]
        sums[0, jq, 8:16, :] = flipped[HD : HD + 8]


def backward_kernel(blocks, size, info, qkv, table, sums, grads, out, bias, qm, km, gm, acc):
    w = 2 * HD
    scale = 1.0 / math.sqrt(HD)
    r, prefix = info[0], info[1]
    for head in range(2):
        lanes = head_lane(head)
        for j in range(blocks):
            rows = pl.ds(j * size, size)
            q = qkv[rows, 0:w].astype(f32) * scale
            k = qkv[rows, w : 2 * w].astype(f32) * scale
            qm[head, rows] = jnp.where(lanes, q, 0.0).astype(bf16)
            km[head, rows] = jnp.where(lanes, k, 0.0).astype(bf16)
            gm[head, rows] = jnp.where(lanes, grads[rows, :].astype(f32), 0.0).astype(bf16)
    acc[...] = jnp.zeros_like(acc)
    places = [pl.ds(pl.multiple_of((j ^ r) * size, size), size) for j in range(blocks)]
    for jq in range(blocks):
        count = key_blocks(jq, blocks)
        rq = places[jq]
        qpos = jq * size + lax.broadcasted_iota(jnp.int32, (size, size), 1)
        grad_q = 0.0
        for head in range(2):
            top = sums[0, jq, 8 * head : 8 * head + 1, :]
            probs = []
            products = []
            inner = 0.0
            for jk in range(count):
                s = nt(qkv[places[jk], w : 2 * w], qm[head, rq])
                p = jnp.exp(s - top)
                kpos = jk * size + lax.broadcasted_iota(jnp.int32, (size, size), 0)
                mask = block_mask(qpos, kpos, jq, jk, blocks, prefix)
                if mask is not None:
                    p = jnp.where(mask, p, 0.0)
                t = p * nt(qkv[places[jk], 2 * w : 3 * w], gm[head, rq])
                inner = inner + jnp.sum(t, axis=0, keepdims=True)
                probs.append(p)
                products.append(t)
            for jk in range(count):
                rk = places[jk]
                d = (products[jk] - probs[jk] * inner).astype(bf16)
                acc[1, rk] += nn(probs[jk].astype(bf16), gm[head, rq])
                acc[0, rk] += nn(d, qm[head, rq])
                grad_q = grad_q + tn(d, km[head, rk])
        cosine, left, right = table[0, rq], table[1, rq], table[2, rq]
        x = grad_q
        x = x * cosine - pltpu.roll(x, 8, 1) * left - pltpu.roll(x, w - 8, 1) * right
        out[rq, 0:w] = x.astype(bf16)
    bias_q = 0.0
    bias_k = 0.0
    bias_v = 0.0
    for j in range(blocks):
        rows = pl.ds(j * size, size)
        x = acc[0, rows]
        x = x * table[0, rows]
        x = x - pltpu.roll(acc[0, rows], 8, 1) * table[1, rows]
        x = x - pltpu.roll(acc[0, rows], w - 8, 1) * table[2, rows]
        x = x.astype(bf16)
        y = acc[1, rows].astype(bf16)
        out[rows, w : 2 * w] = x
        out[rows, 2 * w : 3 * w] = y
        bias_q = bias_q + jnp.sum(out[rows, 0:w].astype(f32), axis=0, keepdims=True)
        bias_k = bias_k + jnp.sum(x.astype(f32), axis=0, keepdims=True)
        bias_v = bias_v + jnp.sum(y.astype(f32), axis=0, keepdims=True)
    row = jnp.concatenate([bias_q, bias_k, bias_v], axis=1)
    bias[0] = jnp.broadcast_to(row, (8, 3 * w))


def attend_forward(info, projected, table, blocks):
    length = projected.shape[0]
    w = 2 * HD
    pairs = projected.shape[1] // (3 * w)
    size = length // blocks
    spec = pltpu.PrefetchScalarGridSpec(
        num_scalar_prefetch=1,
        grid=(pairs,),
        in_specs=[
            pl.BlockSpec((length, 3 * w), lambda p, i: (0, p)),
            pl.BlockSpec((3, length, w), lambda p, i: (0, 0, 0)),
        ],
        out_specs=[
            pl.BlockSpec((length, 3 * w), lambda p, i: (0, p)),
            pl.BlockSpec((length, w), lambda p, i: (0, p)),
            pl.BlockSpec((1, blocks, 16, size), lambda p, i: (p, 0, 0, 0)),
        ],
    )
    return pl.pallas_call(
        lambda *refs: forward_kernel(blocks, size, *refs),
        grid_spec=spec,
        out_shape=[
            jax.ShapeDtypeStruct((length, 3 * w * pairs), bf16),
            jax.ShapeDtypeStruct((length, w * pairs), bf16),
            jax.ShapeDtypeStruct((pairs, blocks, 16, size), f32),
        ],
        name="attn_f",
        compiler_params=pltpu.CompilerParams(vmem_limit_bytes=48 << 20),
    )(info, projected, table)


def attend_backward(info, qkv, table, sums, grads, blocks):
    length = qkv.shape[0]
    w = 2 * HD
    pairs = qkv.shape[1] // (3 * w)
    size = length // blocks
    spec = pltpu.PrefetchScalarGridSpec(
        num_scalar_prefetch=1,
        grid=(pairs,),
        in_specs=[
            pl.BlockSpec((length, 3 * w), lambda p, i: (0, p)),
            pl.BlockSpec((3, length, w), lambda p, i: (0, 0, 0)),
            pl.BlockSpec((1, blocks, 16, size), lambda p, i: (p, 0, 0, 0)),
            pl.BlockSpec((length, w), lambda p, i: (0, p)),
        ],
        out_specs=[
            pl.BlockSpec((length, 3 * w), lambda p, i: (0, p)),
            pl.BlockSpec((1, 8, 3 * w), lambda p, i: (p, 0, 0)),
        ],
        scratch_shapes=[
            pltpu.VMEM((2, length, w), bf16),
            pltpu.VMEM((2, length, w), bf16),
            pltpu.VMEM((2, length, w), bf16),
            pltpu.VMEM((2, length, w), f32),
        ],
    )
    return pl.pallas_call(
        lambda *refs: backward_kernel(blocks, size, *refs),
        grid_spec=spec,
        out_shape=[
            jax.ShapeDtypeStruct((length, 3 * w * pairs), bf16),
            jax.ShapeDtypeStruct((pairs, 8, 3 * w), f32),
        ],
        name="attn_b",
        compiler_params=pltpu.CompilerParams(vmem_limit_bytes=48 << 20),
    )(info, qkv, table, sums, grads)


def pack_kernel(R, q, info, gate_up, down, out):
    fs = down.shape[1] // R
    rows = down.shape[0] // q
    for slot in range(R * q):
        span = pl.ds((slot % q) * rows, rows)
        lo = (slot // q) * fs
        k = slot ^ info[2]
        out[k, :, 0:fs] = gate_up[0, span, lo : lo + fs]
        out[k, :, fs : 2 * fs] = gate_up[1, span, lo : lo + fs]
        out[k, :, 2 * fs : 3 * fs] = down[span, lo : lo + fs]


def unpack_kernel(C, info, *refs):
    pieces, (gate_up, down, held) = refs[:-3], refs[-3:]
    rows = held.shape[1]
    ff = down.shape[1]
    fs = ff // C
    for k, piece in enumerate(pieces):
        held[k ^ info[3]] = piece[...]
    for place in range(len(pieces)):
        span = pl.ds((place // C) * rows, rows)
        lo = (place % C) * fs
        gate_up[span, lo : lo + fs] = held[place, :, 0:fs]
        gate_up[span, ff + lo : ff + lo + fs] = held[place, :, fs : 2 * fs]
        down[span, lo : lo + fs] = held[place, :, 2 * fs : 3 * fs]


def pack_back_kernel(C, info, gate_up, down, out):
    rows = out.shape[1]
    ff = down.shape[1]
    fs = ff // C
    for place in range(out.shape[0]):
        span = pl.ds((place // C) * rows, rows)
        lo = (place % C) * fs
        k = place ^ info[3]
        out[k, :, 0:fs] = gate_up[span, lo : lo + fs]
        out[k, :, fs : 2 * fs] = gate_up[span, ff + lo : ff + lo + fs]
        out[k, :, 2 * fs : 3 * fs] = down[span, lo : lo + fs]


def unpack_back_kernel(R, q, info, *refs):
    pieces, (gate_up, down, held) = refs[:-3], refs[-3:]
    rows = held.shape[1]
    fs = down.shape[1] // R
    for k, piece in enumerate(pieces):
        held[k ^ info[2]] = piece[...]
    for slot in range(len(pieces)):
        span = pl.ds((slot % q) * rows, rows)
        lo = (slot // q) * fs
        gate_up[span, 0, lo : lo + fs] = held[slot, :, 0:fs].astype(f32)
        gate_up[span, 1, lo : lo + fs] = held[slot, :, fs : 2 * fs].astype(f32)
        down[span, lo : lo + fs] = held[slot, :, 2 * fs : 3 * fs].astype(f32)


def prepare_kernel(info, qkv, outer, out):
    w = 2 * HD
    cols = outer.shape[1]
    for pair in range(cols // w):
        for part in range(3):
            lo = (3 * pair + part) * w
            out[:, lo : lo + w] = qkv[part, :, pair * w : (pair + 1) * w]
    out[:, 3 * cols :] = outer[...]


def finish_kernel(info, grads, part_out, qkv, outer):
    w = 2 * HD
    cols = outer.shape[1]
    for pair in range(cols // w):
        for part in range(3):
            lo = (3 * pair + part) * w
            qkv[part, :, pair * w : (pair + 1) * w] = grads[:, lo : lo + w].astype(f32)
    outer[...] = part_out[...].astype(f32)


def whole_call(kernel, info, arrays, shapes, scratch=()):
    def spec(shape):
        return pl.BlockSpec(shape, lambda i, s: (0,) * len(shape))

    return pl.pallas_call(
        kernel,
        grid_spec=pltpu.PrefetchScalarGridSpec(
            num_scalar_prefetch=1,
            grid=(1,),
            in_specs=[spec(a.shape) for a in arrays],
            out_specs=[spec(a.shape) for a in shapes],
            scratch_shapes=list(scratch),
        ),
        out_shape=shapes,
        compiler_params=pltpu.CompilerParams(vmem_limit_bytes=48 << 20),
    )(info, *arrays)


def split_kernel(info, mine, other, mine_out, other_out):
    mine_out[...] = mine[...]
    other_out[...] = other[...]


def split_columns(info, array, parts):
    length, width = array.shape
    block = width // (2 * parts)
    shape = jax.ShapeDtypeStruct((length, width // 2), array.dtype)
    return pl.pallas_call(
        split_kernel,
        grid_spec=pltpu.PrefetchScalarGridSpec(
            num_scalar_prefetch=1,
            grid=(parts,),
            in_specs=[
                pl.BlockSpec((length, block), lambda j, s: (0, 2 * j + s[4])),
                pl.BlockSpec((length, block), lambda j, s: (0, 2 * j + 1 - s[4])),
            ],
            out_specs=[pl.BlockSpec((length, block), lambda j, s: (0, j))] * 2,
        ),
        out_shape=[shape, shape],
    )(info, array, array)


def make_body(mesh):
    R = mesh.shape[ROW]
    C = mesh.shape[COL]
    N = max(R, C)

    def row_permute(block, k):
        return lax.ppermute(block, ROW, [(i, i ^ k) for i in range(R)])

    def gather_rel(block, after=None):
        if R != 4:
            return [block] + [row_permute(block, k) for k in range(1, R)]
        half = block.shape[0] // 2
        if after is not None:
            block, _ = lax.optimization_barrier((block, after))
        one = row_permute(block, 1)
        two = row_permute(block, 2)
        top = row_permute(one[:half], 2)
        low = row_permute(two[half:], 1)
        return [block, one, two, jnp.concatenate([top, low], axis=0)]

    def scatter_rel(blocks):
        if R != 4:
            total = blocks[0]
            for k in range(1, R):
                total = total + row_permute(blocks[k].astype(bf16), k).astype(f32)
            return total
        half = blocks[0].shape[0] // 2
        b = [(x[:half], x[half:]) for x in blocks]
        top2 = row_permute(b[3][0].astype(bf16), 1)
        low1 = row_permute(b[3][1].astype(bf16), 2)
        top0 = row_permute(b[1][0].astype(bf16), 1)
        low0 = row_permute(b[2][1].astype(bf16), 2)
        top2 = row_permute((b[2][0].astype(f32) + top2.astype(f32)).astype(bf16), 2)
        low1 = row_permute((b[1][1].astype(f32) + low1.astype(f32)).astype(bf16), 1)
        top = b[0][0].astype(f32) + top0.astype(f32) + top2.astype(f32)
        low = b[0][1].astype(f32) + low0.astype(f32) + low1.astype(f32)
        return jnp.concatenate([top, low], axis=0)

    def source_place(s, c):
        return (s % (R // C)) * C + c if C <= R else c

    def source_dest(s, c, k):
        slot = source_place(s, c) ^ k
        if C <= R:
            return slot, s // (R // C)
        q = C // R
        return slot // q, s * q + slot % q

    def exchange_pairs(k):
        pairs = []
        for s in range(R):
            for c in range(C):
                dr, dc = source_dest(s, c, k)
                pairs.append((s * C + c, dr * C + dc))
        return pairs

    def spread(packed):
        return [lax.ppermute(packed[k], (ROW, COL), exchange_pairs(k)) for k in range(N)]

    def bring_back(packed):
        return [
            lax.ppermute(packed[k], (ROW, COL), [(b, a) for a, b in exchange_pairs(k)])
            for k in range(N)
        ]

    def sum_everywhere(array):
        for name in (COL, DP, ROW):
            size = mesh.shape[name]
            step = 1
            while step < size:
                other = lax.ppermute(array, name, [(i, i ^ step) for i in range(size)])
                step *= 2
                array = array + other
        return array

    def pair_sum(mine, other, right):
        away = tn(other, right).astype(bf16)
        got = lax.ppermute(away, COL, [(0, 1), (1, 0)])
        return (tn(mine, right) + got.astype(f32)).astype(bf16)

    def body(
        tokens,
        prefix_len,
        norm1_gain,
        norm1_bias,
        query_key_value_weight,
        query_key_value_bias,
        attention_output_weight,
        norm2_gain,
        norm2_bias,
        gate_up_projection_weight,
        down_projection_weight,
        grad_out,
    ):
        r = lax.axis_index(ROW)
        c = lax.axis_index(COL)
        block = tokens.shape[1]
        width = tokens.shape[2]
        head_cols = query_key_value_weight.shape[2]
        pairs = head_cols // (2 * HD)
        places = (jnp.arange(R)[:, None] ^ r) * block + jnp.arange(block)[None, :]
        table = rotary_tables(places.reshape(-1))
        w_rows, _, ff_local = gate_up_projection_weight.shape
        ff_slice = ff_local // R
        ff = ff_slice * C
        q_rows = max(1, C // R)
        u = source_place(r, c)
        v = r if C <= R else r * q_rows + c % q_rows
        info = jnp.stack([r, prefix_len[0], u, v, c]).astype(jnp.int32)
        rows = w_rows // q_rows
        a_rows = N // C * rows
        piece = (3 * ff_slice + 127) // 128 * 128

        gain1 = norm1_gain.astype(f32)
        gain2 = norm2_gain.astype(f32)
        inputs = tokens[0].astype(f32)
        first, first_std, first_inv = layer_norm_forward(inputs, gain1, norm1_bias.astype(f32))
        seq_in = jnp.concatenate(gather_rel(first.astype(bf16)), axis=0)

        (attn_shard,) = whole_call(
            prepare_kernel,
            info,
            [query_key_value_weight.transpose(1, 0, 2), attention_output_weight],
            [jax.ShapeDtypeStruct((attention_output_weight.shape[0], 4 * head_cols), bf16)],
        )
        w_attn = lax.all_gather(attn_shard, (DP, COL), axis=0, tiled=True)
        (packed,) = whole_call(
            functools.partial(pack_kernel, R, q_rows),
            info,
            [gate_up_projection_weight.transpose(1, 0, 2), down_projection_weight],
            [jax.ShapeDtypeStruct((N, rows, piece), bf16)],
        )
        packed, seq_in = lax.optimization_barrier((packed, seq_in))
        held = pltpu.VMEM((N, rows, piece), bf16)
        gu_shard, down_shard = whole_call(
            functools.partial(unpack_kernel, C),
            info,
            spread(packed),
            [
                jax.ShapeDtypeStruct((a_rows, 2 * ff), bf16),
                jax.ShapeDtypeStruct((a_rows, ff), bf16),
            ],
            [held],
        )
        w_gu = lax.all_gather(gu_shard, (DP, COL), axis=0, tiled=True)
        w_down = lax.all_gather(down_shard, (DP, COL), axis=0, tiled=True)

        w_attn, _ = lax.optimization_barrier((w_attn, gu_shard))
        w_qkv = w_attn[:, : 3 * head_cols]
        w_out = w_attn[:, 3 * head_cols :]
        dy_rel = jnp.concatenate(gather_rel(grad_out[0], gu_shard), axis=0)
        dy = grad_out[0]
        bias = query_key_value_bias.astype(f32).reshape(3, pairs, 2 * HD).transpose(1, 0, 2)
        projected = nn(seq_in, w_qkv)
        projected = projected + bias.reshape(-1)

        qkv, attended, log_sums = attend_forward(info, projected, table, R)
        own = nt(attended[:block], w_out)
        others = nt(attended[block:], w_out).astype(bf16)
        residual = scatter_rel([own] + [others[k * block : (k + 1) * block] for k in range(R - 1)])
        middle = inputs + residual

        second, second_std, second_inv = layer_norm_forward(
            middle, gain2, norm2_bias.astype(f32)
        )
        second_in = jnp.concatenate(gather_rel(second.astype(bf16)), axis=0)
        gate_up = nn(second_in, w_gu)
        gate_vals = gate_up[:, :ff]
        up_vals = gate_up[:, ff:]
        sig = jax.nn.sigmoid(gate_vals)
        swish = gate_vals * sig
        hidden = (swish * up_vals).astype(bf16)
        if C == 2:
            seq_halves = split_columns(info, seq_in, mesh.shape[DP])
            halves = split_columns(info, dy_rel, mesh.shape[DP])
            grad_down = pair_sum(*halves, hidden)
            _, w_down = lax.optimization_barrier((grad_down, w_down))
            grad_down = lax.psum_scatter(grad_down, DP, scatter_dimension=0, tiled=True)
        else:
            grad_down = tn(dy_rel, hidden).astype(bf16)
            _, w_down = lax.optimization_barrier((grad_down, w_down))
            grad_down = lax.psum_scatter(
                grad_down, (DP, COL), scatter_dimension=0, tiled=True
            )
        grad_hidden = nn(dy_rel, w_down)
        grad_gate = grad_hidden * up_vals * sig * (1.0 + gate_vals * (1.0 - sig))
        grad_up = grad_hidden * swish
        grad_gu_vals = jnp.concatenate([grad_gate.astype(bf16), grad_up.astype(bf16)], axis=1)
        if C == 2:
            halves = split_columns(info, second_in, mesh.shape[DP])
            away = tn(halves[1], grad_gu_vals).astype(bf16)
            got = lax.ppermute(away, COL, [(0, 1), (1, 0)])
            second_vals, _ = lax.optimization_barrier((grad_gu_vals, away))
        else:
            second_vals = grad_gu_vals
        own = nt(second_vals[:block], w_gu)
        last = (R - 1) * block
        far = nt(second_vals[last:], w_gu).astype(bf16)
        second_vals, _ = lax.optimization_barrier((second_vals, far))
        others = nt(second_vals[block:last], w_gu).astype(bf16)
        _, grad_gu_vals = lax.optimization_barrier((others, grad_gu_vals))
        grad_second = scatter_rel(
            [own] + [others[k * block : (k + 1) * block] for k in range(R - 2)] + [far]
        )
        if C == 2:
            grad_gu = (tn(halves[0], grad_gu_vals) + got.astype(f32)).astype(bf16)
            grad_gu = lax.psum_scatter(grad_gu, DP, scatter_dimension=0, tiled=True)
        else:
            grad_gu = tn(second_in, grad_gu_vals).astype(bf16)
            grad_gu = lax.psum_scatter(grad_gu, (DP, COL), scatter_dimension=0, tiled=True)

        grad_middle = dy.astype(f32) + layer_norm_backward(
            grad_second, second_std, second_inv, gain2
        )
        gain2_grad = jnp.sum(grad_second * second_std, axis=0)
        bias2_grad = jnp.sum(grad_second, axis=0)

        branch = jnp.concatenate(gather_rel(grad_middle.astype(bf16)), axis=0)
        own = nt(hidden[:block], w_down)
        others = nt(hidden[block:], w_down).astype(bf16)
        others, _ = lax.optimization_barrier((others, branch))
        mixed = scatter_rel(
            [own] + [others[k * block : (k + 1) * block] for k in range(R - 1)]
        )
        layer_out = (middle + mixed).astype(bf16)
        grad_heads = nn(branch, w_out).astype(bf16)
        grad_proj, bias_local = attend_backward(info, qkv, table, log_sums, grad_heads, R)
        bias_local = bias_local[:, 0].reshape(pairs, 3, 2 * HD)
        bias_local = bias_local.transpose(1, 0, 2).reshape(3, head_cols)
        if C == 2:
            outer = tn(branch, attended).astype(bf16).reshape(mesh.shape[DP], C, -1, head_cols)
            away = lax.dynamic_index_in_dim(outer, 1 - c, 1, keepdims=False)
            mine = lax.dynamic_index_in_dim(outer, c, 1, keepdims=False)
            got = lax.ppermute(away.reshape(-1, head_cols), COL, [(0, 1), (1, 0)])
            outer = mine.reshape(-1, head_cols).astype(f32) + got.astype(f32)
            outer = outer.astype(bf16)
            grad_attn = pair_sum(*seq_halves, grad_proj)
            grad_proj, _ = lax.optimization_barrier((grad_proj, grad_attn))
            grad_outer = lax.psum_scatter(outer, DP, scatter_dimension=0, tiled=True)
            grad_attn = lax.psum_scatter(grad_attn, DP, scatter_dimension=0, tiled=True)
        else:
            outer = tn(branch, attended).astype(bf16)
            grad_attn = tn(seq_in, grad_proj).astype(bf16)
            grad_outer = lax.psum_scatter(outer, (DP, COL), scatter_dimension=0, tiled=True)
            grad_attn = lax.psum_scatter(grad_attn, (DP, COL), scatter_dimension=0, tiled=True)
        own = nt(grad_proj[:block], w_qkv)
        others = nt(grad_proj[block:], w_qkv).astype(bf16)
        grad_first = scatter_rel(
            [own] + [others[k * block : (k + 1) * block] for k in range(R - 1)]
        )
        input_grad = grad_middle + layer_norm_backward(grad_first, first_std, first_inv, gain1)
        gain1_grad = jnp.sum(grad_first * first_std, axis=0)
        bias1_grad = jnp.sum(grad_first, axis=0)

        col_offset = r * head_cols
        bias_full = lax.dynamic_update_slice(
            jnp.zeros((3, width), f32), bias_local, (jnp.int32(0), col_offset)
        )
        sums = jnp.stack([gain1_grad, bias1_grad, gain2_grad, bias2_grad])
        sums = sum_everywhere(jnp.concatenate([sums, bias_full], axis=0))
        grad_bias = lax.dynamic_slice_in_dim(sums[4:], col_offset, head_cols, 1)

        (packed,) = whole_call(
            functools.partial(pack_back_kernel, C),
            info,
            [grad_gu, grad_down],
            [jax.ShapeDtypeStruct((N, rows, piece), bf16)],
        )
        home_gu, home_down = whole_call(
            functools.partial(unpack_back_kernel, R, q_rows),
            info,
            bring_back(packed),
            [
                jax.ShapeDtypeStruct((w_rows, 2, ff_local), f32),
                jax.ShapeDtypeStruct((w_rows, ff_local), f32),
            ],
            [held],
        )
        home_qkv, home_out = whole_call(
            finish_kernel,
            info,
            [grad_attn, grad_outer],
            [
                jax.ShapeDtypeStruct((3, grad_attn.shape[0], head_cols), f32),
                jax.ShapeDtypeStruct((grad_attn.shape[0], head_cols), f32),
            ],
        )
        return (
            layer_out[None],
            input_grad[None],
            sums[0],
            sums[1],
            home_qkv.transpose(1, 0, 2),
            grad_bias,
            home_out,
            sums[2],
            sums[3],
            home_gu,
            home_down,
        )

    return body


def solution(mesh):
    in_specs = (
        P((DP, COL), ROW, None),
        P((DP, COL)),
        P(),
        P(),
        P((DP, COL), None, ROW),
        P(None, ROW),
        P((DP, COL), ROW),
        P(),
        P(),
        P((DP, ROW), None, COL),
        P((DP, ROW), COL),
        P((DP, COL), ROW, None),
    )
    out_specs = (
        P((DP, COL), ROW, None),
        P((DP, COL), ROW, None),
        P(),
        P(),
        P((DP, COL), None, ROW),
        P(None, ROW),
        P((DP, COL), ROW),
        P(),
        P(),
        P((DP, ROW), None, COL),
        P((DP, ROW), COL),
    )
    body = make_body(mesh)

    return jax.shard_map(body, mesh=mesh, in_specs=in_specs, out_specs=out_specs, check_vma=False)
```

```python
import functools
import math

import jax
import jax.numpy as jnp
from jax import lax
from jax.experimental import pallas as pl
from jax.experimental.pallas import tpu as pltpu
from jax.sharding import PartitionSpec as P


HD = 64
ROT = 16

norm_eps = 1e-05
rope_base = 10000.0
masked_fill = -1e30

DP, ROW, COL = "dp", "row", "col"

bf16 = jnp.bfloat16
f32 = jnp.float32


def layer_norm_forward(values, norm_gain, norm_shift):
    centre = jnp.mean(values, axis=-1, keepdims=True)
    centred = values - centre
    variance = jnp.mean(centred * centred, axis=-1, keepdims=True)
    inverse = lax.rsqrt(variance + norm_eps)
    normed = centred * inverse
    return (normed * norm_gain + norm_shift, normed, inverse)


def layer_norm_backward(incoming, normed, inverse, norm_gain):
    scaled = incoming * norm_gain
    inner = jnp.mean(scaled, axis=-1, keepdims=True)
    along = jnp.mean(scaled * normed, axis=-1, keepdims=True)
    return inverse * (scaled - inner - normed * along)


def rotary_tables(places):
    half_rot = ROT // 2
    column = jnp.arange(2 * HD) % HD
    freqs = rope_base ** (-(column % half_rot).astype(f32) * 2.0 / ROT)
    angles = places.astype(f32)[:, None] * freqs[None, :]
    sines = jnp.sin(angles)
    cosine = jnp.where(column < ROT, jnp.cos(angles), 1.0)
    left = jnp.where((column >= half_rot) & (column < ROT), sines, 0.0)
    right = jnp.where(column < half_rot, -sines, 0.0)
    return jnp.stack([cosine, left, right])


def dot(left, right, dims):
    return lax.dot_general(left, right, (dims, ((), ())), preferred_element_type=f32)


def nn(left, right):
    return dot(left, right, ((1,), (0,)))


def nt(left, right):
    return dot(left, right, ((1,), (1,)))


def tn(left, right):
    return dot(left, right, ((0,), (0,)))


def key_blocks(jq, blocks):
    return max(jq + 1, blocks // 2)


def block_mask(qpos, kpos, jq, jk, blocks, prefix):
    if jk < jq:
        return None
    causal = kpos <= qpos
    if jk >= blocks // 2:
        return causal
    early = kpos < prefix
    return (causal | early) if jk == jq else early


def head_lane(head):
    lane = lax.broadcasted_iota(jnp.int32, (1, 2 * HD), 1)
    return (lane < HD) if head == 0 else (lane >= HD)


def forward_kernel(blocks, size, info, proj, table, qkv, out, sums):
    w = 2 * HD
    scale = 1.0 / math.sqrt(HD)
    r, prefix = info[0], info[1]
    for j in range(blocks):
        rows = pl.ds(j * size, size)
        cosine, left, right = table[0, rows], table[1, rows], table[2, rows]
        for part in range(2):
            x = proj[rows, part * w : (part + 1) * w]
            x = x * cosine + pltpu.roll(x, 8, 1) * left + pltpu.roll(x, w - 8, 1) * right
            qkv[rows, part * w : (part + 1) * w] = x.astype(bf16)
        qkv[rows, 2 * w : 3 * w] = proj[rows, 2 * w : 3 * w].astype(bf16)
    places = [pl.ds(pl.multiple_of((j ^ r) * size, size), size) for j in range(blocks)]
    for jq in range(blocks):
        count = key_blocks(jq, blocks)
        q = qkv[places[jq], 0:w].astype(f32) * scale
        qpos = jq * size + lax.broadcasted_iota(jnp.int32, (size, size), 0)
        results = []
        tops = []
        for head in range(2):
            qh = jnp.where(head_lane(head), q, 0.0).astype(bf16)
            scores = []
            for jk in range(count):
                s = nt(qh, qkv[places[jk], w : 2 * w])
                kpos = jk * size + lax.broadcasted_iota(jnp.int32, (size, size), 1)
                mask = block_mask(qpos, kpos, jq, jk, blocks, prefix)
                scores.append(s if mask is None else jnp.where(mask, s, masked_fill))
            top = jnp.max(scores[0], axis=1, keepdims=True)
            for s in scores[1:]:
                top = jnp.maximum(top, jnp.max(s, axis=1, keepdims=True))
            total = 0.0
            result = 0.0
            for jk in range(count):
                e = jnp.exp(scores[jk] - top)
                total = total + jnp.sum(e, axis=1, keepdims=True)
                result = result + nn(e.astype(bf16), qkv[places[jk], 2 * w : 3 * w])
            results.append(result / total)
            tops.append(top + jnp.log(total))
        out[places[jq], :] = jnp.where(head_lane(0), results[0], results[1]).astype(bf16)
        both = jnp.where(head_lane(0), tops[0], tops[1])
        flipped = both.T
        sums[0, jq, 0:8, :] = flipped[0:8]
        sums[0, jq, 8:16, :] = flipped[HD : HD + 8]


def backward_kernel(blocks, size, info, qkv, table, sums, grads, out, bias, qm, km, gm, acc):
    w = 2 * HD
    scale = 1.0 / math.sqrt(HD)
    r, prefix = info[0], info[1]
    for head in range(2):
        lanes = head_lane(head)
        for j in range(blocks):
            rows = pl.ds(j * size, size)
            q = qkv[rows, 0:w].astype(f32) * scale
            k = qkv[rows, w : 2 * w].astype(f32) * scale
            qm[head, rows] = jnp.where(lanes, q, 0.0).astype(bf16)
            km[head, rows] = jnp.where(lanes, k, 0.0).astype(bf16)
            gm[head, rows] = jnp.where(lanes, grads[rows, :].astype(f32), 0.0).astype(bf16)
    acc[...] = jnp.zeros_like(acc)
    places = [pl.ds(pl.multiple_of((j ^ r) * size, size), size) for j in range(blocks)]
    for jq in range(blocks):
        count = key_blocks(jq, blocks)
        rq = places[jq]
        qpos = jq * size + lax.broadcasted_iota(jnp.int32, (size, size), 1)
        grad_q = 0.0
        for head in range(2):
            top = sums[0, jq, 8 * head : 8 * head + 1, :]
            probs = []
            products = []
            inner = 0.0
            for jk in range(count):
                s = nt(qkv[places[jk], w : 2 * w], qm[head, rq])
                p = jnp.exp(s - top)
                kpos = jk * size + lax.broadcasted_iota(jnp.int32, (size, size), 0)
                mask = block_mask(qpos, kpos, jq, jk, blocks, prefix)
                if mask is not None:
                    p = jnp.where(mask, p, 0.0)
                t = p * nt(qkv[places[jk], 2 * w : 3 * w], gm[head, rq])
                inner = inner + jnp.sum(t, axis=0, keepdims=True)
                probs.append(p)
                products.append(t)
            for jk in range(count):
                rk = places[jk]
                d = (products[jk] - probs[jk] * inner).astype(bf16)
                acc[1, rk] += nn(probs[jk].astype(bf16), gm[head, rq])
                acc[0, rk] += nn(d, qm[head, rq])
                grad_q = grad_q + tn(d, km[head, rk])
        cosine, left, right = table[0, rq], table[1, rq], table[2, rq]
        x = grad_q
        x = x * cosine - pltpu.roll(x, 8, 1) * left - pltpu.roll(x, w - 8, 1) * right
        out[rq, 0:w] = x.astype(bf16)
    bias_q = 0.0
    bias_k = 0.0
    bias_v = 0.0
    for j in range(blocks):
        rows = pl.ds(j * size, size)
        x = acc[0, rows]
        x = x * table[0, rows]
        x = x - pltpu.roll(acc[0, rows], 8, 1) * table[1, rows]
        x = x - pltpu.roll(acc[0, rows], w - 8, 1) * table[2, rows]
        x = x.astype(bf16)
        y = acc[1, rows].astype(bf16)
        out[rows, w : 2 * w] = x
        out[rows, 2 * w : 3 * w] = y
        bias_q = bias_q + jnp.sum(out[rows, 0:w].astype(f32), axis=0, keepdims=True)
        bias_k = bias_k + jnp.sum(x.astype(f32), axis=0, keepdims=True)
        bias_v = bias_v + jnp.sum(y.astype(f32), axis=0, keepdims=True)
    row = jnp.concatenate([bias_q, bias_k, bias_v], axis=1)
    bias[0] = jnp.broadcast_to(row, (8, 3 * w))


def attend_forward(info, projected, table, blocks):
    length = projected.shape[0]
    w = 2 * HD
    pairs = projected.shape[1] // (3 * w)
    size = length // blocks
    spec = pltpu.PrefetchScalarGridSpec(
        num_scalar_prefetch=1,
        grid=(pairs,),
        in_specs=[
            pl.BlockSpec((length, 3 * w), lambda p, i: (0, p)),
            pl.BlockSpec((3, length, w), lambda p, i: (0, 0, 0)),
        ],
        out_specs=[
            pl.BlockSpec((length, 3 * w), lambda p, i: (0, p)),
            pl.BlockSpec((length, w), lambda p, i: (0, p)),
            pl.BlockSpec((1, blocks, 16, size), lambda p, i: (p, 0, 0, 0)),
        ],
    )
    return pl.pallas_call(
        lambda *refs: forward_kernel(blocks, size, *refs),
        grid_spec=spec,
        out_shape=[
            jax.ShapeDtypeStruct((length, 3 * w * pairs), bf16),
            jax.ShapeDtypeStruct((length, w * pairs), bf16),
            jax.ShapeDtypeStruct((pairs, blocks, 16, size), f32),
        ],
        name="attn_f",
        compiler_params=pltpu.CompilerParams(vmem_limit_bytes=48 << 20),
    )(info, projected, table)


def attend_backward(info, qkv, table, sums, grads, blocks):
    length = qkv.shape[0]
    w = 2 * HD
    pairs = qkv.shape[1] // (3 * w)
    size = length // blocks
    spec = pltpu.PrefetchScalarGridSpec(
        num_scalar_prefetch=1,
        grid=(pairs,),
        in_specs=[
            pl.BlockSpec((length, 3 * w), lambda p, i: (0, p)),
            pl.BlockSpec((3, length, w), lambda p, i: (0, 0, 0)),
            pl.BlockSpec((1, blocks, 16, size), lambda p, i: (p, 0, 0, 0)),
            pl.BlockSpec((length, w), lambda p, i: (0, p)),
        ],
        out_specs=[
            pl.BlockSpec((length, 3 * w), lambda p, i: (0, p)),
            pl.BlockSpec((1, 8, 3 * w), lambda p, i: (p, 0, 0)),
        ],
        scratch_shapes=[
            pltpu.VMEM((2, length, w), bf16),
            pltpu.VMEM((2, length, w), bf16),
            pltpu.VMEM((2, length, w), bf16),
            pltpu.VMEM((2, length, w), f32),
        ],
    )
    return pl.pallas_call(
        lambda *refs: backward_kernel(blocks, size, *refs),
        grid_spec=spec,
        out_shape=[
            jax.ShapeDtypeStruct((length, 3 * w * pairs), bf16),
            jax.ShapeDtypeStruct((pairs, 8, 3 * w), f32),
        ],
        name="attn_b",
        compiler_params=pltpu.CompilerParams(vmem_limit_bytes=48 << 20),
    )(info, qkv, table, sums, grads)


def pack_kernel(R, q, info, gate_up, down, out):
    fs = down.shape[1] // R
    rows = down.shape[0] // q
    for slot in range(R * q):
        span = pl.ds((slot % q) * rows, rows)
        lo = (slot // q) * fs
        k = slot ^ info[2]
        out[k, :, 0:fs] = gate_up[0, span, lo : lo + fs]
        out[k, :, fs : 2 * fs] = gate_up[1, span, lo : lo + fs]
        out[k, :, 2 * fs : 3 * fs] = down[span, lo : lo + fs]


def unpack_kernel(C, info, *refs):
    pieces, (gate_up, down, held) = refs[:-3], refs[-3:]
    rows = held.shape[1]
    ff = down.shape[1]
    fs = ff // C
    for k, piece in enumerate(pieces):
        held[k ^ info[3]] = piece[...]
    for place in range(len(pieces)):
        span = pl.ds((place // C) * rows, rows)
        lo = (place % C) * fs
        gate_up[span, lo : lo + fs] = held[place, :, 0:fs]
        gate_up[span, ff + lo : ff + lo + fs] = held[place, :, fs : 2 * fs]
        down[span, lo : lo + fs] = held[place, :, 2 * fs : 3 * fs]


def pack_back_kernel(C, info, gate_up, down, out):
    rows = out.shape[1]
    ff = down.shape[1]
    fs = ff // C
    for place in range(out.shape[0]):
        span = pl.ds((place // C) * rows, rows)
        lo = (place % C) * fs
        k = place ^ info[3]
        out[k, :, 0:fs] = gate_up[span, lo : lo + fs]
        out[k, :, fs : 2 * fs] = gate_up[span, ff + lo : ff + lo + fs]
        out[k, :, 2 * fs : 3 * fs] = down[span, lo : lo + fs]


def unpack_back_kernel(R, q, info, *refs):
    pieces, (gate_up, down, held) = refs[:-3], refs[-3:]
    rows = held.shape[1]
    fs = down.shape[1] // R
    for k, piece in enumerate(pieces):
        held[k ^ info[2]] = piece[...]
    for slot in range(len(pieces)):
        span = pl.ds((slot % q) * rows, rows)
        lo = (slot // q) * fs
        gate_up[span, 0, lo : lo + fs] = held[slot, :, 0:fs].astype(f32)
        gate_up[span, 1, lo : lo + fs] = held[slot, :, fs : 2 * fs].astype(f32)
        down[span, lo : lo + fs] = held[slot, :, 2 * fs : 3 * fs].astype(f32)


def prepare_kernel(info, qkv, outer, out):
    w = 2 * HD
    cols = outer.shape[1]
    for pair in range(cols // w):
        for part in range(3):
            lo = (3 * pair + part) * w
            out[:, lo : lo + w] = qkv[part, :, pair * w : (pair + 1) * w]
    out[:, 3 * cols :] = outer[...]


def finish_kernel(info, grads, qkv, outer):
    w = 2 * HD
    cols = outer.shape[1]
    for pair in range(cols // w):
        for part in range(3):
            lo = (3 * pair + part) * w
            qkv[part, :, pair * w : (pair + 1) * w] = grads[:, lo : lo + w].astype(f32)
    outer[...] = grads[:, 3 * cols :].astype(f32)


def whole_call(kernel, info, arrays, shapes, scratch=()):
    def spec(shape):
        return pl.BlockSpec(shape, lambda i, s: (0,) * len(shape))

    return pl.pallas_call(
        kernel,
        grid_spec=pltpu.PrefetchScalarGridSpec(
            num_scalar_prefetch=1,
            grid=(1,),
            in_specs=[spec(a.shape) for a in arrays],
            out_specs=[spec(a.shape) for a in shapes],
            scratch_shapes=list(scratch),
        ),
        out_shape=shapes,
        compiler_params=pltpu.CompilerParams(vmem_limit_bytes=48 << 20),
    )(info, *arrays)


def split_kernel(info, mine, other, mine_out, other_out):
    mine_out[...] = mine[...]
    other_out[...] = other[...]


def split_columns(info, array, parts):
    length, width = array.shape
    block = width // (2 * parts)
    shape = jax.ShapeDtypeStruct((length, width // 2), array.dtype)
    return pl.pallas_call(
        split_kernel,
        grid_spec=pltpu.PrefetchScalarGridSpec(
            num_scalar_prefetch=1,
            grid=(parts,),
            in_specs=[
                pl.BlockSpec((length, block), lambda j, s: (0, 2 * j + s[4])),
                pl.BlockSpec((length, block), lambda j, s: (0, 2 * j + 1 - s[4])),
            ],
            out_specs=[pl.BlockSpec((length, block), lambda j, s: (0, j))] * 2,
        ),
        out_shape=[shape, shape],
    )(info, array, array)


def make_body(mesh):
    R = mesh.shape[ROW]
    C = mesh.shape[COL]
    N = max(R, C)

    def row_permute(block, k):
        return lax.ppermute(block, ROW, [(i, i ^ k) for i in range(R)])

    def gather_rel(block, after=None):
        if R != 4:
            return [block] + [row_permute(block, k) for k in range(1, R)]
        half = block.shape[0] // 2
        if after is not None:
            block, _ = lax.optimization_barrier((block, after))
        one = row_permute(block, 1)
        two = row_permute(block, 2)
        top = row_permute(one[:half], 2)
        low = row_permute(two[half:], 1)
        return [block, one, two, jnp.concatenate([top, low], axis=0)]

    def scatter_rel(blocks):
        if R != 4:
            total = blocks[0]
            for k in range(1, R):
                total = total + row_permute(blocks[k].astype(bf16), k).astype(f32)
            return total
        half = blocks[0].shape[0] // 2
        b = [(x[:half], x[half:]) for x in blocks]
        top2 = row_permute(b[3][0].astype(bf16), 1)
        low1 = row_permute(b[3][1].astype(bf16), 2)
        top0 = row_permute(b[1][0].astype(bf16), 1)
        low0 = row_permute(b[2][1].astype(bf16), 2)
        top2 = row_permute((b[2][0].astype(f32) + top2.astype(f32)).astype(bf16), 2)
        low1 = row_permute((b[1][1].astype(f32) + low1.astype(f32)).astype(bf16), 1)
        top = b[0][0].astype(f32) + top0.astype(f32) + top2.astype(f32)
        low = b[0][1].astype(f32) + low0.astype(f32) + low1.astype(f32)
        return jnp.concatenate([top, low], axis=0)

    def source_place(s, c):
        return (s % (R // C)) * C + c if C <= R else c

    def source_dest(s, c, k):
        slot = source_place(s, c) ^ k
        if C <= R:
            return slot, s // (R // C)
        q = C // R
        return slot // q, s * q + slot % q

    def exchange_pairs(k):
        pairs = []
        for s in range(R):
            for c in range(C):
                dr, dc = source_dest(s, c, k)
                pairs.append((s * C + c, dr * C + dc))
        return pairs

    def spread(packed):
        return [lax.ppermute(packed[k], (ROW, COL), exchange_pairs(k)) for k in range(N)]

    def bring_back(packed):
        return [
            lax.ppermute(packed[k], (ROW, COL), [(b, a) for a, b in exchange_pairs(k)])
            for k in range(N)
        ]

    def sum_everywhere(array):
        for name in (COL, DP, ROW):
            size = mesh.shape[name]
            if size == 4:
                other = []
                for k in range(1, 4):
                    pairs = [(i, i ^ k) for i in range(4)]
                    other.append(lax.ppermute(array, name, pairs))
                array = (array + other[0]) + (other[1] + other[2])
                continue
            step = 1
            while step < size:
                other = lax.ppermute(array, name, [(i, i ^ step) for i in range(size)])
                step *= 2
                array = array + other
        return array

    def pair_sum(mine, other, right):
        away = tn(other, right).astype(bf16)
        got = lax.ppermute(away, COL, [(0, 1), (1, 0)])
        return (tn(mine, right) + got.astype(f32)).astype(bf16)

    def body(
        tokens,
        prefix_len,
        norm1_gain,
        norm1_bias,
        query_key_value_weight,
        query_key_value_bias,
        attention_output_weight,
        norm2_gain,
        norm2_bias,
        gate_up_projection_weight,
        down_projection_weight,
        grad_out,
    ):
        r = lax.axis_index(ROW)
        c = lax.axis_index(COL)
        block = tokens.shape[1]
        width = tokens.shape[2]
        head_cols = query_key_value_weight.shape[2]
        pairs = head_cols // (2 * HD)
        places = (jnp.arange(R)[:, None] ^ r) * block + jnp.arange(block)[None, :]
        table = rotary_tables(places.reshape(-1))
        w_rows, _, ff_local = gate_up_projection_weight.shape
        ff_slice = ff_local // R
        ff = ff_slice * C
        q_rows = max(1, C // R)
        u = source_place(r, c)
        v = r if C <= R else r * q_rows + c % q_rows
        info = jnp.stack([r, prefix_len[0], u, v, c]).astype(jnp.int32)
        rows = w_rows // q_rows
        a_rows = N // C * rows
        piece = (3 * ff_slice + 127) // 128 * 128

        gain1 = norm1_gain.astype(f32)
        gain2 = norm2_gain.astype(f32)
        inputs = tokens[0].astype(f32)
        first, first_std, first_inv = layer_norm_forward(inputs, gain1, norm1_bias.astype(f32))
        seq_in = jnp.concatenate(gather_rel(first.astype(bf16)), axis=0)

        (attn_shard,) = whole_call(
            prepare_kernel,
            info,
            [query_key_value_weight.transpose(1, 0, 2), attention_output_weight],
            [jax.ShapeDtypeStruct((attention_output_weight.shape[0], 4 * head_cols), bf16)],
        )
        w_attn = lax.all_gather(attn_shard, (DP, COL), axis=0, tiled=True)
        (packed,) = whole_call(
            functools.partial(pack_kernel, R, q_rows),
            info,
            [gate_up_projection_weight.transpose(1, 0, 2), down_projection_weight],
            [jax.ShapeDtypeStruct((N, rows, piece), bf16)],
        )
        packed, seq_in = lax.optimization_barrier((packed, seq_in))
        held = pltpu.VMEM((N, rows, piece), bf16)
        gu_shard, down_shard = whole_call(
            functools.partial(unpack_kernel, C),
            info,
            spread(packed),
            [
                jax.ShapeDtypeStruct((a_rows, 2 * ff), bf16),
                jax.ShapeDtypeStruct((a_rows, ff), bf16),
            ],
            [held],
        )
        w_gu = lax.all_gather(gu_shard, (DP, COL), axis=0, tiled=True)
        w_down = lax.all_gather(down_shard, (DP, COL), axis=0, tiled=True)

        w_attn, _ = lax.optimization_barrier((w_attn, gu_shard))
        w_qkv = w_attn[:, : 3 * head_cols]
        w_out = w_attn[:, 3 * head_cols :]
        dy_rel = jnp.concatenate(gather_rel(grad_out[0], gu_shard), axis=0)
        dy = grad_out[0]
        bias = query_key_value_bias.astype(f32).reshape(3, pairs, 2 * HD).transpose(1, 0, 2)
        projected = nn(seq_in, w_qkv)
        projected = projected + bias.reshape(-1)

        qkv, attended, log_sums = attend_forward(info, projected, table, R)
        own = nt(attended[:block], w_out)
        others = nt(attended[block:], w_out).astype(bf16)
        residual = scatter_rel([own] + [others[k * block : (k + 1) * block] for k in range(R - 1)])
        middle = inputs + residual

        second, second_std, second_inv = layer_norm_forward(
            middle, gain2, norm2_bias.astype(f32)
        )
        second_in = jnp.concatenate(gather_rel(second.astype(bf16)), axis=0)
        gate_up = nn(second_in, w_gu)
        gate_vals = gate_up[:, :ff]
        up_vals = gate_up[:, ff:]
        sig = jax.nn.sigmoid(gate_vals)
        swish = gate_vals * sig
        hidden = (swish * up_vals).astype(bf16)
        if C == 2:
            seq_halves = split_columns(info, seq_in, mesh.shape[DP])
            halves = split_columns(info, dy_rel, mesh.shape[DP])
            grad_down = pair_sum(*halves, hidden)
            _, w_down = lax.optimization_barrier((grad_down, w_down))
            grad_down = lax.psum_scatter(grad_down, DP, scatter_dimension=0, tiled=True)
        else:
            grad_down = tn(dy_rel, hidden).astype(bf16)
            _, w_down = lax.optimization_barrier((grad_down, w_down))
            grad_down = lax.psum_scatter(
                grad_down, (DP, COL), scatter_dimension=0, tiled=True
            )
        grad_hidden = nn(dy_rel, w_down)
        grad_gate = grad_hidden * up_vals * sig * (1.0 + gate_vals * (1.0 - sig))
        grad_up = grad_hidden * swish
        grad_gu_vals = jnp.concatenate([grad_gate.astype(bf16), grad_up.astype(bf16)], axis=1)
        if C == 2:
            halves = split_columns(info, second_in, mesh.shape[DP])
            away = tn(halves[1], grad_gu_vals).astype(bf16)
            got = lax.ppermute(away, COL, [(0, 1), (1, 0)])
            second_vals, _ = lax.optimization_barrier((grad_gu_vals, away))
        else:
            second_vals = grad_gu_vals
        own = nt(second_vals[:block], w_gu)
        last = (R - 1) * block
        far = nt(second_vals[last:], w_gu).astype(bf16)
        second_vals, _ = lax.optimization_barrier((second_vals, far))
        others = nt(second_vals[block:last], w_gu).astype(bf16)
        _, grad_gu_vals = lax.optimization_barrier((others, grad_gu_vals))
        grad_second = scatter_rel(
            [own] + [others[k * block : (k + 1) * block] for k in range(R - 2)] + [far]
        )
        if C == 2:
            grad_gu = (tn(halves[0], grad_gu_vals) + got.astype(f32)).astype(bf16)
            grad_gu = lax.psum_scatter(grad_gu, DP, scatter_dimension=0, tiled=True)
        else:
            grad_gu = tn(second_in, grad_gu_vals).astype(bf16)
            grad_gu = lax.psum_scatter(grad_gu, (DP, COL), scatter_dimension=0, tiled=True)

        grad_middle = dy.astype(f32) + layer_norm_backward(
            grad_second, second_std, second_inv, gain2
        )
        gain2_grad = jnp.sum(grad_second * second_std, axis=0)
        bias2_grad = jnp.sum(grad_second, axis=0)

        branch = jnp.concatenate(gather_rel(grad_middle.astype(bf16)), axis=0)
        own = nt(hidden[:block], w_down)
        others = nt(hidden[block:], w_down).astype(bf16)
        others, _ = lax.optimization_barrier((others, branch))
        mixed = scatter_rel(
            [own] + [others[k * block : (k + 1) * block] for k in range(R - 1)]
        )
        layer_out = (middle + mixed).astype(bf16)
        grad_heads = nn(branch, w_out).astype(bf16)
        grad_proj, bias_local = attend_backward(info, qkv, table, log_sums, grad_heads, R)
        bias_local = bias_local[:, 0].reshape(pairs, 3, 2 * HD)
        bias_local = bias_local.transpose(1, 0, 2).reshape(3, head_cols)
        if C == 2:
            outer = tn(branch, attended).astype(bf16).reshape(mesh.shape[DP], C, -1, head_cols)
            away = lax.dynamic_index_in_dim(outer, 1 - c, 1, keepdims=False)
            mine = lax.dynamic_index_in_dim(outer, c, 1, keepdims=False)
            got = lax.ppermute(away.reshape(-1, head_cols), COL, [(0, 1), (1, 0)])
            outer = mine.reshape(-1, head_cols).astype(f32) + got.astype(f32)
            grad_attn = jnp.concatenate(
                [pair_sum(*seq_halves, grad_proj), outer.astype(bf16)], axis=1
            )
            grad_proj, _ = lax.optimization_barrier((grad_proj, grad_attn))
            grad_attn = lax.psum_scatter(grad_attn, DP, scatter_dimension=0, tiled=True)
        else:
            grad_attn = jnp.concatenate(
                [tn(seq_in, grad_proj).astype(bf16), tn(branch, attended).astype(bf16)], axis=1
            )
            grad_attn = lax.psum_scatter(
                grad_attn, (DP, COL), scatter_dimension=0, tiled=True
            )
        own = nt(grad_proj[:block], w_qkv)
        others = nt(grad_proj[block:], w_qkv).astype(bf16)
        grad_first = scatter_rel(
            [own] + [others[k * block : (k + 1) * block] for k in range(R - 1)]
        )
        input_grad = grad_middle + layer_norm_backward(grad_first, first_std, first_inv, gain1)
        gain1_grad = jnp.sum(grad_first * first_std, axis=0)
        bias1_grad = jnp.sum(grad_first, axis=0)

        col_offset = r * head_cols
        bias_full = lax.dynamic_update_slice(
            jnp.zeros((3, width), f32), bias_local, (jnp.int32(0), col_offset)
        )
        sums = jnp.stack([gain1_grad, bias1_grad, gain2_grad, bias2_grad])
        sums = sum_everywhere(jnp.concatenate([sums, bias_full], axis=0))
        grad_bias = lax.dynamic_slice_in_dim(sums[4:], col_offset, head_cols, 1)

        (packed,) = whole_call(
            functools.partial(pack_back_kernel, C),
            info,
            [grad_gu, grad_down],
            [jax.ShapeDtypeStruct((N, rows, piece), bf16)],
        )
        home_gu, home_down = whole_call(
            functools.partial(unpack_back_kernel, R, q_rows),
            info,
            bring_back(packed),
            [
                jax.ShapeDtypeStruct((w_rows, 2, ff_local), f32),
                jax.ShapeDtypeStruct((w_rows, ff_local), f32),
            ],
            [held],
        )
        home_qkv, home_out = whole_call(
            finish_kernel,
            info,
            [grad_attn],
            [
                jax.ShapeDtypeStruct((3, grad_attn.shape[0], head_cols), f32),
                jax.ShapeDtypeStruct((grad_attn.shape[0], head_cols), f32),
            ],
        )
        return (
            layer_out[None],
            input_grad[None],
            sums[0],
            sums[1],
            home_qkv.transpose(1, 0, 2),
            grad_bias,
            home_out,
            sums[2],
            sums[3],
            home_gu,
            home_down,
        )

    return body


def solution(mesh):
    in_specs = (
        P((DP, COL), ROW, None),
        P((DP, COL)),
        P(),
        P(),
        P((DP, COL), None, ROW),
        P(None, ROW),
        P((DP, COL), ROW),
        P(),
        P(),
        P((DP, ROW), None, COL),
        P((DP, ROW), COL),
        P((DP, COL), ROW, None),
    )
    out_specs = (
        P((DP, COL), ROW, None),
        P((DP, COL), ROW, None),
        P(),
        P(),
        P((DP, COL), None, ROW),
        P(None, ROW),
        P((DP, COL), ROW),
        P(),
        P(),
        P((DP, ROW), None, COL),
        P((DP, ROW), COL),
    )
    body = make_body(mesh)

    return jax.shard_map(body, mesh=mesh, in_specs=in_specs, out_specs=out_specs, check_vma=False)
```
